32 devices in a mesh: occ: 8 (over z, x), aux: 4 (over y, core).
Axes of the slice: x: 2, y: 2, z: 4, core: 2. Of those that a mesh axis runs over, the one named last changes fastest.
Arguments:
- half_integrals: bfloat16 [8, 1024, 1024], P(None, 'aux'), may hold values from -1 to 1
- vir_coef: bfloat16 [1024, 768], P(None, 'occ'), may hold values from -0.1875 to 0.1875
- occ_energy: float32 [8], replicated, may hold values from -3 to -0.3
- vir_energy: float32 [768], replicated, may hold values from 0.1 to 2
Outputs:
- three_index: float32 [1024, 8, 768], P('aux', 'occ')
- vir_density: float32 [768, 768], P(('occ', 'aux'))
The draws below stay inside these ranges and needn't reach their ends.
All inputs are finite; a program needn't handle non-finite values.
Results may differ from the reference program's by a relative error of at most 0.0006.
The reference program's roundings to bfloat16 on the way (of `coupled` and `amplitude`) count: a program that leaves them out, or rounds other values in their place, can miss the bound.
Values may be sent and summed in bfloat16 or wider, within the bound.
A program may use at most 64 MiB of HBM per device.

```python
import jax
import jax.numpy as jnp
from jax import lax

NBF = 1024
NV = 768
NAUX = 1024
NO = 8


def draw_occ_energy(key, part):
    offsets = jnp.arange(NO, dtype=jnp.int32).astype(jnp.float32)
    jitter = jax.random.uniform(key, (NO,), jnp.float32)
    return -3.0 + 2.7 * (offsets + jitter) / NO


def draw_vir_energy(key, part):
    offsets = jnp.arange(NV, dtype=jnp.int32).astype(jnp.float32)
    jitter = jax.random.uniform(jax.random.fold_in(key, 7), (NV,), jnp.float32)
    return 0.1 + 1.9 * (offsets + jitter) / NV


def block_scale(own_key, extent, pieces, smallest, top_value):
    def one(position, blocks):
        steps = jax.random.uniform(jax.random.fold_in(jax.random.fold_in(own_key, 6), position), (blocks,), jnp.float32, smallest / len(pieces), top_value / len(pieces))
        return jnp.repeat(jnp.exp(steps), extent[position] // blocks).reshape((-1,) + (1,) * (len(extent) - position - 1))

    gain = one(*pieces[0])
    for cut in pieces[1:]:
        gain = gain * one(*cut)
    return gain


def centred(stream_key, extent, deviation, limit, split=(), kind=jnp.bfloat16):
    level = block_scale(stream_key, extent, split, -0.22, 0.18) if split else 1.0
    result = jax.random.normal(stream_key, extent, jnp.float32) * deviation * level
    return jnp.minimum(jnp.maximum(result, -limit), limit).astype(kind)


def setup_inputs(seed: int = 0) -> dict:
    arg_keys = jax.random.split(jax.random.key(seed), 5)
    half_integrals = centred(arg_keys[0], (NO, NAUX, NBF), (NAUX ** -0.25), 1.0, ((1, 4),))
    vir_coef = centred(arg_keys[1], (NBF, NV), NBF ** -0.5, 0.1875, ((1, 8),))
    occ_energy = draw_occ_energy(jax.random.fold_in(arg_keys[4], 71), 0)
    vir_energy = draw_vir_energy(jax.random.fold_in(arg_keys[4], 71), 0)
    return dict(half_integrals=half_integrals, vir_coef=vir_coef, occ_energy=occ_energy, vir_energy=vir_energy)


def reference(half_integrals, vir_coef, occ_energy, vir_energy):
    coupled = jnp.einsum('ipm,ma->iap', half_integrals.astype(jnp.float32), vir_coef.astype(jnp.float32)).astype(jnp.bfloat16)
    coupled = lax.optimization_barrier(coupled)
    spread = coupled.astype(jnp.float32)

    def one_orbital(density, orbital):
        own_rows = lax.dynamic_index_in_dim(spread, orbital, 0, keepdims=False)
        coulomb = jnp.einsum('jbp,ap->jba', spread, own_rows)
        denominator = occ_energy[orbital] + occ_energy[:, None, None] - vir_energy[None, :, None] - vir_energy[None, None, :]
        amplitude = (coulomb / denominator).astype(jnp.bfloat16)
        amplitude = lax.optimization_barrier(amplitude).astype(jnp.float32)
        gamma_rows = jnp.einsum('jba,jbp->pa', amplitude, spread)
        density = density + jnp.einsum('jca,jcd->ad', amplitude, amplitude)
        return density, gamma_rows

    density, stacked = lax.scan(one_orbital, jnp.zeros((NV, NV), jnp.float32), jnp.arange(NO, dtype=jnp.int32))
    three_index = jnp.transpose(stacked, (1, 0, 2))
    return three_index, density / (NO * NV)
```

```python
import functools

import jax
import jax.numpy as jnp
from jax import lax
from jax.experimental import pallas as pl
from jax.experimental.pallas import tpu as pltpu
from jax.sharding import PartitionSpec as P

MESH = pl.DeviceIdType.MESH
F32 = jnp.float32
LIMIT = 56 * 1024 * 1024


def remote(src, dst, send, recv, target):
    return pltpu.make_async_remote_copy(
        src_ref=src, dst_ref=dst, send_sem=send, recv_sem=recv, device_id=target, device_id_type=MESH
    )


def nearest_first(z, k, count):
    near = jnp.minimum(z, count - 1 - z)
    step = (k + 1) // 2
    both = z + step * (2 * (k % 2) - 1)
    low = z < count - 1 - z
    return jnp.where(k <= 2 * near, both, jnp.where(low, k, count - 1 - k))


def greet(n, nq):
    o = lax.axis_index("occ")
    s = lax.axis_index("aux")
    q, c = s // 2, s % 2
    z, low = o // 2, o % 2
    nz = n // 2
    barrier = pltpu.get_barrier_semaphore()
    peers = [(2 * z + 1 - low, s), (o, 2 * q + 1 - c)]
    peers += [(o, 2 * ((q + d) % nq) + c) for d in range(1, nq)]
    peers += [(2 * ((z + d) % nz) + low, s) for d in range(1, nz)]
    for peer in peers:
        pl.semaphore_signal(barrier, inc=1, device_id=peer, device_id_type=MESH)
    return lambda: pl.semaphore_wait(barrier, len(peers))


def make_densities(
    n, nq, occ_e, half, coef, vir_e, three, vir,
    ints, full, own, held, gift, amps,
    i_sem, c_copy, o_copy, c_recv, c_up, c_down, c_side, cp_send, cp_recv,
    own_send, own_recv, fw_send, fw_recv, pr_send, pr_recv, g_send, g_recv,
    h_recv, h_up, h_down, h_side,
    vir_done=lambda: None,
):
    o = lax.axis_index("occ")
    s = lax.axis_index("aux")
    q, c = s // 2, s % 2
    z, low = o // 2, o % 2
    nz = n // 2
    width = amps.shape[0] // n
    part = coef.shape[0]
    cut = coef.shape[1] // 2
    virtuals = amps.shape[1]
    above, below, side = o + 2, o - 2, 2 * z + 1 - low
    partner = (o, 2 * q + 1 - c)
    entered = greet(n, nq)

    fetch = pltpu.make_async_copy(half, ints, i_sem)
    fetch.start()

    def span(index, size):
        return pl.ds(pl.multiple_of(index * size, size), size)

    def keep(h):
        return pltpu.make_async_copy(coef.at[:, h * cut : (h + 1) * cut], full.at[h, span(o, part)], c_copy.at[h])

    keep(0).start()
    keep(1).start()
    entered()

    def relay(chain, src, dst, up, down, across, recv, act):
        pl.when(jnp.logical_and(chain <= z, z < nz - 1))(lambda: act(remote(src, dst, up, recv, (above, s))))
        pl.when(jnp.logical_and(chain >= z, z > 0))(lambda: act(remote(src, dst, down, recv, (below, s))))
        act(remote(src, dst, across, recv, (side, s)))

    def start(copy):
        copy.start()

    def sent(copy):
        copy.wait_send()

    def coef_slot(block):
        return full.at[c, span(block, part)]

    def coef_relay(chain, src, act):
        block = 2 * chain + low
        relay(chain, src, coef_slot(block), c_up.at[chain], c_down.at[chain], c_side.at[chain], c_recv.at[block], act)

    def coef_across(block):
        return remote(coef_slot(block), coef_slot(block), cp_send.at[block], cp_recv.at[block], partner)

    def coef_arrived(block):
        remote(coef_slot(block), coef_slot(block), c_side.at[0], c_recv.at[block], (side, s)).wait_recv()
        coef_across(block).start()

    coef_relay(z, coef.at[:, span(c, cut)], start)
    three[...] = jnp.zeros_like(three)
    vir[...] = jnp.zeros_like(vir)
    row_e = vir_e[...].reshape(1, virtuals)
    here = lax.broadcasted_iota(jnp.int32, (width, virtuals), 0) + s * width
    there = lax.broadcasted_iota(jnp.int32, (width, virtuals), 1)
    col_e = jnp.sum(jnp.where(here == there, row_e, 0.0), axis=1, keepdims=True)

    @pl.loop(1, nz)
    def _(k):
        chain = nearest_first(z, k, nz)
        block = 2 * chain + low
        remote(coef_slot(block), coef_slot(block), c_side.at[0], c_recv.at[block], (side, s)).wait_recv()
        coef_relay(chain, coef_slot(block), start)
        coef_across(block).start()
        coef_arrived(2 * nearest_first(z, k - 1, nz) + 1 - low)

    coef_arrived(2 * nearest_first(z, nz - 1, nz) + 1 - low)

    @pl.loop(1, n)
    def _(d):
        block = (o + d) % n
        other = full.at[1 - c, span(block, part)]
        remote(other, other, cp_send.at[block], cp_recv.at[block], partner).wait_recv()

    keep(0).wait()
    keep(1).wait()
    fetch.wait()

    def transform(block, rows):
        contract = (((1,), (1,)), ((), ()))
        return sum(
            lax.dot_general(
                full[h, rows, :], ints[block, :, h * cut : (h + 1) * cut], contract, preferred_element_type=F32
            )
            for h in range(2)
        ).astype(jnp.bfloat16)

    order = list(range(1, nq)) + [0]

    def chunk(there, core, group):
        return own.at[there, core, group]

    def to_partner(r):
        ref = chunk(q, c, (q + r) % nq)
        return remote(ref, ref, pr_send.at[r], pr_recv.at[r], partner)

    def to_chip(d, r):
        ref = chunk(q, c, (q + r) % nq)
        return remote(ref, ref, own_send.at[d, r], own_recv.at[d, r], (o, 2 * ((q + d) % nq) + c))

    def onward(d, r, core):
        there = (q + nq - d) % nq
        ref = chunk(there, core, (there + r) % nq)
        return remote(ref, ref, fw_send.at[d, r], fw_recv.at[d, r], partner)

    def from_chip(d, r):
        there = (q + nq - d) % nq
        ref = chunk(there, c, (there + r) % nq)
        remote(ref, ref, own_send.at[d, r], own_recv.at[d, r], partner).wait_recv()
        onward(d, r, c).start()

    for r in order:
        group = (q + r) % nq
        own[q, c, group] = transform(o, span(group, 2 * width))
        for d in range(1, nq):
            to_chip(d, r).start()
        to_partner(r).start()

    def give(block, core):
        return remote(
            gift.at[block], held.at[q, core, span(block, width)], g_send.at[block], g_recv.at[block], partner
        )

    @pl.loop(1, n)
    def _(d):
        block = (o + d) % n
        gift[block] = transform(block, span(2 * q + 1 - c, width))
        give(block, c).start()
        held[q, c, span(block, width), :] = transform(block, span(s, width))

    def held_slot(d, block):
        return held.at[(q + nq - d) % nq, :, span(block, width)]

    def own_slot(d):
        return own.at[(q + nq - d) % nq, :, q, span(c, width)]

    def held_relay(d, chain, src, act):
        block = 2 * chain + low
        relay(
            chain, src, held_slot(d, block), h_up.at[d, chain], h_down.at[d, chain], h_side.at[d, chain],
            h_recv.at[d, block], act,
        )

    def arrived(block):
        for d in range(1, nq):
            ref = held_slot(d, block)
            remote(ref, ref, h_side.at[d, 0], h_recv.at[d, block], (side, s)).wait_recv()

    for d in range(1, nq):
        from_chip(d, d)
    for d in range(1, nq):
        onward(d, d, 1 - c).wait_recv()
        held_relay(d, z, own_slot(d), start)
    rest = [(d, r) for d in range(1, nq) for r in order if r != d]
    for d, r in rest:
        from_chip(d, r)
    for r in order:
        ref = chunk(q, 1 - c, (q + r) % nq)
        remote(ref, ref, pr_send.at[r], pr_recv.at[r], partner).wait_recv()

    @pl.loop(1, n)
    def _(d):
        give((o + d) % n, 1 - c).wait_recv()

    for d, r in rest:
        onward(d, r, 1 - c).wait_recv()
    mine = pltpu.make_async_copy(
        own.at[:, :, q, span(c, width)], held.at[:, :, span(o, width)], o_copy
    )
    mine.start()
    mine.wait()

    def absorb(block):
        rows = span(block, width)
        coulomb = sum(
            lax.dot_general(
                held[t // 2, t % 2, rows, :], own[t // 2, t % 2].reshape(virtuals, -1),
                (((1,), (1,)), ((), ())), preferred_element_type=F32,
            )
            for t in range(2 * nq)
        )
        denominator = occ_e[o] + occ_e[block] - col_e - row_e
        amps[rows, :] = (coulomb / denominator).astype(jnp.bfloat16)

    contract = (((0,), (0,)), ((), ()))
    piece = virtuals // 2 if len(vir.shape) > 2 else 256

    def add_vir(chain):
        rows = span(chain, 2 * width)

        @pl.loop(0, virtuals // piece)
        def _(t):
            new = lax.dot_general(
                amps[rows, span(t, piece)], amps[rows, :], contract, preferred_element_type=F32
            )
            where = span(t, vir.shape[0] * piece // virtuals)
            vir[where] += new.reshape((-1,) + vir.shape[1:])

    def add_three(chain):
        rows = span(chain, 2 * width)

        @pl.loop(0, 2 * nq)
        def _(t):
            three[t // 2, t % 2] += lax.dot_general(
                held[t // 2, t % 2, rows, :], amps[rows, :], contract, preferred_element_type=F32
            )

    def both(chain):
        absorb(2 * chain + low)
        arrived(2 * chain + 1 - low)
        absorb(2 * chain + 1 - low)

    @pl.loop(1, nz)
    def _(k):
        chain = nearest_first(z, k, nz)
        arrived(2 * chain + low)
        for d in range(1, nq):
            held_relay(d, chain, held_slot(d, 2 * chain + low), start)
        before = nearest_first(z, k - 1, nz)
        both(before)
        add_vir(before)
        add_three(before)

    last = nearest_first(z, nz - 1, nz)
    both(last)
    add_vir(last)
    vir_done()
    add_three(last)

    def finish():
        @pl.loop(0, nz)
        def _(chain):
            coef_relay(chain, coef_slot(2 * chain + low), sent)
            for d in range(1, nq):
                held_relay(d, chain, held_slot(d, 2 * chain + low), sent)

        @pl.loop(1, n)
        def _(d):
            block = (o + d) % n
            coef_across(block).wait_send()
            give(block, c).wait_send()

        for r in order:
            to_partner(r).wait_send()
            for d in range(1, nq):
                to_chip(d, r).wait_send()
                onward(d, r, c).wait_send()

    return finish


def reduction(
    n, nq, three, vir, near_out, far_out, vir_out,
    t_pair, t_out, t_far, v_pair, v_sum, v_side, v_line, v_chain, v_col, v_far,
    pair_send, pair_recv, t_send, t_recv, vp_send, vp_recv, x_send, x_recv, z_send, z_recv, y_send, y_recv,
):
    o = lax.axis_index("occ")
    s = lax.axis_index("aux")
    q, c = s // 2, s % 2
    z, low = o // 2, o % 2
    nz = n // 2
    chunks, chunk = v_pair.shape[0], v_pair.shape[-1]
    partner = (o, 2 * q + 1 - c)
    side = (2 * z + 1 - low, s)

    def cols(k):
        return pl.ds(k * chunk, chunk)

    def v_swap(k):
        return remote(vir.at[:, :, 1 - c, :, cols(k)], v_pair.at[k], vp_send.at[k], vp_recv.at[k], partner)

    def x_swap(k):
        return remote(v_sum.at[k, :, 1 - low], v_side.at[k], x_send.at[k], x_recv.at[k], side)

    def along(k, d):
        there = (z + d) % nz
        return remote(
            v_line.at[k, there], v_chain.at[k, d], z_send.at[k, d], z_recv.at[k, d], (2 * there + low, s)
        )

    def between(k, d):
        there = (q + d) % nq
        return remote(v_col.at[k, there], v_far.at[k, d], y_send.at[k, d], y_recv.at[k, d], (o, 2 * there + c))

    def swap(d):
        return remote(three.at[(q + d) % nq, 1 - c], t_pair.at[d], pair_send.at[d], pair_recv.at[d], partner)

    def spread(d):
        return remote(t_out.at[d], t_far.at[d], t_send.at[d], t_recv.at[d], (o, 2 * ((q + d) % nq) + c))

    order = list(range(1, nq)) + [0]

    def open_vir():
        for k in range(chunks):
            v_swap(k).start()

    def close():
        for d in order:
            swap(d).start()
        for k in range(chunks):
            v_swap(k).wait()
            v_sum[k] = (vir[:, :, c, :, cols(k)] + v_pair[k]).reshape(v_sum.shape[1:])
            x_swap(k).start()
        for d in order[:-1]:
            swap(d).wait()
            t_out[d] = three[(q + d) % nq, c] + t_pair[d]
            spread(d).start()
        for k in range(chunks):
            x_swap(k).wait()
            v_line[k] = v_sum[k, :, low] + v_side[k]
            for d in range(1, nz):
                along(k, d).start()
            if k == 0:
                swap(0).wait()
                near_out[...] = three[q, c] + t_pair[0]
        for k in range(chunks):
            held = v_line[k, z]
            for d in range(1, nz):
                along(k, d).wait()
                held += v_chain[k, d]
            v_col[k] = held
            for d in range(1, nq):
                between(k, d).start()
        for d in order[:-1]:
            spread(d).wait()
            far_out[...] = t_far[d] if d == 1 else far_out[...] + t_far[d]
        for k in range(chunks):
            rows = v_col[k, q]
            for d in range(1, nq):
                between(k, d).wait()
                rows += v_far[k, d]
            vir_out[:, cols(k)] = rows

    return open_vir, close


def amplitude_kernel(n, nq, *refs):
    make_densities(n, nq, *refs)()


def reduce_kernel(n, nq, *refs):
    greet(n, nq)()
    open_vir, close = reduction(n, nq, *refs)
    open_vir()
    close()


def whole_kernel(n, nq, inputs, outputs, count, *refs):
    operands, results, scratch = refs[:inputs], refs[inputs : inputs + outputs], refs[inputs + outputs :]
    three, vir, rest = scratch[0], scratch[1], scratch[2:]
    open_vir, close = reduction(n, nq, three, vir, *results, *rest[count:])
    finish = make_densities(n, nq, *operands, three, vir, *rest[:count], vir_done=open_vir)
    close()
    finish()


def paired_kernel(
    n, occ_e, half, coef, vir_e, three_out, vir_out,
    ints, raw, full, own, held, gift, cross, amps, vir,
    t_give, t_got, t_sum, t_far, n_give, n_got, v_pair, v_sum, v_side, v_line, v_chain, v_col, v_far,
    i_sem, keep_sem, o_sem, raw_sems, c_recv, c_up, c_down, c_side, cp_send, cp_recv,
    pn_sems, pf_sems, f_recv, f_send, z_fwd, x_fwd, y_send, g_send, g_recv,
    t_sems, ts_sems, n_sems, vp_send, vp_recv, x_send, x_recv, z_send, z_recv, yv_send, yv_recv,
):
    o = lax.axis_index("occ")
    s = lax.axis_index("aux")
    q, c = s // 2, s % 2
    z, low = o // 2, o % 2
    nz = n // 2
    far = 1 - q
    part, basis = coef.shape
    tile = raw.shape[0]
    virtuals = full.shape[0]
    width = virtuals // 4
    piece = basis // 4
    above, below, side = o + 2, o - 2, 2 * z + 1 - low
    other = 2 * q + 1 - c
    partner = (o, other)
    opposite = (o, 2 * far + c)

    def span(index, size):
        return pl.ds(pl.multiple_of(index * size, size), size)

    def start(copy):
        copy.start()

    def sent(copy):
        copy.wait_send()

    def nearest(k):
        return nearest_first(z, k, nz)

    barrier = pltpu.get_barrier_semaphore()
    peers = [partner, opposite, (o, 2 * far + 1 - c), (side, s), (side, other)]
    peers += [(2 * ((z + d) % nz) + low, t) for d in range(1, nz) for t in (s, other)]
    for peer in peers:
        pl.semaphore_signal(barrier, inc=1, device_id=peer, device_id_type=MESH)
    fetch = pltpu.make_async_copy(half, ints, i_sem)
    fetch.start()
    keep = pltpu.make_async_copy(coef, full.at[span(o, part)], keep_sem)
    keep.start()
    pl.semaphore_wait(barrier, len(peers))

    lend = remote(half.at[o], raw, raw_sems.at[0], raw_sems.at[1], opposite)
    lend.start()

    def coef_slot(block, core, h):
        return full.at[span(block, part), pl.ds(pl.multiple_of((2 * core + h) * piece, piece), piece)]

    def coef_relay(chain, h, src, act):
        block = 2 * chain + low
        dst = coef_slot(block, c, h)
        recv = c_recv.at[block, h]
        pl.when(jnp.logical_and(chain <= z, z < nz - 1))(
            lambda: act(remote(src, dst, c_up.at[chain, h], recv, (above, s)))
        )
        pl.when(jnp.logical_and(chain >= z, z > 0))(
            lambda: act(remote(src, dst, c_down.at[chain, h], recv, (below, s)))
        )
        act(remote(src, dst, c_side.at[chain, h], recv, (side, s)))

    def coef_across(block, h, core):
        ref = coef_slot(block, core, h)
        return remote(ref, ref, cp_send.at[block, h], cp_recv.at[block, h], partner)

    def coef_wait(block, h):
        ref = coef_slot(block, c, h)
        remote(ref, ref, c_side.at[0, h], c_recv.at[block, h], (side, s)).wait_recv()

    for h in range(2):
        coef_relay(z, h, coef.at[:, pl.ds(pl.multiple_of((2 * c + h) * piece, piece), piece)], start)
    row_e = vir_e[...].reshape(1, virtuals)
    here = lax.broadcasted_iota(jnp.int32, (width, virtuals), 0) + s * width
    there = lax.broadcasted_iota(jnp.int32, (width, virtuals), 1)
    col_e = jnp.sum(jnp.where(here == there, row_e, 0.0), axis=1, keepdims=True)

    def coef_beside(k):
        block = 2 * nearest(k) + 1 - low
        for h in range(2):
            coef_wait(block, h)
            coef_across(block, h, c).start()

    @pl.loop(1, nz)
    def _(k):
        chain = nearest(k)
        block = 2 * chain + low
        for h in range(2):
            coef_wait(block, h)
            coef_relay(chain, h, coef_slot(block, c, h), start)
            coef_across(block, h, c).start()
        coef_beside(k - 1)

    coef_beside(nz - 1)

    @pl.loop(1, n)
    def _(d):
        block = (o + d) % n
        for h in range(2):
            coef_across(block, h, 1 - c).wait_recv()

    keep.wait()
    fetch.wait()

    def transform(rows, source):
        return lax.dot_general(rows, source, (((1,), (1,)), ((), ())), preferred_element_type=F32).astype(jnp.bfloat16)

    def cols(group, core):
        return span(2 * group + core, tile)

    def lend_block(block, act):
        for core in range(2):
            act(
                remote(
                    cross.at[block, pl.ds(core * width, width)], held.at[span(block, width), cols(q, c)],
                    y_send.at[block, core], f_recv.at[block, c], (o, 2 * far + core),
                )
            )

    def distant(chain):
        return jnp.abs(chain - z) > 2

    def lend_blocks(k, act):
        chain = nearest(k)
        act(2 * chain + 1 - low)
        pl.when(distant(chain))(lambda: act(2 * chain + low))

    def cross_over(block):
        cross[block] = transform(full[span(far, 2 * width), :], ints[block])
        lend_block(block, start)

    @pl.loop(2, nz)
    def _(k):
        lend_blocks(k, cross_over)

    def own_part(group, core):
        return own.at[:, cols(group, core)]

    def near_part(core):
        ref = own_part(q, core)
        return remote(ref, ref, pn_sems.at[0], pn_sems.at[1], partner)

    def far_part(core):
        ref = own_part(far, core)
        return remote(ref, ref, pf_sems.at[0], pf_sems.at[1], partner)

    def hand_out(act):
        for core in range(2):
            src = own.at[span(2 * q + core, width), cols(far, c)]
            dst = held.at[span(o, width), cols(far, c)]
            recv = f_recv.at[o, c]
            pl.when(z < nz - 1)(lambda: act(remote(src, dst, f_send.at[0, core], recv, (above, 2 * q + core))))
            pl.when(z > 0)(lambda: act(remote(src, dst, f_send.at[1, core], recv, (below, 2 * q + core))))
        for core in range(2):
            src = own.at[span(2 * q + core, width), cols(far, c)]
            dst = held.at[span(o, width), cols(far, c)]
            act(remote(src, dst, f_send.at[2, core], f_recv.at[o, c], (side, 2 * q + core)))

    lend.wait_recv()
    own[:, cols(far, c)] = transform(full[...], raw[...])
    hand_out(start)
    far_part(c).start()
    own[:, cols(q, c)] = transform(full[...], ints[o])
    near_part(c).start()

    def give(block, core):
        return remote(
            gift.at[block], held.at[span(block, width), cols(q, core)], g_send.at[block], g_recv.at[block], partner
        )

    @pl.loop(1, n)
    def _(d):
        block = (o + d) % n
        rows = jnp.concatenate([full[span(s, width), :], full[span(other, width), :]], axis=0)
        both = transform(rows, ints[block])
        held[span(block, width), cols(q, c)] = both[:width]
        gift[block] = both[width:]
        give(block, c).start()

    far_part(1 - c).wait_recv()
    near_part(1 - c).wait_recv()
    mine = pltpu.make_async_copy(own.at[span(s, width)], held.at[span(o, width)], o_sem)
    mine.start()

    def far_slot(block, core):
        return held.at[span(block, width), cols(far, core)]

    def arrive(block):
        for core in range(2):
            ref = far_slot(block, core)
            remote(ref, ref, x_fwd.at[0], f_recv.at[block, core], (side, s)).wait_recv()

    def pass_on(chain, act):
        block = 2 * chain + low
        for core in range(2):
            ref = far_slot(block, core)
            recv = f_recv.at[block, core]
            pl.when(jnp.logical_and(chain < z, z < nz - 1))(
                lambda: act(remote(ref, ref, z_fwd.at[0, core], recv, (above, s)))
            )
            pl.when(jnp.logical_and(chain > z, z > 0))(
                lambda: act(remote(ref, ref, z_fwd.at[1, core], recv, (below, s)))
            )
            pl.when(chain == nearest(1))(lambda: act(remote(ref, ref, x_fwd.at[core], recv, (side, s))))

    def beside_each(act):
        pl.when(z > 0)(lambda: act(z - 1))
        pl.when(z < nz - 1)(lambda: act(z + 1))

    def take(chain):
        arrive(2 * chain + low)
        pass_on(chain, start)

    beside_each(take)
    mine.wait()

    def absorb(chain):
        rows = span(chain, 2 * width)
        coulomb = lax.dot_general(
            held[rows, :], own[...], (((1,), (1,)), ((), ())), preferred_element_type=F32
        )
        left = jnp.concatenate([occ_e[o] + occ_e[2 * chain + t] - col_e for t in range(2)], axis=0)
        amps[rows, :] = (coulomb / (left - row_e)).astype(jnp.bfloat16)

    @pl.loop(0, nz)
    def _(k):
        chain = nearest(k)
        pl.when(jnp.abs(chain - z) > 1)(lambda: arrive(2 * chain + low))
        arrive(2 * chain + 1 - low)
        pl.when(chain != z)(lambda: give(2 * chain + low, 1 - c).wait_recv())
        give(2 * chain + 1 - low, 1 - c).wait_recv()
        absorb(chain)

    contract = (((0,), (0,)), ((), ()))
    strips, strip = t_give.shape[0], t_give.shape[-1]
    chunks, chunk = v_pair.shape[0], v_pair.shape[-1]

    def lanes(k):
        return pl.ds(k * chunk, chunk)

    def wide(k):
        return pl.ds(k * strip, strip)

    def part_three(group, core, where):
        return lax.dot_general(
            held[:, cols(group, core)], amps[:, where], contract, preferred_element_type=F32
        )

    def far_swap(k):
        return remote(t_give.at[k], t_got.at[k], t_sems.at[0, k], t_sems.at[1, k], partner)

    def far_send(k):
        return remote(t_sum.at[k], t_far.at[k], ts_sems.at[0, k], ts_sems.at[1, k], opposite)

    def v_swap(k):
        return remote(vir.at[:, :, 1 - c, :, lanes(k)], v_pair.at[k], vp_send.at[k], vp_recv.at[k], partner)

    def x_swap(k):
        return remote(v_sum.at[k, :, 1 - low], v_side.at[k], x_send.at[k], x_recv.at[k], (side, s))

    def along(k, d):
        to = (z + d) % nz
        return remote(v_line.at[k, to], v_chain.at[k, d], z_send.at[k, d], z_recv.at[k, d], (2 * to + low, s))

    def between(k):
        return remote(v_col.at[k, far], v_far.at[k], yv_send.at[k], yv_recv.at[k], opposite)

    near_swap = remote(n_give, n_got, n_sems.at[0], n_sems.at[1], partner)
    for k in range(strips):
        t_give[k] = part_three(far, 1 - c, wide(k))
        far_swap(k).start()
    for k in range(strips):
        t_sum[k] = part_three(far, c, wide(k))
        far_swap(k).wait_recv()
        t_sum[k] += t_got[k]
        far_send(k).start()
    for k in range(strips):
        new = lax.dot_general(amps[...], amps[:, wide(k)], contract, preferred_element_type=F32)
        vir[:, :, :, :, wide(k)] = new.reshape(vir.shape[:-1] + (strip,))
        for t in range(k * strip // chunk, (k + 1) * strip // chunk):
            v_swap(t).start()
    n_give[...] = part_three(q, 1 - c, slice(None))
    near_swap.start()
    for k in range(chunks):
        v_swap(k).wait_recv()
        v_sum[k] = (vir[:, :, c, :, lanes(k)] + v_pair[k]).reshape(v_sum.shape[1:])
        x_swap(k).start()
    three_out[...] = part_three(q, c, slice(None))
    for k in range(chunks):
        x_swap(k).wait_recv()
        v_line[k] = v_sum[k, :, low] + v_side[k]
        for d in range(1, nz):
            along(k, d).start()
    near_swap.wait_recv()
    three_out[...] += n_got[...]
    for k in range(chunks):
        total = v_line[k, z]
        for d in range(1, nz):
            along(k, d).wait_recv()
            total += v_chain[k, d]
        v_col[k] = total
        between(k).start()
    for k in range(strips):
        far_send(k).wait_recv()
        three_out[:, wide(k)] += t_far[k]
    for k in range(chunks):
        between(k).wait_recv()
        vir_out[:, lanes(k)] = (v_col[k, q] + v_far[k]) / (n * virtuals)

    lend.wait_send()

    @pl.loop(0, nz)
    def _(chain):
        for h in range(2):
            coef_relay(chain, h, coef_slot(2 * chain + low, c, h), sent)

    @pl.loop(1, n)
    def _(d):
        block = (o + d) % n
        for h in range(2):
            coef_across(block, h, c).wait_send()
        give(block, c).wait_send()

    @pl.loop(2, nz)
    def _(k):
        lend_blocks(k, lambda block: lend_block(block, sent))

    hand_out(sent)
    far_part(c).wait_send()
    near_part(c).wait_send()
    beside_each(lambda chain: pass_on(chain, sent))
    near_swap.wait_send()
    for k in range(strips):
        far_swap(k).wait_send()
        far_send(k).wait_send()
    for k in range(chunks):
        v_swap(k).wait_send()
        x_swap(k).wait_send()
        between(k).wait_send()
        for d in range(1, nz):
            along(k, d).wait_send()


def paired(n, half_integrals, coef, occ_energy, vir_energy):
    _, tile, basis = half_integrals.shape
    part = coef.shape[0]
    virtuals = part * n
    width, rows, nz = virtuals // 4, virtuals // (4 * n), n // 2
    vmem = pl.BlockSpec(memory_space=pltpu.VMEM)
    dma = pltpu.SemaphoreType.DMA
    lanes = 128
    chunks = virtuals // lanes
    strip = 2 * lanes if chunks % 2 == 0 else lanes
    strips = virtuals // strip

    def room(*shape):
        return pltpu.VMEM(shape, F32)

    def packed(*shape):
        return pltpu.VMEM(shape, jnp.bfloat16)

    scratch = [
        packed(n, tile, basis), packed(tile, basis), packed(virtuals, basis), packed(virtuals, 4 * tile),
        packed(n * width, 4 * tile), packed(n, width, tile), packed(n, 2 * width, tile), packed(n * width, virtuals),
        room(n, 2, 2, rows, virtuals),
        room(strips, tile, strip), room(strips, tile, strip), room(strips, tile, strip), room(strips, tile, strip),
        room(tile, virtuals), room(tile, virtuals),
        room(chunks, n, 2, rows, lanes), room(chunks, nz, 2, 2, rows, lanes), room(chunks, nz, 2, rows, lanes),
        room(chunks, nz, 2, rows, lanes), room(chunks, nz, 2, rows, lanes), room(chunks, 2, rows, lanes),
        room(chunks, rows, lanes),
        dma, dma, dma, dma((2,)), dma((n, 2)), dma((nz, 2)), dma((nz, 2)), dma((nz, 2)), dma((n, 2)), dma((n, 2)),
        dma((2,)), dma((2,)), dma((n, 2)), dma((3, 2)), dma((2, 2)), dma((2,)), dma((n, 2)), dma((n,)), dma((n,)),
        dma((2, strips)), dma((2, strips)), dma((2,)),
        dma((chunks,)), dma((chunks,)), dma((chunks,)), dma((chunks,)), dma((chunks, nz)), dma((chunks, nz)),
        dma((chunks,)), dma((chunks,)),
    ]
    return pl.pallas_call(
        functools.partial(paired_kernel, n),
        out_shape=(
            jax.ShapeDtypeStruct((tile, virtuals), F32), jax.ShapeDtypeStruct((rows, virtuals), F32),
        ),
        in_specs=[pl.BlockSpec(memory_space=pltpu.SMEM), pl.BlockSpec(memory_space=pl.ANY), vmem, vmem],
        out_specs=(vmem, vmem),
        scratch_shapes=scratch,
        compiler_params=pltpu.CompilerParams(
            collective_id=0, has_side_effects=True, vmem_limit_bytes=LIMIT
        ),
        name="densities",
    )(occ_energy, half_integrals, coef, vir_energy)


def per_device(half_integrals, vir_coef, occ_energy, vir_energy):
    n, aux = lax.axis_size("occ"), lax.axis_size("aux")
    nz, nq = n // 2, aux // 2
    _, tile, basis = half_integrals.shape
    part = vir_coef.shape[1]
    virtuals = part * n
    if nq == 2 and n % 2 == 0 and nz > 1 and virtuals % (32 * n) == 0 and virtuals % 128 == 0:
        three, vir_rows = paired(n, half_integrals, vir_coef.T, occ_energy, vir_energy)
        return three[:, None, :], vir_rows
    width, rows = virtuals // aux, virtuals // (n * aux)
    vmem = pl.BlockSpec(memory_space=pltpu.VMEM)
    dma = pltpu.SemaphoreType.DMA
    half = jnp.bfloat16
    lanes = 128
    chunks = virtuals // lanes

    def room(*shape):
        return pltpu.VMEM(shape, F32)

    def result(*shape):
        return jax.ShapeDtypeStruct(shape, F32)

    def call(kernel, name, number, in_specs, out_shape, scratch, operands):
        return pl.pallas_call(
            kernel,
            out_shape=out_shape,
            in_specs=in_specs,
            out_specs=(vmem,) * len(out_shape),
            scratch_shapes=scratch,
            compiler_params=pltpu.CompilerParams(
                collective_id=number, has_side_effects=True, vmem_limit_bytes=LIMIT
            ),
            name=name,
        )(*operands)

    operands = (occ_energy, half_integrals, vir_coef.T, vir_energy)
    specs = [pl.BlockSpec(memory_space=pltpu.SMEM), pl.BlockSpec(memory_space=pl.ANY), vmem, vmem]
    make_scratch = [
        pltpu.VMEM(half_integrals.shape, half),
        pltpu.VMEM((2, virtuals, basis // 2), half),
        pltpu.VMEM((nq, 2, nq, 2 * width, tile), half),
        pltpu.VMEM((nq, 2, n * width, tile), half),
        pltpu.VMEM((n, width, tile), half),
        pltpu.VMEM((n * width, virtuals), half),
        dma, dma((2,)), dma, dma((n,)), dma((nz,)), dma((nz,)), dma((nz,)), dma((n,)), dma((n,)),
        dma((nq, nq)), dma((nq, nq)), dma((nq, nq)), dma((nq, nq)), dma((nq,)), dma((nq,)), dma((n,)), dma((n,)),
        dma((nq, n)), dma((nq, nz)), dma((nq, nz)), dma((nq, nz)),
    ]
    reduce_scratch = [
        room(nq, tile, virtuals), room(nq, tile, virtuals), room(nq, tile, virtuals),
        room(chunks, n, nq, rows, lanes), room(chunks, nz, 2, nq, rows, lanes),
        room(chunks, nz, nq, rows, lanes), room(chunks, nz, nq, rows, lanes), room(chunks, nz, nq, rows, lanes),
        room(chunks, nq, rows, lanes), room(chunks, nq, rows, lanes),
        dma((nq,)), dma((nq,)), dma((nq,)), dma((nq,)), dma((chunks,)), dma((chunks,)), dma((chunks,)), dma((chunks,)),
        dma((chunks, nz)), dma((chunks, nz)), dma((chunks, nq)), dma((chunks, nq)),
    ]
    sums = (nq, 2, tile, virtuals)
    groups = (n, nq, 2, rows, virtuals)
    finals = (result(tile, virtuals), result(tile, virtuals), result(rows, virtuals))
    if rows % 8 == 0:
        kernel = functools.partial(whole_kernel, n, nq, len(specs), len(finals), len(make_scratch))
        scratch = [room(*sums), room(*groups)] + make_scratch + reduce_scratch
        near, far, vir_rows = call(kernel, "densities", 0, specs, finals, scratch, operands)
    else:
        kernel = functools.partial(amplitude_kernel, n, nq)
        partials = (result(*sums), result(virtuals, virtuals))
        three, vir = call(kernel, "amplitude", 0, specs, partials, make_scratch, operands)
        kernel = functools.partial(reduce_kernel, n, nq)
        near, far, vir_rows = call(
            kernel, "reduce", 1, [vmem, vmem], finals, reduce_scratch, (three, vir.reshape(groups))
        )
    return (near + far)[:, None, :], vir_rows / (n * virtuals)


def solution(mesh):
    return jax.shard_map(
        per_device,
        mesh=mesh,
        in_specs=(P(None, "aux", None), P(None, "occ"), P(), P()),
        out_specs=(P("aux", "occ", None), P(("occ", "aux"), None)),
        check_vma=False,
    )
```

```python
import functools

import jax
import jax.numpy as jnp
from jax import lax
from jax.experimental import pallas as pl
from jax.experimental.pallas import tpu as pltpu
from jax.sharding import PartitionSpec as P

MESH = pl.DeviceIdType.MESH
F32 = jnp.float32
PIECES = 4
SPAN = 80.0
TINY = 1e-30
LIMIT = 56 * 1024 * 1024


def remote(src, dst, send, recv, target):
    return pltpu.make_async_remote_copy(
        src_ref=src, dst_ref=dst, send_sem=send, recv_sem=recv, device_id=target, device_id_type=MESH
    )


def nearest_first(z, k, count):
    near = jnp.minimum(z, count - 1 - z)
    step = (k + 1) // 2
    both = z + step * (2 * (k % 2) - 1)
    low = z < count - 1 - z
    return jnp.where(k <= 2 * near, both, jnp.where(low, k, count - 1 - k))


def greet(n, nq):
    o = lax.axis_index("occ")
    s = lax.axis_index("aux")
    q, c = s // 2, s % 2
    z, low = o // 2, o % 2
    nz = n // 2
    barrier = pltpu.get_barrier_semaphore()
    peers = [(2 * z + 1 - low, s), (o, 2 * q + 1 - c)]
    peers += [(o, 2 * ((q + d) % nq) + c) for d in range(1, nq)]
    peers += [(2 * ((z + d) % nz) + low, s) for d in range(1, nz)]
    for peer in peers:
        pl.semaphore_signal(barrier, inc=1, device_id=peer, device_id_type=MESH)
    return lambda: pl.semaphore_wait(barrier, len(peers))


def make_densities(
    n, nq, occ_e, half, coef, vir_e, three, vir,
    ints, full, own, held, gift, amps,
    i_sem, c_copy, o_copy, c_recv, c_up, c_down, c_side, cp_send, cp_recv,
    own_send, own_recv, fw_send, fw_recv, pr_send, pr_recv, g_send, g_recv,
    h_recv, h_up, h_down, h_side,
    vir_done=lambda: None,
):
    o = lax.axis_index("occ")
    s = lax.axis_index("aux")
    q, c = s // 2, s % 2
    z, low = o // 2, o % 2
    nz = n // 2
    width = amps.shape[0] // n
    part = coef.shape[0]
    cut = coef.shape[1] // 2
    virtuals = amps.shape[1]
    above, below, side = o + 2, o - 2, 2 * z + 1 - low
    partner = (o, 2 * q + 1 - c)
    entered = greet(n, nq)

    fetch = pltpu.make_async_copy(half, ints, i_sem)
    fetch.start()

    def span(index, size):
        return pl.ds(pl.multiple_of(index * size, size), size)

    def keep(h):
        return pltpu.make_async_copy(coef.at[:, h * cut : (h + 1) * cut], full.at[h, span(o, part)], c_copy.at[h])

    keep(0).start()
    keep(1).start()
    entered()

    def relay(chain, src, dst, up, down, across, recv, act):
        pl.when(jnp.logical_and(chain <= z, z < nz - 1))(lambda: act(remote(src, dst, up, recv, (above, s))))
        pl.when(jnp.logical_and(chain >= z, z > 0))(lambda: act(remote(src, dst, down, recv, (below, s))))
        act(remote(src, dst, across, recv, (side, s)))

    def start(copy):
        copy.start()

    def sent(copy):
        copy.wait_send()

    def coef_slot(block):
        return full.at[c, span(block, part)]

    def coef_relay(chain, src, act):
        block = 2 * chain + low
        relay(chain, src, coef_slot(block), c_up.at[chain], c_down.at[chain], c_side.at[chain], c_recv.at[block], act)

    def coef_across(block):
        return remote(coef_slot(block), coef_slot(block), cp_send.at[block], cp_recv.at[block], partner)

    def coef_arrived(block):
        remote(coef_slot(block), coef_slot(block), c_side.at[0], c_recv.at[block], (side, s)).wait_recv()
        coef_across(block).start()

    coef_relay(z, coef.at[:, span(c, cut)], start)
    three[...] = jnp.zeros_like(three)
    vir[...] = jnp.zeros_like(vir)
    row_e = vir_e[...].reshape(1, virtuals)
    here = lax.broadcasted_iota(jnp.int32, (width, virtuals), 0) + s * width
    there = lax.broadcasted_iota(jnp.int32, (width, virtuals), 1)
    col_e = jnp.sum(jnp.where(here == there, row_e, 0.0), axis=1, keepdims=True)

    @pl.loop(1, nz)
    def _(k):
        chain = nearest_first(z, k, nz)
        block = 2 * chain + low
        remote(coef_slot(block), coef_slot(block), c_side.at[0], c_recv.at[block], (side, s)).wait_recv()
        coef_relay(chain, coef_slot(block), start)
        coef_across(block).start()
        coef_arrived(2 * nearest_first(z, k - 1, nz) + 1 - low)

    coef_arrived(2 * nearest_first(z, nz - 1, nz) + 1 - low)

    @pl.loop(1, n)
    def _(d):
        block = (o + d) % n
        other = full.at[1 - c, span(block, part)]
        remote(other, other, cp_send.at[block], cp_recv.at[block], partner).wait_recv()

    keep(0).wait()
    keep(1).wait()
    fetch.wait()

    def transform(block, rows):
        contract = (((1,), (1,)), ((), ()))
        return sum(
            lax.dot_general(
                full[h, rows, :], ints[block, :, h * cut : (h + 1) * cut], contract, preferred_element_type=F32
            )
            for h in range(2)
        ).astype(jnp.bfloat16)

    order = list(range(1, nq)) + [0]

    def chunk(there, core, group):
        return own.at[there, core, group]

    def to_partner(r):
        ref = chunk(q, c, (q + r) % nq)
        return remote(ref, ref, pr_send.at[r], pr_recv.at[r], partner)

    def to_chip(d, r):
        ref = chunk(q, c, (q + r) % nq)
        return remote(ref, ref, own_send.at[d, r], own_recv.at[d, r], (o, 2 * ((q + d) % nq) + c))

    def onward(d, r, core):
        there = (q + nq - d) % nq
        ref = chunk(there, core, (there + r) % nq)
        return remote(ref, ref, fw_send.at[d, r], fw_recv.at[d, r], partner)

    def from_chip(d, r):
        there = (q + nq - d) % nq
        ref = chunk(there, c, (there + r) % nq)
        remote(ref, ref, own_send.at[d, r], own_recv.at[d, r], partner).wait_recv()
        onward(d, r, c).start()

    for r in order:
        group = (q + r) % nq
        own[q, c, group] = transform(o, span(group, 2 * width))
        for d in range(1, nq):
            to_chip(d, r).start()
        to_partner(r).start()

    def give(block, core):
        return remote(
            gift.at[block], held.at[q, core, span(block, width)], g_send.at[block], g_recv.at[block], partner
        )

    @pl.loop(1, n)
    def _(d):
        block = (o + d) % n
        gift[block] = transform(block, span(2 * q + 1 - c, width))
        give(block, c).start()
        held[q, c, span(block, width), :] = transform(block, span(s, width))

    def held_slot(d, block):
        return held.at[(q + nq - d) % nq, :, span(block, width)]

    def own_slot(d):
        return own.at[(q + nq - d) % nq, :, q, span(c, width)]

    def held_relay(d, chain, src, act):
        block = 2 * chain + low
        relay(
            chain, src, held_slot(d, block), h_up.at[d, chain], h_down.at[d, chain], h_side.at[d, chain],
            h_recv.at[d, block], act,
        )

    def arrived(block):
        for d in range(1, nq):
            ref = held_slot(d, block)
            remote(ref, ref, h_side.at[d, 0], h_recv.at[d, block], (side, s)).wait_recv()

    for d in range(1, nq):
        from_chip(d, d)
    for d in range(1, nq):
        onward(d, d, 1 - c).wait_recv()
        held_relay(d, z, own_slot(d), start)
    rest = [(d, r) for d in range(1, nq) for r in order if r != d]
    for d, r in rest:
        from_chip(d, r)
    for r in order:
        ref = chunk(q, 1 - c, (q + r) % nq)
        remote(ref, ref, pr_send.at[r], pr_recv.at[r], partner).wait_recv()

    @pl.loop(1, n)
    def _(d):
        give((o + d) % n, 1 - c).wait_recv()

    for d, r in rest:
        onward(d, r, 1 - c).wait_recv()
    mine = pltpu.make_async_copy(
        own.at[:, :, q, span(c, width)], held.at[:, :, span(o, width)], o_copy
    )
    mine.start()
    mine.wait()

    def absorb(block):
        rows = span(block, width)
        coulomb = sum(
            lax.dot_general(
                held[t // 2, t % 2, rows, :], own[t // 2, t % 2].reshape(virtuals, -1),
                (((1,), (1,)), ((), ())), preferred_element_type=F32,
            )
            for t in range(2 * nq)
        )
        denominator = occ_e[o] + occ_e[block] - col_e - row_e
        amps[rows, :] = (coulomb / denominator).astype(jnp.bfloat16)

    contract = (((0,), (0,)), ((), ()))
    piece = virtuals // 2 if len(vir.shape) > 2 else 256

    def add_vir(chain):
        rows = span(chain, 2 * width)

        @pl.loop(0, virtuals // piece)
        def _(t):
            new = lax.dot_general(
                amps[rows, span(t, piece)], amps[rows, :], contract, preferred_element_type=F32
            )
            where = span(t, vir.shape[0] * piece // virtuals)
            vir[where] += new.reshape((-1,) + vir.shape[1:])

    def add_three(chain):
        rows = span(chain, 2 * width)

        @pl.loop(0, 2 * nq)
        def _(t):
            three[t // 2, t % 2] += lax.dot_general(
                held[t // 2, t % 2, rows, :], amps[rows, :], contract, preferred_element_type=F32
            )

    def both(chain):
        absorb(2 * chain + low)
        arrived(2 * chain + 1 - low)
        absorb(2 * chain + 1 - low)

    @pl.loop(1, nz)
    def _(k):
        chain = nearest_first(z, k, nz)
        arrived(2 * chain + low)
        for d in range(1, nq):
            held_relay(d, chain, held_slot(d, 2 * chain + low), start)
        before = nearest_first(z, k - 1, nz)
        both(before)
        add_vir(before)
        add_three(before)

    last = nearest_first(z, nz - 1, nz)
    both(last)
    add_vir(last)
    vir_done()
    add_three(last)

    def finish():
        @pl.loop(0, nz)
        def _(chain):
            coef_relay(chain, coef_slot(2 * chain + low), sent)
            for d in range(1, nq):
                held_relay(d, chain, held_slot(d, 2 * chain + low), sent)

        @pl.loop(1, n)
        def _(d):
            block = (o + d) % n
            coef_across(block).wait_send()
            give(block, c).wait_send()

        for r in order:
            to_partner(r).wait_send()
            for d in range(1, nq):
                to_chip(d, r).wait_send()
                onward(d, r, c).wait_send()

    return finish


def reduction(
    n, nq, three, vir, near_out, far_out, vir_out,
    t_pair, t_out, t_far, v_pair, v_sum, v_side, v_line, v_chain, v_col, v_far,
    pair_send, pair_recv, t_send, t_recv, vp_send, vp_recv, x_send, x_recv, z_send, z_recv, y_send, y_recv,
):
    o = lax.axis_index("occ")
    s = lax.axis_index("aux")
    q, c = s // 2, s % 2
    z, low = o // 2, o % 2
    nz = n // 2
    chunks, chunk = v_pair.shape[0], v_pair.shape[-1]
    partner = (o, 2 * q + 1 - c)
    side = (2 * z + 1 - low, s)

    def cols(k):
        return pl.ds(k * chunk, chunk)

    def v_swap(k):
        return remote(vir.at[:, :, 1 - c, :, cols(k)], v_pair.at[k], vp_send.at[k], vp_recv.at[k], partner)

    def x_swap(k):
        return remote(v_sum.at[k, :, 1 - low], v_side.at[k], x_send.at[k], x_recv.at[k], side)

    def along(k, d):
        there = (z + d) % nz
        return remote(
            v_line.at[k, there], v_chain.at[k, d], z_send.at[k, d], z_recv.at[k, d], (2 * there + low, s)
        )

    def between(k, d):
        there = (q + d) % nq
        return remote(v_col.at[k, there], v_far.at[k, d], y_send.at[k, d], y_recv.at[k, d], (o, 2 * there + c))

    def swap(d):
        return remote(three.at[(q + d) % nq, 1 - c], t_pair.at[d], pair_send.at[d], pair_recv.at[d], partner)

    def spread(d):
        return remote(t_out.at[d], t_far.at[d], t_send.at[d], t_recv.at[d], (o, 2 * ((q + d) % nq) + c))

    order = list(range(1, nq)) + [0]

    def open_vir():
        for k in range(chunks):
            v_swap(k).start()

    def close():
        for d in order:
            swap(d).start()
        for k in range(chunks):
            v_swap(k).wait()
            v_sum[k] = (vir[:, :, c, :, cols(k)] + v_pair[k]).reshape(v_sum.shape[1:])
            x_swap(k).start()
        for d in order[:-1]:
            swap(d).wait()
            t_out[d] = three[(q + d) % nq, c] + t_pair[d]
            spread(d).start()
        for k in range(chunks):
            x_swap(k).wait()
            v_line[k] = v_sum[k, :, low] + v_side[k]
            for d in range(1, nz):
                along(k, d).start()
            if k == 0:
                swap(0).wait()
                near_out[...] = three[q, c] + t_pair[0]
        for k in range(chunks):
            held = v_line[k, z]
            for d in range(1, nz):
                along(k, d).wait()
                held += v_chain[k, d]
            v_col[k] = held
            for d in range(1, nq):
                between(k, d).start()
        for d in order[:-1]:
            spread(d).wait()
            far_out[...] = t_far[d] if d == 1 else far_out[...] + t_far[d]
        for k in range(chunks):
            rows = v_col[k, q]
            for d in range(1, nq):
                between(k, d).wait()
                rows += v_far[k, d]
            vir_out[:, cols(k)] = rows

    return open_vir, close


def amplitude_kernel(n, nq, *refs):
    make_densities(n, nq, *refs)()


def reduce_kernel(n, nq, *refs):
    greet(n, nq)()
    open_vir, close = reduction(n, nq, *refs)
    open_vir()
    close()


def whole_kernel(n, nq, inputs, outputs, count, *refs):
    operands, results, scratch = refs[:inputs], refs[inputs : inputs + outputs], refs[inputs + outputs :]
    three, vir, rest = scratch[0], scratch[1], scratch[2:]
    open_vir, close = reduction(n, nq, three, vir, *results, *rest[count:])
    finish = make_densities(n, nq, *operands, three, vir, *rest[:count], vir_done=open_vir)
    close()
    finish()


def paired_kernel(
    n, occ_e, half, coef, vir_e, three_out, vir_out,
    ints, raw, full, own, held, gift, cross, amps, vir,
    t_give, t_got, n_give, n_got, v_pair, v_line, v_col, v_far,
    t_code, t_scale, t_code_in, t_scale_in, x_code, x_scale, x_code_in, x_scale_in,
    z_code, z_scale, z_code_in, z_scale_in,
    i_sem, keep_sem, o_sem, raw_sems, c_recv, c_up, c_down, c_side, cp_send, cp_recv,
    pn_sems, pf_sems, f_recv, f_send, z_fwd, x_fwd, y_send, g_send, g_recv,
    t_sems, ts_send, ts_recv, n_sems, vp_send, vp_recv, x_send, x_recv, z_send, z_recv, yv_send, yv_recv,
):
    o = lax.axis_index("occ")
    s = lax.axis_index("aux")
    q, c = s // 2, s % 2
    z, low = o // 2, o % 2
    nz = n // 2
    far = 1 - q
    part, basis = coef.shape
    tile = raw.shape[0]
    virtuals = full.shape[0]
    width = virtuals // 4
    pieces = c_recv.shape[1]
    piece = basis // (2 * pieces)
    above, below, side = o + 2, o - 2, 2 * z + 1 - low
    other = 2 * q + 1 - c
    partner = (o, other)
    opposite = (o, 2 * far + c)

    def span(index, size):
        return pl.ds(pl.multiple_of(index * size, size), size)

    def start(copy):
        copy.start()

    def sent(copy):
        copy.wait_send()

    def nearest(k):
        return nearest_first(z, k, nz)

    barrier = pltpu.get_barrier_semaphore()
    peers = [partner, opposite, (o, 2 * far + 1 - c), (side, s), (side, other)]
    peers += [(2 * ((z + d) % nz) + low, t) for d in range(1, nz) for t in (s, other)]
    for peer in peers:
        pl.semaphore_signal(barrier, inc=1, device_id=peer, device_id_type=MESH)
    fetch = pltpu.make_async_copy(half, ints, i_sem)
    fetch.start()
    keep = pltpu.make_async_copy(coef, full.at[span(o, part)], keep_sem)
    keep.start()
    pl.semaphore_wait(barrier, len(peers))

    lend = remote(half.at[o], raw, raw_sems.at[0], raw_sems.at[1], opposite)
    lend.start()

    def coef_slot(block, core, h):
        return full.at[span(block, part), pl.ds(pl.multiple_of((pieces * core + h) * piece, piece), piece)]

    def coef_relay(chain, h, src, act):
        block = 2 * chain + low
        dst = coef_slot(block, c, h)
        recv = c_recv.at[block, h]
        pl.when(jnp.logical_and(chain <= z, z < nz - 1))(
            lambda: act(remote(src, dst, c_up.at[chain, h], recv, (above, s)))
        )
        pl.when(jnp.logical_and(chain >= z, z > 0))(
            lambda: act(remote(src, dst, c_down.at[chain, h], recv, (below, s)))
        )
        act(remote(src, dst, c_side.at[chain, h], recv, (side, s)))

    def coef_across(block, h, core):
        ref = coef_slot(block, core, h)
        return remote(ref, ref, cp_send.at[block, h], cp_recv.at[block, h], partner)

    def coef_wait(block, h):
        ref = coef_slot(block, c, h)
        remote(ref, ref, c_side.at[0, h], c_recv.at[block, h], (side, s)).wait_recv()

    for h in range(pieces):
        coef_relay(z, h, coef.at[:, pl.ds(pl.multiple_of((pieces * c + h) * piece, piece), piece)], start)
    row_e = vir_e[...].reshape(1, virtuals)
    here = lax.broadcasted_iota(jnp.int32, (width, virtuals), 0) + s * width
    there = lax.broadcasted_iota(jnp.int32, (width, virtuals), 1)
    col_e = jnp.sum(jnp.where(here == there, row_e, 0.0), axis=1, keepdims=True)

    def coef_beside(k):
        block = 2 * nearest(k) + 1 - low
        for h in range(pieces):
            coef_wait(block, h)
            coef_across(block, h, c).start()

    @pl.loop(1, nz)
    def _(k):
        chain = nearest(k)
        block = 2 * chain + low
        for h in range(pieces):
            coef_wait(block, h)
            coef_relay(chain, h, coef_slot(block, c, h), start)
            coef_across(block, h, c).start()
        coef_beside(k - 1)

    coef_beside(nz - 1)

    @pl.loop(1, n)
    def _(d):
        block = (o + d) % n
        for h in range(pieces):
            coef_across(block, h, 1 - c).wait_recv()

    keep.wait()
    fetch.wait()

    def transform(rows, source):
        return lax.dot_general(rows, source, (((1,), (1,)), ((), ())), preferred_element_type=F32).astype(jnp.bfloat16)

    def cols(group, core):
        return span(2 * group + core, tile)

    def lend_block(block, act):
        for core in range(2):
            act(
                remote(
                    cross.at[block, pl.ds(core * width, width)], held.at[span(block, width), cols(q, c)],
                    y_send.at[block, core], f_recv.at[block, c], (o, 2 * far + core),
                )
            )

    def distant(chain):
        return jnp.abs(chain - z) > 2

    def lend_blocks(k, act):
        chain = nearest(k)
        act(2 * chain + 1 - low)
        pl.when(distant(chain))(lambda: act(2 * chain + low))

    def cross_over(block):
        cross[block] = transform(full[span(far, 2 * width), :], ints[block])
        lend_block(block, start)

    @pl.loop(2, nz)
    def _(k):
        lend_blocks(k, cross_over)

    def own_part(group, core):
        return own.at[:, cols(group, core)]

    def near_part(core):
        ref = own_part(q, core)
        return remote(ref, ref, pn_sems.at[0], pn_sems.at[1], partner)

    def far_part(core):
        ref = own_part(far, core)
        return remote(ref, ref, pf_sems.at[0], pf_sems.at[1], partner)

    def hand_out(act):
        for core in range(2):
            src = own.at[span(2 * q + core, width), cols(far, c)]
            dst = held.at[span(o, width), cols(far, c)]
            recv = f_recv.at[o, c]
            pl.when(z < nz - 1)(lambda: act(remote(src, dst, f_send.at[0, core], recv, (above, 2 * q + core))))
            pl.when(z > 0)(lambda: act(remote(src, dst, f_send.at[1, core], recv, (below, 2 * q + core))))
        for core in range(2):
            src = own.at[span(2 * q + core, width), cols(far, c)]
            dst = held.at[span(o, width), cols(far, c)]
            act(remote(src, dst, f_send.at[2, core], f_recv.at[o, c], (side, 2 * q + core)))

    lend.wait_recv()
    own[:, cols(far, c)] = transform(full[...], raw[...])
    hand_out(start)
    far_part(c).start()
    own[:, cols(q, c)] = transform(full[...], ints[o])
    near_part(c).start()

    def give(block, core):
        return remote(
            gift.at[block], held.at[span(block, width), cols(q, core)], g_send.at[block], g_recv.at[block], partner
        )

    @pl.loop(1, n)
    def _(d):
        block = (o + d) % n
        rows = jnp.concatenate([full[span(s, width), :], full[span(other, width), :]], axis=0)
        both = transform(rows, ints[block])
        held[span(block, width), cols(q, c)] = both[:width]
        gift[block] = both[width:]
        give(block, c).start()

    far_part(1 - c).wait_recv()
    near_part(1 - c).wait_recv()
    mine = pltpu.make_async_copy(own.at[span(s, width)], held.at[span(o, width)], o_sem)
    mine.start()

    def far_slot(block, core):
        return held.at[span(block, width), cols(far, core)]

    def arrive(block):
        for core in range(2):
            ref = far_slot(block, core)
            remote(ref, ref, x_fwd.at[0], f_recv.at[block, core], (side, s)).wait_recv()

    def pass_on(chain, act):
        block = 2 * chain + low
        for core in range(2):
            ref = far_slot(block, core)
            recv = f_recv.at[block, core]
            pl.when(jnp.logical_and(chain < z, z < nz - 1))(
                lambda: act(remote(ref, ref, z_fwd.at[0, core], recv, (above, s)))
            )
            pl.when(jnp.logical_and(chain > z, z > 0))(
                lambda: act(remote(ref, ref, z_fwd.at[1, core], recv, (below, s)))
            )
            pl.when(chain == nearest(1))(lambda: act(remote(ref, ref, x_fwd.at[core], recv, (side, s))))

    def beside_each(act):
        pl.when(z > 0)(lambda: act(z - 1))
        pl.when(z < nz - 1)(lambda: act(z + 1))

    def take(chain):
        arrive(2 * chain + low)
        pass_on(chain, start)

    beside_each(take)
    mine.wait()

    def absorb(chain):
        rows = span(chain, 2 * width)
        coulomb = lax.dot_general(
            held[rows, :], own[...], (((1,), (1,)), ((), ())), preferred_element_type=F32
        )
        left = jnp.concatenate([occ_e[o] + occ_e[2 * chain + t] - col_e for t in range(2)], axis=0)
        amps[rows, :] = (coulomb / (left - row_e)).astype(jnp.bfloat16)

    @pl.loop(0, nz)
    def _(i):
        chain = nearest(jnp.where(i == 0, 0, jnp.where(i == nz - 1, 1, i + 1)))
        pl.when(jnp.abs(chain - z) > 1)(lambda: arrive(2 * chain + low))
        arrive(2 * chain + 1 - low)
        pl.when(chain != z)(lambda: give(2 * chain + low, 1 - c).wait_recv())
        give(2 * chain + 1 - low, 1 - c).wait_recv()
        absorb(chain)

    contract = (((0,), (0,)), ((), ()))
    strips, strip = t_give.shape[0], t_give.shape[-1]
    rows = vir.shape[4]
    middle = virtuals // 2

    def wide(k):
        return pl.ds(k * strip, strip)

    def part_three(group, core, where):
        return lax.dot_general(
            held[:, cols(group, core)], amps[:, where], contract, preferred_element_type=F32
        )

    def far_swap(k):
        return remote(t_give.at[k], t_got.at[k], t_sems.at[0, k], t_sems.at[1, k], partner)

    def coded_copies(code, scale, code_to, scale_to, sems, target):
        return (
            remote(code, code_to, sems[0].at[0], sems[1].at[0], target),
            remote(scale, scale_to, sems[0].at[1], sems[1].at[1], target),
        )

    def far_send(k):
        sems = (ts_send.at[k], ts_recv.at[k])
        return coded_copies(t_code.at[k], t_scale.at[k], t_code_in.at[k], t_scale_in.at[k], sems, opposite)

    def x_swap(chain):
        sems = (x_send.at[chain], x_recv.at[chain])
        return coded_copies(
            x_code.at[chain], x_scale.at[chain], x_code_in.at[chain], x_scale_in.at[chain], sems, (side, s)
        )

    def along(to, sender):
        sems = (z_send.at[to], z_recv.at[sender])
        return coded_copies(
            z_code.at[to], z_scale.at[to], z_code_in.at[sender], z_scale_in.at[sender], sems, (2 * to + low, s)
        )

    def both_start(copies):
        for copy in copies:
            copy.start()

    def both_recv(copies):
        for copy in copies:
            copy.wait_recv()

    def both_sent(copies):
        for copy in copies:
            copy.wait_send()

    def encode(value, code, scale):
        parts = scale.shape[0]
        size = value.shape[0] // parts
        grouped = value.reshape(parts, size, value.shape[1])
        top = jnp.maximum(jnp.max(jnp.abs(grouped), axis=1, keepdims=True), TINY)
        scale[...] = top
        code[...] = jnp.exp(grouped * (SPAN / top)).astype(jnp.bfloat16).reshape(value.shape)

    def decode(code, scale):
        parts = scale.shape[0]
        words = jnp.log(code[...].astype(F32)).reshape(parts, code.shape[0] // parts, code.shape[1])
        return (words * (scale[...] * (1.0 / SPAN))).reshape(code.shape)

    def v_swap(chain):
        return remote(vir.at[chain, :, :, 1 - c], v_pair.at[chain], vp_send.at[chain], vp_recv.at[chain], partner)

    def between():
        return remote(v_col.at[far], v_far, yv_send, yv_recv, opposite)

    near_swap = remote(n_give, n_got, n_sems.at[0], n_sems.at[1], partner)
    first = jnp.where(z < nz // 2, 1, 0)
    for half in (first, 1 - first):
        new = lax.dot_general(
            amps[:, span(half, middle)], amps[...], contract, preferred_element_type=F32
        )
        vir[pl.ds(half * (nz // 2), nz // 2)] = new.reshape((nz // 2,) + vir.shape[1:])
        for t in range(nz // 2):
            v_swap(half * (nz // 2) + t).start()

    def pair_sum(chain, across):
        return (vir[chain, across, :, c] + v_pair[chain, across]).reshape(2 * rows, virtuals)

    farthest = [nearest(k) for k in reversed(range(nz))]

    def add_pair(chain):
        v_swap(chain).wait_recv()
        encode(pair_sum(chain, 1 - low), x_code.at[chain], x_scale.at[chain])
        both_start(x_swap(chain))

    for k in range(max(strips, nz)):
        if k < strips:
            t_give[k] = part_three(far, 1 - c, wide(k))
            far_swap(k).start()
        if k < nz:
            add_pair(farthest[k])
    for k in range(strips):
        new = part_three(far, c, wide(k))
        far_swap(k).wait_recv()
        encode(new + t_got[k], t_code.at[k], t_scale.at[k])
        both_start(far_send(k))
    n_give[...] = part_three(q, 1 - c, slice(None))
    near_swap.start()
    three_out[...] = part_three(q, c, slice(None))
    for chain in farthest:
        both_recv(x_swap(chain))
        total = pair_sum(chain, low) + decode(x_code_in.at[chain], x_scale_in.at[chain])
        v_line[...] = total
        if chain is not farthest[-1]:
            encode(total, z_code.at[chain], z_scale.at[chain])
            both_start(along(chain, z))
    near_swap.wait_recv()
    three_out[...] += n_got[...]
    for k in range(1, nz):
        sender = nearest(k)
        both_recv(along(sender, sender))
        v_line[...] += decode(z_code_in.at[sender], z_scale_in.at[sender])
    v_col[...] = v_line[...].reshape(v_col.shape)
    between().start()
    for k in range(strips):
        both_recv(far_send(k))
        three_out[:, wide(k)] += decode(t_code_in.at[k], t_scale_in.at[k])
    between().wait_recv()
    vir_out[...] = (v_col[q] + v_far[...]) / (n * virtuals)

    lend.wait_send()

    @pl.loop(0, nz)
    def _(chain):
        for h in range(pieces):
            coef_relay(chain, h, coef_slot(2 * chain + low, c, h), sent)

    @pl.loop(1, n)
    def _(d):
        block = (o + d) % n
        for h in range(pieces):
            coef_across(block, h, c).wait_send()
        give(block, c).wait_send()

    @pl.loop(2, nz)
    def _(k):
        lend_blocks(k, lambda block: lend_block(block, sent))

    hand_out(sent)
    far_part(c).wait_send()
    near_part(c).wait_send()
    beside_each(lambda chain: pass_on(chain, sent))
    near_swap.wait_send()
    for k in range(strips):
        far_swap(k).wait_send()
        both_sent(far_send(k))
    for chain in range(nz):
        v_swap(chain).wait_send()
        both_sent(x_swap(chain))
    for k in range(1, nz):
        both_sent(along(nearest(k), z))
    between().wait_send()


def paired(n, half_integrals, coef, occ_energy, vir_energy):
    _, tile, basis = half_integrals.shape
    part = coef.shape[0]
    virtuals = part * n
    width, rows, nz = virtuals // 4, virtuals // (4 * n), n // 2
    pieces = PIECES if basis % (256 * PIECES) == 0 else 1
    vmem = pl.BlockSpec(memory_space=pltpu.VMEM)
    dma = pltpu.SemaphoreType.DMA
    lanes = 128
    chunks = virtuals // lanes
    strip = 2 * lanes if chunks % 2 == 0 else lanes
    strips = virtuals // strip

    def room(*shape):
        return pltpu.VMEM(shape, F32)

    def packed(*shape):
        return pltpu.VMEM(shape, jnp.bfloat16)

    scratch = [
        packed(n, tile, basis), packed(tile, basis), packed(virtuals, basis), packed(virtuals, 4 * tile),
        packed(n * width, 4 * tile), packed(n, width, tile), packed(n, 2 * width, tile), packed(n * width, virtuals),
        room(nz, 2, 2, 2, rows, virtuals),
        room(strips, tile, strip), room(strips, tile, strip), room(tile, virtuals), room(tile, virtuals),
        room(nz, 2, 2, rows, virtuals), room(2 * rows, virtuals), room(2, rows, virtuals), room(rows, virtuals),
    ]
    groups = tile // 32
    for _ in range(2):
        scratch += [packed(strips, tile, strip), room(strips, groups, 1, strip)]
    for _ in range(4):
        scratch += [packed(nz, 2 * rows, virtuals), room(nz, 2, 1, virtuals)]
    scratch += [
        dma, dma, dma, dma((2,)), dma((n, pieces)), dma((nz, pieces)), dma((nz, pieces)), dma((nz, pieces)),
        dma((n, pieces)), dma((n, pieces)),
        dma((2,)), dma((2,)), dma((n, 2)), dma((3, 2)), dma((2, 2)), dma((2,)), dma((n, 2)), dma((n,)), dma((n,)),
        dma((2, strips)), dma((strips, 2)), dma((strips, 2)), dma((2,)),
        dma((nz,)), dma((nz,)), dma((nz, 2)), dma((nz, 2)), dma((nz, 2)), dma((nz, 2)), dma, dma,
    ]
    return pl.pallas_call(
        functools.partial(paired_kernel, n),
        out_shape=(
            jax.ShapeDtypeStruct((tile, virtuals), F32), jax.ShapeDtypeStruct((rows, virtuals), F32),
        ),
        in_specs=[pl.BlockSpec(memory_space=pltpu.SMEM), pl.BlockSpec(memory_space=pl.ANY), vmem, vmem],
        out_specs=(vmem, vmem),
        scratch_shapes=scratch,
        compiler_params=pltpu.CompilerParams(
            collective_id=0, has_side_effects=True, vmem_limit_bytes=LIMIT
        ),
        name="densities",
    )(occ_energy, half_integrals, coef, vir_energy)


def per_device(half_integrals, vir_coef, occ_energy, vir_energy):
    n, aux = lax.axis_size("occ"), lax.axis_size("aux")
    nz, nq = n // 2, aux // 2
    _, tile, basis = half_integrals.shape
    part = vir_coef.shape[1]
    virtuals = part * n
    if nq == 2 and n % 2 == 0 and nz > 1 and nz % 2 == 0 and virtuals % (32 * n) == 0 and virtuals % 256 == 0 and tile % 32 == 0:
        three, vir_rows = paired(n, half_integrals, vir_coef.T, occ_energy, vir_energy)
        return three[:, None, :], vir_rows
    width, rows = virtuals // aux, virtuals // (n * aux)
    vmem = pl.BlockSpec(memory_space=pltpu.VMEM)
    dma = pltpu.SemaphoreType.DMA
    half = jnp.bfloat16
    lanes = 128
    chunks = virtuals // lanes

    def room(*shape):
        return pltpu.VMEM(shape, F32)

    def result(*shape):
        return jax.ShapeDtypeStruct(shape, F32)

    def call(kernel, name, number, in_specs, out_shape, scratch, operands):
        return pl.pallas_call(
            kernel,
            out_shape=out_shape,
            in_specs=in_specs,
            out_specs=(vmem,) * len(out_shape),
            scratch_shapes=scratch,
            compiler_params=pltpu.CompilerParams(
                collective_id=number, has_side_effects=True, vmem_limit_bytes=LIMIT
            ),
            name=name,
        )(*operands)

    operands = (occ_energy, half_integrals, vir_coef.T, vir_energy)
    specs = [pl.BlockSpec(memory_space=pltpu.SMEM), pl.BlockSpec(memory_space=pl.ANY), vmem, vmem]
    make_scratch = [
        pltpu.VMEM(half_integrals.shape, half),
        pltpu.VMEM((2, virtuals, basis // 2), half),
        pltpu.VMEM((nq, 2, nq, 2 * width, tile), half),
        pltpu.VMEM((nq, 2, n * width, tile), half),
        pltpu.VMEM((n, width, tile), half),
        pltpu.VMEM((n * width, virtuals), half),
        dma, dma((2,)), dma, dma((n,)), dma((nz,)), dma((nz,)), dma((nz,)), dma((n,)), dma((n,)),
        dma((nq, nq)), dma((nq, nq)), dma((nq, nq)), dma((nq, nq)), dma((nq,)), dma((nq,)), dma((n,)), dma((n,)),
        dma((nq, n)), dma((nq, nz)), dma((nq, nz)), dma((nq, nz)),
    ]
    reduce_scratch = [
        room(nq, tile, virtuals), room(nq, tile, virtuals), room(nq, tile, virtuals),
        room(chunks, n, nq, rows, lanes), room(chunks, nz, 2, nq, rows, lanes),
        room(chunks, nz, nq, rows, lanes), room(chunks, nz, nq, rows, lanes), room(chunks, nz, nq, rows, lanes),
        room(chunks, nq, rows, lanes), room(chunks, nq, rows, lanes),
        dma((nq,)), dma((nq,)), dma((nq,)), dma((nq,)), dma((chunks,)), dma((chunks,)), dma((chunks,)), dma((chunks,)),
        dma((chunks, nz)), dma((chunks, nz)), dma((chunks, nq)), dma((chunks, nq)),
    ]
    sums = (nq, 2, tile, virtuals)
    groups = (n, nq, 2, rows, virtuals)
    finals = (result(tile, virtuals), result(tile, virtuals), result(rows, virtuals))
    if rows % 8 == 0:
        kernel = functools.partial(whole_kernel, n, nq, len(specs), len(finals), len(make_scratch))
        scratch = [room(*sums), room(*groups)] + make_scratch + reduce_scratch
        near, far, vir_rows = call(kernel, "densities", 0, specs, finals, scratch, operands)
    else:
        kernel = functools.partial(amplitude_kernel, n, nq)
        partials = (result(*sums), result(virtuals, virtuals))
        three, vir = call(kernel, "amplitude", 0, specs, partials, make_scratch, operands)
        kernel = functools.partial(reduce_kernel, n, nq)
        near, far, vir_rows = call(
            kernel, "reduce", 1, [vmem, vmem], finals, reduce_scratch, (three, vir.reshape(groups))
        )
    return (near + far)[:, None, :], vir_rows / (n * virtuals)


def solution(mesh):
    return jax.shard_map(
        per_device,
        mesh=mesh,
        in_specs=(P(None, "aux", None), P(None, "occ"), P(), P()),
        out_specs=(P("aux", "occ", None), P(("occ", "aux"), None)),
        check_vma=False,
    )
```

```python
import functools

import jax
import jax.numpy as jnp
from jax import lax
from jax.experimental import pallas as pl
from jax.experimental.pallas import tpu as pltpu
from jax.sharding import PartitionSpec as P

MESH = pl.DeviceIdType.MESH
F32 = jnp.float32
PIECES = 4
SPAN = 80.0
TINY = 1e-30
LIMIT = 56 * 1024 * 1024


def remote(src, dst, send, recv, target):
    return pltpu.make_async_remote_copy(
        src_ref=src, dst_ref=dst, send_sem=send, recv_sem=recv, device_id=target, device_id_type=MESH
    )


def nearest_first(z, k, count):
    near = jnp.minimum(z, count - 1 - z)
    step = (k + 1) // 2
    both = z + step * (2 * (k % 2) - 1)
    low = z < count - 1 - z
    return jnp.where(k <= 2 * near, both, jnp.where(low, k, count - 1 - k))


def greet(n, nq):
    o = lax.axis_index("occ")
    s = lax.axis_index("aux")
    q, c = s // 2, s % 2
    z, low = o // 2, o % 2
    nz = n // 2
    barrier = pltpu.get_barrier_semaphore()
    peers = [(2 * z + 1 - low, s), (o, 2 * q + 1 - c)]
    peers += [(o, 2 * ((q + d) % nq) + c) for d in range(1, nq)]
    peers += [(2 * ((z + d) % nz) + low, s) for d in range(1, nz)]
    for peer in peers:
        pl.semaphore_signal(barrier, inc=1, device_id=peer, device_id_type=MESH)
    return lambda: pl.semaphore_wait(barrier, len(peers))


def make_densities(
    n, nq, occ_e, half, coef, vir_e, three, vir,
    ints, full, own, held, gift, amps,
    i_sem, c_copy, o_copy, c_recv, c_up, c_down, c_side, cp_send, cp_recv,
    own_send, own_recv, fw_send, fw_recv, pr_send, pr_recv, g_send, g_recv,
    h_recv, h_up, h_down, h_side,
    vir_done=lambda: None,
):
    o = lax.axis_index("occ")
    s = lax.axis_index("aux")
    q, c = s // 2, s % 2
    z, low = o // 2, o % 2
    nz = n // 2
    width = amps.shape[0] // n
    part = coef.shape[0]
    cut = coef.shape[1] // 2
    virtuals = amps.shape[1]
    above, below, side = o + 2, o - 2, 2 * z + 1 - low
    partner = (o, 2 * q + 1 - c)
    entered = greet(n, nq)

    fetch = pltpu.make_async_copy(half, ints, i_sem)
    fetch.start()

    def span(index, size):
        return pl.ds(pl.multiple_of(index * size, size), size)

    def keep(h):
        return pltpu.make_async_copy(coef.at[:, h * cut : (h + 1) * cut], full.at[h, span(o, part)], c_copy.at[h])

    keep(0).start()
    keep(1).start()
    entered()

    def relay(chain, src, dst, up, down, across, recv, act):
        pl.when(jnp.logical_and(chain <= z, z < nz - 1))(lambda: act(remote(src, dst, up, recv, (above, s))))
        pl.when(jnp.logical_and(chain >= z, z > 0))(lambda: act(remote(src, dst, down, recv, (below, s))))
        act(remote(src, dst, across, recv, (side, s)))

    def start(copy):
        copy.start()

    def sent(copy):
        copy.wait_send()

    def coef_slot(block):
        return full.at[c, span(block, part)]

    def coef_relay(chain, src, act):
        block = 2 * chain + low
        relay(chain, src, coef_slot(block), c_up.at[chain], c_down.at[chain], c_side.at[chain], c_recv.at[block], act)

    def coef_across(block):
        return remote(coef_slot(block), coef_slot(block), cp_send.at[block], cp_recv.at[block], partner)

    def coef_arrived(block):
        remote(coef_slot(block), coef_slot(block), c_side.at[0], c_recv.at[block], (side, s)).wait_recv()
        coef_across(block).start()

    coef_relay(z, coef.at[:, span(c, cut)], start)
    three[...] = jnp.zeros_like(three)
    vir[...] = jnp.zeros_like(vir)
    row_e = vir_e[...].reshape(1, virtuals)
    here = lax.broadcasted_iota(jnp.int32, (width, virtuals), 0) + s * width
    there = lax.broadcasted_iota(jnp.int32, (width, virtuals), 1)
    col_e = jnp.sum(jnp.where(here == there, row_e, 0.0), axis=1, keepdims=True)

    @pl.loop(1, nz)
    def _(k):
        chain = nearest_first(z, k, nz)
        block = 2 * chain + low
        remote(coef_slot(block), coef_slot(block), c_side.at[0], c_recv.at[block], (side, s)).wait_recv()
        coef_relay(chain, coef_slot(block), start)
        coef_across(block).start()
        coef_arrived(2 * nearest_first(z, k - 1, nz) + 1 - low)

    coef_arrived(2 * nearest_first(z, nz - 1, nz) + 1 - low)

    @pl.loop(1, n)
    def _(d):
        block = (o + d) % n
        other = full.at[1 - c, span(block, part)]
        remote(other, other, cp_send.at[block], cp_recv.at[block], partner).wait_recv()

    keep(0).wait()
    keep(1).wait()
    fetch.wait()

    def transform(block, rows):
        contract = (((1,), (1,)), ((), ()))
        return sum(
            lax.dot_general(
                full[h, rows, :], ints[block, :, h * cut : (h + 1) * cut], contract, preferred_element_type=F32
            )
            for h in range(2)
        ).astype(jnp.bfloat16)

    order = list(range(1, nq)) + [0]

    def chunk(there, core, group):
        return own.at[there, core, group]

    def to_partner(r):
        ref = chunk(q, c, (q + r) % nq)
        return remote(ref, ref, pr_send.at[r], pr_recv.at[r], partner)

    def to_chip(d, r):
        ref = chunk(q, c, (q + r) % nq)
        return remote(ref, ref, own_send.at[d, r], own_recv.at[d, r], (o, 2 * ((q + d) % nq) + c))

    def onward(d, r, core):
        there = (q + nq - d) % nq
        ref = chunk(there, core, (there + r) % nq)
        return remote(ref, ref, fw_send.at[d, r], fw_recv.at[d, r], partner)

    def from_chip(d, r):
        there = (q + nq - d) % nq
        ref = chunk(there, c, (there + r) % nq)
        remote(ref, ref, own_send.at[d, r], own_recv.at[d, r], partner).wait_recv()
        onward(d, r, c).start()

    for r in order:
        group = (q + r) % nq
        own[q, c, group] = transform(o, span(group, 2 * width))
        for d in range(1, nq):
            to_chip(d, r).start()
        to_partner(r).start()

    def give(block, core):
        return remote(
            gift.at[block], held.at[q, core, span(block, width)], g_send.at[block], g_recv.at[block], partner
        )

    @pl.loop(1, n)
    def _(d):
        block = (o + d) % n
        gift[block] = transform(block, span(2 * q + 1 - c, width))
        give(block, c).start()
        held[q, c, span(block, width), :] = transform(block, span(s, width))

    def held_slot(d, block):
        return held.at[(q + nq - d) % nq, :, span(block, width)]

    def own_slot(d):
        return own.at[(q + nq - d) % nq, :, q, span(c, width)]

    def held_relay(d, chain, src, act):
        block = 2 * chain + low
        relay(
            chain, src, held_slot(d, block), h_up.at[d, chain], h_down.at[d, chain], h_side.at[d, chain],
            h_recv.at[d, block], act,
        )

    def arrived(block):
        for d in range(1, nq):
            ref = held_slot(d, block)
            remote(ref, ref, h_side.at[d, 0], h_recv.at[d, block], (side, s)).wait_recv()

    for d in range(1, nq):
        from_chip(d, d)
    for d in range(1, nq):
        onward(d, d, 1 - c).wait_recv()
        held_relay(d, z, own_slot(d), start)
    rest = [(d, r) for d in range(1, nq) for r in order if r != d]
    for d, r in rest:
        from_chip(d, r)
    for r in order:
        ref = chunk(q, 1 - c, (q + r) % nq)
        remote(ref, ref, pr_send.at[r], pr_recv.at[r], partner).wait_recv()

    @pl.loop(1, n)
    def _(d):
        give((o + d) % n, 1 - c).wait_recv()

    for d, r in rest:
        onward(d, r, 1 - c).wait_recv()
    mine = pltpu.make_async_copy(
        own.at[:, :, q, span(c, width)], held.at[:, :, span(o, width)], o_copy
    )
    mine.start()
    mine.wait()

    def absorb(block):
        rows = span(block, width)
        coulomb = sum(
            lax.dot_general(
                held[t // 2, t % 2, rows, :], own[t // 2, t % 2].reshape(virtuals, -1),
                (((1,), (1,)), ((), ())), preferred_element_type=F32,
            )
            for t in range(2 * nq)
        )
        denominator = occ_e[o] + occ_e[block] - col_e - row_e
        amps[rows, :] = (coulomb / denominator).astype(jnp.bfloat16)

    contract = (((0,), (0,)), ((), ()))
    piece = virtuals // 2 if len(vir.shape) > 2 else 256

    def add_vir(chain):
        rows = span(chain, 2 * width)

        @pl.loop(0, virtuals // piece)
        def _(t):
            new = lax.dot_general(
                amps[rows, span(t, piece)], amps[rows, :], contract, preferred_element_type=F32
            )
            where = span(t, vir.shape[0] * piece // virtuals)
            vir[where] += new.reshape((-1,) + vir.shape[1:])

    def add_three(chain):
        rows = span(chain, 2 * width)

        @pl.loop(0, 2 * nq)
        def _(t):
            three[t // 2, t % 2] += lax.dot_general(
                held[t // 2, t % 2, rows, :], amps[rows, :], contract, preferred_element_type=F32
            )

    def both(chain):
        absorb(2 * chain + low)
        arrived(2 * chain + 1 - low)
        absorb(2 * chain + 1 - low)

    @pl.loop(1, nz)
    def _(k):
        chain = nearest_first(z, k, nz)
        arrived(2 * chain + low)
        for d in range(1, nq):
            held_relay(d, chain, held_slot(d, 2 * chain + low), start)
        before = nearest_first(z, k - 1, nz)
        both(before)
        add_vir(before)
        add_three(before)

    last = nearest_first(z, nz - 1, nz)
    both(last)
    add_vir(last)
    vir_done()
    add_three(last)

    def finish():
        @pl.loop(0, nz)
        def _(chain):
            coef_relay(chain, coef_slot(2 * chain + low), sent)
            for d in range(1, nq):
                held_relay(d, chain, held_slot(d, 2 * chain + low), sent)

        @pl.loop(1, n)
        def _(d):
            block = (o + d) % n
            coef_across(block).wait_send()
            give(block, c).wait_send()

        for r in order:
            to_partner(r).wait_send()
            for d in range(1, nq):
                to_chip(d, r).wait_send()
                onward(d, r, c).wait_send()

    return finish


def reduction(
    n, nq, three, vir, near_out, far_out, vir_out,
    t_pair, t_out, t_far, v_pair, v_sum, v_side, v_line, v_chain, v_col, v_far,
    pair_send, pair_recv, t_send, t_recv, vp_send, vp_recv, x_send, x_recv, z_send, z_recv, y_send, y_recv,
):
    o = lax.axis_index("occ")
    s = lax.axis_index("aux")
    q, c = s // 2, s % 2
    z, low = o // 2, o % 2
    nz = n // 2
    chunks, chunk = v_pair.shape[0], v_pair.shape[-1]
    partner = (o, 2 * q + 1 - c)
    side = (2 * z + 1 - low, s)

    def cols(k):
        return pl.ds(k * chunk, chunk)

    def v_swap(k):
        return remote(vir.at[:, :, 1 - c, :, cols(k)], v_pair.at[k], vp_send.at[k], vp_recv.at[k], partner)

    def x_swap(k):
        return remote(v_sum.at[k, :, 1 - low], v_side.at[k], x_send.at[k], x_recv.at[k], side)

    def along(k, d):
        there = (z + d) % nz
        return remote(
            v_line.at[k, there], v_chain.at[k, d], z_send.at[k, d], z_recv.at[k, d], (2 * there + low, s)
        )

    def between(k, d):
        there = (q + d) % nq
        return remote(v_col.at[k, there], v_far.at[k, d], y_send.at[k, d], y_recv.at[k, d], (o, 2 * there + c))

    def swap(d):
        return remote(three.at[(q + d) % nq, 1 - c], t_pair.at[d], pair_send.at[d], pair_recv.at[d], partner)

    def spread(d):
        return remote(t_out.at[d], t_far.at[d], t_send.at[d], t_recv.at[d], (o, 2 * ((q + d) % nq) + c))

    order = list(range(1, nq)) + [0]

    def open_vir():
        for k in range(chunks):
            v_swap(k).start()

    def close():
        for d in order:
            swap(d).start()
        for k in range(chunks):
            v_swap(k).wait()
            v_sum[k] = (vir[:, :, c, :, cols(k)] + v_pair[k]).reshape(v_sum.shape[1:])
            x_swap(k).start()
        for d in order[:-1]:
            swap(d).wait()
            t_out[d] = three[(q + d) % nq, c] + t_pair[d]
            spread(d).start()
        for k in range(chunks):
            x_swap(k).wait()
            v_line[k] = v_sum[k, :, low] + v_side[k]
            for d in range(1, nz):
                along(k, d).start()
            if k == 0:
                swap(0).wait()
                near_out[...] = three[q, c] + t_pair[0]
        for k in range(chunks):
            held = v_line[k, z]
            for d in range(1, nz):
                along(k, d).wait()
                held += v_chain[k, d]
            v_col[k] = held
            for d in range(1, nq):
                between(k, d).start()
        for d in order[:-1]:
            spread(d).wait()
            far_out[...] = t_far[d] if d == 1 else far_out[...] + t_far[d]
        for k in range(chunks):
            rows = v_col[k, q]
            for d in range(1, nq):
                between(k, d).wait()
                rows += v_far[k, d]
            vir_out[:, cols(k)] = rows

    return open_vir, close


def amplitude_kernel(n, nq, *refs):
    make_densities(n, nq, *refs)()


def reduce_kernel(n, nq, *refs):
    greet(n, nq)()
    open_vir, close = reduction(n, nq, *refs)
    open_vir()
    close()


def whole_kernel(n, nq, inputs, outputs, count, *refs):
    operands, results, scratch = refs[:inputs], refs[inputs : inputs + outputs], refs[inputs + outputs :]
    three, vir, rest = scratch[0], scratch[1], scratch[2:]
    open_vir, close = reduction(n, nq, three, vir, *results, *rest[count:])
    finish = make_densities(n, nq, *operands, three, vir, *rest[:count], vir_done=open_vir)
    close()
    finish()


def paired_kernel(
    n, occ_e, half, coef, vir_e, three_out, vir_out,
    ints, raw, full, own, held, gift, cross, amps, vir,
    t_give, t_got, n_give, n_got, near_sum, v_pair, v_line, v_col,
    t_code, t_scale, t_code_in, t_scale_in, x_code, x_scale, x_code_in, x_scale_in,
    z_code, z_scale, z_code_in, z_scale_in, y_code, y_scale, y_code_in, y_scale_in, energies, levels,
    e_sems, i_sem, keep_sem, o_sem, raw_sems, c_recv, c_up, c_down, c_side, c_jump, cp_send, cp_recv,
    pn_sems, pf_sems, f_recv, f_send, z_fwd, x_fwd, y_send, g_send, g_recv,
    t_sems, ts_send, ts_recv, n_sems, vp_send, vp_recv, x_send, x_recv, z_send, z_recv, yv_send, yv_recv,
):
    o = lax.axis_index("occ")
    s = lax.axis_index("aux")
    q, c = s // 2, s % 2
    z, low = o // 2, o % 2
    nz = n // 2
    far = 1 - q
    part, basis = coef.shape
    tile = raw.shape[0]
    virtuals = full.shape[0]
    width = virtuals // 4
    pieces = c_recv.shape[1]
    piece = basis // (2 * pieces)
    above, below, side = o + 2, o - 2, 2 * z + 1 - low
    other = 2 * q + 1 - c
    partner = (o, other)
    opposite = (o, 2 * far + c)

    def span(index, size):
        return pl.ds(pl.multiple_of(index * size, size), size)

    def start(copy):
        copy.start()

    def sent(copy):
        copy.wait_send()

    def nearest(k):
        return nearest_first(z, k, nz)

    barrier = pltpu.get_barrier_semaphore()
    peers = [partner, opposite, (o, 2 * far + 1 - c), (side, s), (side, other)]
    peers += [(2 * ((z + d) % nz) + low, t) for d in range(1, nz) for t in (s, other)]
    for peer in peers:
        pl.semaphore_signal(barrier, inc=1, device_id=peer, device_id_type=MESH)
    small = [pltpu.make_async_copy(occ_e, energies, e_sems.at[0]), pltpu.make_async_copy(vir_e, levels, e_sems.at[1])]
    fetch = pltpu.make_async_copy(half, ints, i_sem)
    fetch.start()
    keep = pltpu.make_async_copy(coef, full.at[span(o, part)], keep_sem)
    keep.start()
    for copy in small:
        copy.start()
    pl.semaphore_wait(barrier, len(peers))

    lend = remote(half.at[o], raw, raw_sems.at[0], raw_sems.at[1], opposite)
    lend.start()

    def coef_slot(block, core, h):
        return full.at[span(block, part), pl.ds(pl.multiple_of((pieces * core + h) * piece, piece), piece)]

    def coef_relay(chain, h, src, act):
        block = 2 * chain + low
        dst = coef_slot(block, c, h)
        recv = c_recv.at[block, h]
        pl.when(jnp.logical_and(jnp.logical_and(chain <= z, chain > z - 2), z < nz - 1))(
            lambda: act(remote(src, dst, c_up.at[chain, h], recv, (above, s)))
        )
        pl.when(jnp.logical_and(jnp.logical_and(chain >= z, chain < z + 2), z > 0))(
            lambda: act(remote(src, dst, c_down.at[chain, h], recv, (below, s)))
        )
        act(remote(src, dst, c_side.at[chain, h], recv, (side, s)))

    def coef_across(block, h, core):
        ref = coef_slot(block, core, h)
        return remote(ref, ref, cp_send.at[block, h], cp_recv.at[block, h], partner)

    def coef_wait(block, h):
        ref = coef_slot(block, c, h)
        remote(ref, ref, c_side.at[0, h], c_recv.at[block, h], (side, s)).wait_recv()

    def coef_far(h, act):
        src = coef.at[:, pl.ds(pl.multiple_of((pieces * c + h) * piece, piece), piece)]
        recv = c_recv.at[o, h]
        for d in range(3, nz):
            pl.when(z + d < nz)(
                lambda: act(remote(src, coef_slot(o, c, h), c_jump.at[0, d, h], recv, (o + 2 * d, s)))
            )
            pl.when(z >= d)(
                lambda: act(remote(src, coef_slot(o, c, h), c_jump.at[1, d, h], recv, (o - 2 * d, s)))
            )

    for h in range(pieces):
        coef_far(h, start)
        coef_relay(z, h, coef.at[:, pl.ds(pl.multiple_of((pieces * c + h) * piece, piece), piece)], start)
    for copy in small:
        copy.wait()
    row_e = levels[...].reshape(1, virtuals)
    here = lax.broadcasted_iota(jnp.int32, (width, virtuals), 0) + s * width
    there = lax.broadcasted_iota(jnp.int32, (width, virtuals), 1)
    col_e = jnp.sum(jnp.where(here == there, row_e, 0.0), axis=1, keepdims=True)

    def coef_beside(k):
        block = 2 * nearest(k) + 1 - low
        for h in range(pieces):
            coef_wait(block, h)
            coef_across(block, h, c).start()

    @pl.loop(1, nz)
    def _(k):
        chain = nearest(k)
        block = 2 * chain + low
        for h in range(pieces):
            coef_wait(block, h)
            coef_relay(chain, h, coef_slot(block, c, h), start)
            coef_across(block, h, c).start()
        coef_beside(k - 1)

    coef_beside(nz - 1)

    @pl.loop(1, n)
    def _(d):
        block = (o + d) % n
        for h in range(pieces):
            coef_across(block, h, 1 - c).wait_recv()

    keep.wait()
    fetch.wait()

    def transform(rows, source):
        return lax.dot_general(rows, source, (((1,), (1,)), ((), ())), preferred_element_type=F32).astype(jnp.bfloat16)

    def cols(group, core):
        return span(2 * group + core, tile)

    def lend_block(block, act):
        for core in range(2):
            act(
                remote(
                    cross.at[block, pl.ds(core * width, width)], held.at[span(block, width), cols(q, c)],
                    y_send.at[block, core], f_recv.at[block, c], (o, 2 * far + core),
                )
            )

    def distant(chain):
        return jnp.abs(chain - z) > 2

    def lend_blocks(k, act):
        chain = nearest(k)
        act(2 * chain + 1 - low)
        pl.when(distant(chain))(lambda: act(2 * chain + low))

    def cross_over(block):
        cross[block] = transform(full[span(far, 2 * width), :], ints[block])
        lend_block(block, start)

    @pl.loop(2, nz)
    def _(k):
        lend_blocks(k, cross_over)

    def own_part(group, core):
        return own.at[:, cols(group, core)]

    def near_part(core):
        ref = own_part(q, core)
        return remote(ref, ref, pn_sems.at[0], pn_sems.at[1], partner)

    def far_part(core):
        ref = own_part(far, core)
        return remote(ref, ref, pf_sems.at[0], pf_sems.at[1], partner)

    def hand_out(act):
        for core in range(2):
            src = own.at[span(2 * q + core, width), cols(far, c)]
            dst = held.at[span(o, width), cols(far, c)]
            recv = f_recv.at[o, c]
            pl.when(z < nz - 1)(lambda: act(remote(src, dst, f_send.at[0, core], recv, (above, 2 * q + core))))
            pl.when(z > 0)(lambda: act(remote(src, dst, f_send.at[1, core], recv, (below, 2 * q + core))))
        for core in range(2):
            src = own.at[span(2 * q + core, width), cols(far, c)]
            dst = held.at[span(o, width), cols(far, c)]
            act(remote(src, dst, f_send.at[2, core], f_recv.at[o, c], (side, 2 * q + core)))

    lend.wait_recv()
    own[:, cols(far, c)] = transform(full[...], raw[...])
    hand_out(start)
    far_part(c).start()
    own[:, cols(q, c)] = transform(full[...], ints[o])
    near_part(c).start()

    def give(block, core):
        return remote(
            gift.at[block], held.at[span(block, width), cols(q, core)], g_send.at[block], g_recv.at[block], partner
        )

    @pl.loop(1, n)
    def _(d):
        block = (o + d) % n
        rows = jnp.concatenate([full[span(s, width), :], full[span(other, width), :]], axis=0)
        both = transform(rows, ints[block])
        held[span(block, width), cols(q, c)] = both[:width]
        gift[block] = both[width:]
        give(block, c).start()

    far_part(1 - c).wait_recv()
    near_part(1 - c).wait_recv()
    mine = pltpu.make_async_copy(own.at[span(s, width)], held.at[span(o, width)], o_sem)
    mine.start()

    def far_slot(block, core):
        return held.at[span(block, width), cols(far, core)]

    def arrive(block):
        for core in range(2):
            ref = far_slot(block, core)
            remote(ref, ref, x_fwd.at[0], f_recv.at[block, core], (side, s)).wait_recv()

    def pass_on(chain, act):
        block = 2 * chain + low
        for core in range(2):
            ref = far_slot(block, core)
            recv = f_recv.at[block, core]
            pl.when(jnp.logical_and(chain < z, z < nz - 1))(
                lambda: act(remote(ref, ref, z_fwd.at[0, core], recv, (above, s)))
            )
            pl.when(jnp.logical_and(chain > z, z > 0))(
                lambda: act(remote(ref, ref, z_fwd.at[1, core], recv, (below, s)))
            )
            pl.when(chain == nearest(1))(lambda: act(remote(ref, ref, x_fwd.at[core], recv, (side, s))))

    def beside_each(act):
        pl.when(z > 0)(lambda: act(z - 1))
        pl.when(z < nz - 1)(lambda: act(z + 1))

    def take(chain):
        arrive(2 * chain + low)
        pass_on(chain, start)

    beside_each(take)
    mine.wait()

    def absorb(chain):
        rows = span(chain, 2 * width)
        coulomb = lax.dot_general(
            held[rows, :], own[...], (((1,), (1,)), ((), ())), preferred_element_type=F32
        )
        left = jnp.concatenate([energies[o] + energies[2 * chain + t] - col_e for t in range(2)], axis=0)
        amps[rows, :] = (coulomb / (left - row_e)).astype(jnp.bfloat16)

    @pl.loop(0, nz)
    def _(i):
        chain = nearest(jnp.where(i == 0, 0, jnp.where(i == nz - 1, 1, i + 1)))
        pl.when(jnp.abs(chain - z) > 1)(lambda: arrive(2 * chain + low))
        arrive(2 * chain + 1 - low)
        pl.when(chain != z)(lambda: give(2 * chain + low, 1 - c).wait_recv())
        give(2 * chain + 1 - low, 1 - c).wait_recv()
        absorb(chain)

    contract = (((0,), (0,)), ((), ()))
    strips, strip = t_give.shape[0], t_give.shape[-1]
    rows = vir.shape[4]
    middle = virtuals // 2

    def wide(k):
        return pl.ds(k * strip, strip)

    def part_three(group, core, where):
        return lax.dot_general(
            held[:, cols(group, core)], amps[:, where], contract, preferred_element_type=F32
        )

    def far_swap(k):
        return remote(t_give.at[k], t_got.at[k], t_sems.at[0, k], t_sems.at[1, k], partner)

    def coded_copies(code, scale, code_to, scale_to, sems, target):
        return (
            remote(code, code_to, sems[0].at[0], sems[1].at[0], target),
            remote(scale, scale_to, sems[0].at[1], sems[1].at[1], target),
        )

    def far_send(k):
        sems = (ts_send.at[k], ts_recv.at[k])
        return coded_copies(t_code.at[k], t_scale.at[k], t_code_in.at[k], t_scale_in.at[k], sems, opposite)

    def x_swap(chain):
        sems = (x_send.at[chain], x_recv.at[chain])
        return coded_copies(
            x_code.at[chain], x_scale.at[chain], x_code_in.at[chain], x_scale_in.at[chain], sems, (side, s)
        )

    def along(to, sender):
        sems = (z_send.at[to], z_recv.at[sender])
        return coded_copies(
            z_code.at[to], z_scale.at[to], z_code_in.at[sender], z_scale_in.at[sender], sems, (2 * to + low, s)
        )

    def both_start(copies):
        for copy in copies:
            copy.start()

    def both_recv(copies):
        for copy in copies:
            copy.wait_recv()

    def both_sent(copies):
        for copy in copies:
            copy.wait_send()

    def encode(value, code, scale):
        parts = scale.shape[0]
        size = value.shape[0] // parts
        grouped = value.reshape(parts, size, value.shape[1])
        top = jnp.maximum(jnp.max(jnp.abs(grouped), axis=1, keepdims=True), TINY)
        scale[...] = top
        code[...] = jnp.exp(grouped * (SPAN / top)).astype(jnp.bfloat16).reshape(value.shape)

    def decode(code, scale):
        parts = scale.shape[0]
        words = jnp.log(code[...].astype(F32)).reshape(parts, code.shape[0] // parts, code.shape[1])
        return (words * (scale[...] * (1.0 / SPAN))).reshape(code.shape)

    def v_swap(chain):
        return remote(vir.at[chain, :, :, 1 - c], v_pair.at[chain], vp_send.at[chain], vp_recv.at[chain], partner)

    def between():
        return coded_copies(y_code, y_scale, y_code_in, y_scale_in, (yv_send, yv_recv), opposite)

    near_swap = remote(n_give, n_got, n_sems.at[0], n_sems.at[1], partner)
    first = jnp.where(z < nz // 2, 1, 0)
    for half in (first, 1 - first):
        new = lax.dot_general(
            amps[:, span(half, middle)], amps[...], contract, preferred_element_type=F32
        )
        vir[pl.ds(half * (nz // 2), nz // 2)] = new.reshape((nz // 2,) + vir.shape[1:])
        for t in range(nz // 2):
            v_swap(half * (nz // 2) + t).start()

    def pair_sum(chain, across):
        return (vir[chain, across, :, c] + v_pair[chain, across]).reshape(2 * rows, virtuals)

    farthest = [nearest(k) for k in reversed(range(nz))]

    def add_pair(chain):
        v_swap(chain).wait_recv()
        encode(pair_sum(chain, 1 - low), x_code.at[chain], x_scale.at[chain])
        both_start(x_swap(chain))

    for k in range(max(strips, nz)):
        if k < strips:
            t_give[k] = part_three(far, 1 - c, wide(k))
            far_swap(k).start()
        if k < nz:
            add_pair(farthest[k])
    for k in range(strips):
        new = part_three(far, c, wide(k))
        far_swap(k).wait_recv()
        encode(new + t_got[k], t_code.at[k], t_scale.at[k])
        both_start(far_send(k))
    def add_beside(chain, last):
        both_recv(x_swap(chain))
        total = pair_sum(chain, low) + decode(x_code_in.at[chain], x_scale_in.at[chain])
        if last:
            v_line[...] = total
        else:
            encode(total, z_code.at[chain], z_scale.at[chain])
            both_start(along(chain, z))

    def near_give():
        n_give[...] = part_three(q, 1 - c, slice(None))
        near_swap.start()

    def near_keep():
        near_sum[...] = part_three(q, c, slice(None))

    fillers = [near_give, near_keep]
    for k in range(nz):
        add_beside(farthest[k], k == nz - 1)
        if k < len(fillers):
            fillers[k]()
    for filler in fillers[nz:]:
        filler()
    near_swap.wait_recv()
    near_sum[...] += n_got[...]
    for k in range(1, nz):
        sender = nearest(k)
        both_recv(along(sender, sender))
        v_line[...] += decode(z_code_in.at[sender], z_scale_in.at[sender])
    v_col[...] = v_line[...].reshape(v_col.shape)
    encode(v_col[far], y_code, y_scale)
    both_start(between())
    for k in range(strips):
        both_recv(far_send(k))
        near_sum[:, wide(k)] += decode(t_code_in.at[k], t_scale_in.at[k])
    three_out[...] = near_sum[...].reshape(three_out.shape)
    both_recv(between())
    vir_out[...] = (v_col[q] + decode(y_code_in, y_scale_in)) / (n * virtuals)

    lend.wait_send()

    @pl.loop(0, nz)
    def _(chain):
        for h in range(pieces):
            coef_relay(chain, h, coef_slot(2 * chain + low, c, h), sent)

    for h in range(pieces):
        coef_far(h, sent)

    @pl.loop(1, n)
    def _(d):
        block = (o + d) % n
        for h in range(pieces):
            coef_across(block, h, c).wait_send()
        give(block, c).wait_send()

    @pl.loop(2, nz)
    def _(k):
        lend_blocks(k, lambda block: lend_block(block, sent))

    hand_out(sent)
    far_part(c).wait_send()
    near_part(c).wait_send()
    beside_each(lambda chain: pass_on(chain, sent))
    near_swap.wait_send()
    for k in range(strips):
        far_swap(k).wait_send()
        both_sent(far_send(k))
    for chain in range(nz):
        v_swap(chain).wait_send()
        both_sent(x_swap(chain))
    for k in range(1, nz):
        both_sent(along(nearest(k), z))
    both_sent(between())


def paired(n, half_integrals, coef, occ_energy, vir_energy):
    _, tile, basis = half_integrals.shape
    part = coef.shape[0]
    virtuals = part * n
    width, rows, nz = virtuals // 4, virtuals // (4 * n), n // 2
    pieces = PIECES if basis % (256 * PIECES) == 0 else 1
    vmem = pl.BlockSpec(memory_space=pltpu.VMEM)
    dma = pltpu.SemaphoreType.DMA
    lanes = 128
    chunks = virtuals // lanes
    strip = 2 * lanes if chunks % 2 == 0 else lanes
    strips = virtuals // strip

    def room(*shape):
        return pltpu.VMEM(shape, F32)

    def packed(*shape):
        return pltpu.VMEM(shape, jnp.bfloat16)

    scratch = [
        packed(n, tile, basis), packed(tile, basis), packed(virtuals, basis), packed(virtuals, 4 * tile),
        packed(n * width, 4 * tile), packed(n, width, tile), packed(n, 2 * width, tile), packed(n * width, virtuals),
        room(nz, 2, 2, 2, rows, virtuals),
        room(strips, tile, strip), room(strips, tile, strip), room(tile, virtuals), room(tile, virtuals),
        room(tile, virtuals), room(nz, 2, 2, rows, virtuals), room(2 * rows, virtuals), room(2, rows, virtuals),
    ]
    groups = tile // 32
    for _ in range(2):
        scratch += [packed(strips, tile, strip), room(strips, groups, 1, strip)]
    for _ in range(4):
        scratch += [packed(nz, 2 * rows, virtuals), room(nz, 2, 1, virtuals)]
    for _ in range(2):
        scratch += [packed(rows, virtuals), room(1, 1, virtuals)]
    scratch += [pltpu.SMEM((n,), F32), room(virtuals)]
    scratch += [
        dma((2,)), dma, dma, dma, dma((2,)), dma((n, pieces)), dma((nz, pieces)), dma((nz, pieces)), dma((nz, pieces)), dma((2, nz, pieces)),
        dma((n, pieces)), dma((n, pieces)),
        dma((2,)), dma((2,)), dma((n, 2)), dma((3, 2)), dma((2, 2)), dma((2,)), dma((n, 2)), dma((n,)), dma((n,)),
        dma((2, strips)), dma((strips, 2)), dma((strips, 2)), dma((2,)),
        dma((nz,)), dma((nz,)), dma((nz, 2)), dma((nz, 2)), dma((nz, 2)), dma((nz, 2)), dma((2,)), dma((2,)),
    ]
    return pl.pallas_call(
        functools.partial(paired_kernel, n),
        out_shape=(
            pltpu.VMEM((tile, 1, virtuals), F32), pltpu.VMEM((rows, virtuals), F32),
        ),
        in_specs=[pl.BlockSpec(memory_space=pl.ANY)] * 4,
        out_specs=(vmem, vmem),
        scratch_shapes=scratch,
        compiler_params=pltpu.CompilerParams(
            collective_id=0, has_side_effects=True, vmem_limit_bytes=LIMIT
        ),
        name="densities",
    )(occ_energy, half_integrals, coef, vir_energy)


def per_device(half_integrals, vir_coef, occ_energy, vir_energy):
    n, aux = lax.axis_size("occ"), lax.axis_size("aux")
    nz, nq = n // 2, aux // 2
    _, tile, basis = half_integrals.shape
    part = vir_coef.shape[1]
    virtuals = part * n
    if nq == 2 and n % 2 == 0 and nz > 1 and nz % 2 == 0 and virtuals % (32 * n) == 0 and virtuals % 256 == 0 and tile % 32 == 0:
        three, vir_rows = paired(n, half_integrals, vir_coef.T, occ_energy, vir_energy)
        return three, vir_rows
    width, rows = virtuals // aux, virtuals // (n * aux)
    vmem = pl.BlockSpec(memory_space=pltpu.VMEM)
    dma = pltpu.SemaphoreType.DMA
    half = jnp.bfloat16
    lanes = 128
    chunks = virtuals // lanes

    def room(*shape):
        return pltpu.VMEM(shape, F32)

    def result(*shape):
        return jax.ShapeDtypeStruct(shape, F32)

    def call(kernel, name, number, in_specs, out_shape, scratch, operands):
        return pl.pallas_call(
            kernel,
            out_shape=out_shape,
            in_specs=in_specs,
            out_specs=(vmem,) * len(out_shape),
            scratch_shapes=scratch,
            compiler_params=pltpu.CompilerParams(
                collective_id=number, has_side_effects=True, vmem_limit_bytes=LIMIT
            ),
            name=name,
        )(*operands)

    operands = (occ_energy, half_integrals, vir_coef.T, vir_energy)
    specs = [pl.BlockSpec(memory_space=pltpu.SMEM), pl.BlockSpec(memory_space=pl.ANY), vmem, vmem]
    make_scratch = [
        pltpu.VMEM(half_integrals.shape, half),
        pltpu.VMEM((2, virtuals, basis // 2), half),
        pltpu.VMEM((nq, 2, nq, 2 * width, tile), half),
        pltpu.VMEM((nq, 2, n * width, tile), half),
        pltpu.VMEM((n, width, tile), half),
        pltpu.VMEM((n * width, virtuals), half),
        dma, dma((2,)), dma, dma((n,)), dma((nz,)), dma((nz,)), dma((nz,)), dma((n,)), dma((n,)),
        dma((nq, nq)), dma((nq, nq)), dma((nq, nq)), dma((nq, nq)), dma((nq,)), dma((nq,)), dma((n,)), dma((n,)),
        dma((nq, n)), dma((nq, nz)), dma((nq, nz)), dma((nq, nz)),
    ]
    reduce_scratch = [
        room(nq, tile, virtuals), room(nq, tile, virtuals), room(nq, tile, virtuals),
        room(chunks, n, nq, rows, lanes), room(chunks, nz, 2, nq, rows, lanes),
        room(chunks, nz, nq, rows, lanes), room(chunks, nz, nq, rows, lanes), room(chunks, nz, nq, rows, lanes),
        room(chunks, nq, rows, lanes), room(chunks, nq, rows, lanes),
        dma((nq,)), dma((nq,)), dma((nq,)), dma((nq,)), dma((chunks,)), dma((chunks,)), dma((chunks,)), dma((chunks,)),
        dma((chunks, nz)), dma((chunks, nz)), dma((chunks, nq)), dma((chunks, nq)),
    ]
    sums = (nq, 2, tile, virtuals)
    groups = (n, nq, 2, rows, virtuals)
    finals = (result(tile, virtuals), result(tile, virtuals), result(rows, virtuals))
    if rows % 8 == 0:
        kernel = functools.partial(whole_kernel, n, nq, len(specs), len(finals), len(make_scratch))
        scratch = [room(*sums), room(*groups)] + make_scratch + reduce_scratch
        near, far, vir_rows = call(kernel, "densities", 0, specs, finals, scratch, operands)
    else:
        kernel = functools.partial(amplitude_kernel, n, nq)
        partials = (result(*sums), result(virtuals, virtuals))
        three, vir = call(kernel, "amplitude", 0, specs, partials, make_scratch, operands)
        kernel = functools.partial(reduce_kernel, n, nq)
        near, far, vir_rows = call(
            kernel, "reduce", 1, [vmem, vmem], finals, reduce_scratch, (three, vir.reshape(groups))
        )
    return (near + far)[:, None, :], vir_rows / (n * virtuals)


def solution(mesh):
    return jax.shard_map(
        per_device,
        mesh=mesh,
        in_specs=(P(None, "aux", None), P(None, "occ"), P(), P()),
        out_specs=(P("aux", "occ", None), P(("occ", "aux"), None)),
        check_vma=False,
    )
```

```python
import functools

import jax
import jax.numpy as jnp
from jax import lax
from jax.experimental import pallas as pl
from jax.experimental.pallas import tpu as pltpu
from jax.sharding import PartitionSpec as P

MESH = pl.DeviceIdType.MESH
F32 = jnp.float32
PIECES = 4
SPAN = 80.0
TINY = 1e-30
LIMIT = 56 * 1024 * 1024


def remote(src, dst, send, recv, target):
    return pltpu.make_async_remote_copy(
        src_ref=src, dst_ref=dst, send_sem=send, recv_sem=recv, device_id=target, device_id_type=MESH
    )


def nearest_first(z, k, count):
    near = jnp.minimum(z, count - 1 - z)
    step = (k + 1) // 2
    both = z + step * (2 * (k % 2) - 1)
    low = z < count - 1 - z
    return jnp.where(k <= 2 * near, both, jnp.where(low, k, count - 1 - k))


def greet(n, nq):
    o = lax.axis_index("occ")
    s = lax.axis_index("aux")
    q, c = s // 2, s % 2
    z, low = o // 2, o % 2
    nz = n // 2
    barrier = pltpu.get_barrier_semaphore()
    peers = [(2 * z + 1 - low, s), (o, 2 * q + 1 - c)]
    peers += [(o, 2 * ((q + d) % nq) + c) for d in range(1, nq)]
    peers += [(2 * ((z + d) % nz) + low, s) for d in range(1, nz)]
    for peer in peers:
        pl.semaphore_signal(barrier, inc=1, device_id=peer, device_id_type=MESH)
    return lambda: pl.semaphore_wait(barrier, len(peers))


def make_densities(
    n, nq, occ_e, half, coef, vir_e, three, vir,
    ints, full, own, held, gift, amps,
    i_sem, c_copy, o_copy, c_recv, c_up, c_down, c_side, cp_send, cp_recv,
    own_send, own_recv, fw_send, fw_recv, pr_send, pr_recv, g_send, g_recv,
    h_recv, h_up, h_down, h_side,
    vir_done=lambda: None,
):
    o = lax.axis_index("occ")
    s = lax.axis_index("aux")
    q, c = s // 2, s % 2
    z, low = o // 2, o % 2
    nz = n // 2
    width = amps.shape[0] // n
    part = coef.shape[0]
    cut = coef.shape[1] // 2
    virtuals = amps.shape[1]
    above, below, side = o + 2, o - 2, 2 * z + 1 - low
    partner = (o, 2 * q + 1 - c)
    entered = greet(n, nq)

    fetch = pltpu.make_async_copy(half, ints, i_sem)
    fetch.start()

    def span(index, size):
        return pl.ds(pl.multiple_of(index * size, size), size)

    def keep(h):
        return pltpu.make_async_copy(coef.at[:, h * cut : (h + 1) * cut], full.at[h, span(o, part)], c_copy.at[h])

    keep(0).start()
    keep(1).start()
    entered()

    def relay(chain, src, dst, up, down, across, recv, act):
        pl.when(jnp.logical_and(chain <= z, z < nz - 1))(lambda: act(remote(src, dst, up, recv, (above, s))))
        pl.when(jnp.logical_and(chain >= z, z > 0))(lambda: act(remote(src, dst, down, recv, (below, s))))
        act(remote(src, dst, across, recv, (side, s)))

    def start(copy):
        copy.start()

    def sent(copy):
        copy.wait_send()

    def coef_slot(block):
        return full.at[c, span(block, part)]

    def coef_relay(chain, src, act):
        block = 2 * chain + low
        relay(chain, src, coef_slot(block), c_up.at[chain], c_down.at[chain], c_side.at[chain], c_recv.at[block], act)

    def coef_across(block):
        return remote(coef_slot(block), coef_slot(block), cp_send.at[block], cp_recv.at[block], partner)

    def coef_arrived(block):
        remote(coef_slot(block), coef_slot(block), c_side.at[0], c_recv.at[block], (side, s)).wait_recv()
        coef_across(block).start()

    coef_relay(z, coef.at[:, span(c, cut)], start)
    three[...] = jnp.zeros_like(three)
    vir[...] = jnp.zeros_like(vir)
    row_e = vir_e[...].reshape(1, virtuals)
    here = lax.broadcasted_iota(jnp.int32, (width, virtuals), 0) + s * width
    there = lax.broadcasted_iota(jnp.int32, (width, virtuals), 1)
    col_e = jnp.sum(jnp.where(here == there, row_e, 0.0), axis=1, keepdims=True)

    @pl.loop(1, nz)
    def _(k):
        chain = nearest_first(z, k, nz)
        block = 2 * chain + low
        remote(coef_slot(block), coef_slot(block), c_side.at[0], c_recv.at[block], (side, s)).wait_recv()
        coef_relay(chain, coef_slot(block), start)
        coef_across(block).start()
        coef_arrived(2 * nearest_first(z, k - 1, nz) + 1 - low)

    coef_arrived(2 * nearest_first(z, nz - 1, nz) + 1 - low)

    @pl.loop(1, n)
    def _(d):
        block = (o + d) % n
        other = full.at[1 - c, span(block, part)]
        remote(other, other, cp_send.at[block], cp_recv.at[block], partner).wait_recv()

    keep(0).wait()
    keep(1).wait()
    fetch.wait()

    def transform(block, rows):
        contract = (((1,), (1,)), ((), ()))
        return sum(
            lax.dot_general(
                full[h, rows, :], ints[block, :, h * cut : (h + 1) * cut], contract, preferred_element_type=F32
            )
            for h in range(2)
        ).astype(jnp.bfloat16)

    order = list(range(1, nq)) + [0]

    def chunk(there, core, group):
        return own.at[there, core, group]

    def to_partner(r):
        ref = chunk(q, c, (q + r) % nq)
        return remote(ref, ref, pr_send.at[r], pr_recv.at[r], partner)

    def to_chip(d, r):
        ref = chunk(q, c, (q + r) % nq)
        return remote(ref, ref, own_send.at[d, r], own_recv.at[d, r], (o, 2 * ((q + d) % nq) + c))

    def onward(d, r, core):
        there = (q + nq - d) % nq
        ref = chunk(there, core, (there + r) % nq)
        return remote(ref, ref, fw_send.at[d, r], fw_recv.at[d, r], partner)

    def from_chip(d, r):
        there = (q + nq - d) % nq
        ref = chunk(there, c, (there + r) % nq)
        remote(ref, ref, own_send.at[d, r], own_recv.at[d, r], partner).wait_recv()
        onward(d, r, c).start()

    for r in order:
        group = (q + r) % nq
        own[q, c, group] = transform(o, span(group, 2 * width))
        for d in range(1, nq):
            to_chip(d, r).start()
        to_partner(r).start()

    def give(block, core):
        return remote(
            gift.at[block], held.at[q, core, span(block, width)], g_send.at[block], g_recv.at[block], partner
        )

    @pl.loop(1, n)
    def _(d):
        block = (o + d) % n
        gift[block] = transform(block, span(2 * q + 1 - c, width))
        give(block, c).start()
        held[q, c, span(block, width), :] = transform(block, span(s, width))

    def held_slot(d, block):
        return held.at[(q + nq - d) % nq, :, span(block, width)]

    def own_slot(d):
        return own.at[(q + nq - d) % nq, :, q, span(c, width)]

    def held_relay(d, chain, src, act):
        block = 2 * chain + low
        relay(
            chain, src, held_slot(d, block), h_up.at[d, chain], h_down.at[d, chain], h_side.at[d, chain],
            h_recv.at[d, block], act,
        )

    def arrived(block):
        for d in range(1, nq):
            ref = held_slot(d, block)
            remote(ref, ref, h_side.at[d, 0], h_recv.at[d, block], (side, s)).wait_recv()

    for d in range(1, nq):
        from_chip(d, d)
    for d in range(1, nq):
        onward(d, d, 1 - c).wait_recv()
        held_relay(d, z, own_slot(d), start)
    rest = [(d, r) for d in range(1, nq) for r in order if r != d]
    for d, r in rest:
        from_chip(d, r)
    for r in order:
        ref = chunk(q, 1 - c, (q + r) % nq)
        remote(ref, ref, pr_send.at[r], pr_recv.at[r], partner).wait_recv()

    @pl.loop(1, n)
    def _(d):
        give((o + d) % n, 1 - c).wait_recv()

    for d, r in rest:
        onward(d, r, 1 - c).wait_recv()
    mine = pltpu.make_async_copy(
        own.at[:, :, q, span(c, width)], held.at[:, :, span(o, width)], o_copy
    )
    mine.start()
    mine.wait()

    def absorb(block):
        rows = span(block, width)
        coulomb = sum(
            lax.dot_general(
                held[t // 2, t % 2, rows, :], own[t // 2, t % 2].reshape(virtuals, -1),
                (((1,), (1,)), ((), ())), preferred_element_type=F32,
            )
            for t in range(2 * nq)
        )
        denominator = occ_e[o] + occ_e[block] - col_e - row_e
        amps[rows, :] = (coulomb / denominator).astype(jnp.bfloat16)

    contract = (((0,), (0,)), ((), ()))
    piece = virtuals // 2 if len(vir.shape) > 2 else 256

    def add_vir(chain):
        rows = span(chain, 2 * width)

        @pl.loop(0, virtuals // piece)
        def _(t):
            new = lax.dot_general(
                amps[rows, span(t, piece)], amps[rows, :], contract, preferred_element_type=F32
            )
            where = span(t, vir.shape[0] * piece // virtuals)
            vir[where] += new.reshape((-1,) + vir.shape[1:])

    def add_three(chain):
        rows = span(chain, 2 * width)

        @pl.loop(0, 2 * nq)
        def _(t):
            three[t // 2, t % 2] += lax.dot_general(
                held[t // 2, t % 2, rows, :], amps[rows, :], contract, preferred_element_type=F32
            )

    def both(chain):
        absorb(2 * chain + low)
        arrived(2 * chain + 1 - low)
        absorb(2 * chain + 1 - low)

    @pl.loop(1, nz)
    def _(k):
        chain = nearest_first(z, k, nz)
        arrived(2 * chain + low)
        for d in range(1, nq):
            held_relay(d, chain, held_slot(d, 2 * chain + low), start)
        before = nearest_first(z, k - 1, nz)
        both(before)
        add_vir(before)
        add_three(before)

    last = nearest_first(z, nz - 1, nz)
    both(last)
    add_vir(last)
    vir_done()
    add_three(last)

    def finish():
        @pl.loop(0, nz)
        def _(chain):
            coef_relay(chain, coef_slot(2 * chain + low), sent)
            for d in range(1, nq):
                held_relay(d, chain, held_slot(d, 2 * chain + low), sent)

        @pl.loop(1, n)
        def _(d):
            block = (o + d) % n
            coef_across(block).wait_send()
            give(block, c).wait_send()

        for r in order:
            to_partner(r).wait_send()
            for d in range(1, nq):
                to_chip(d, r).wait_send()
                onward(d, r, c).wait_send()

    return finish


def reduction(
    n, nq, three, vir, near_out, far_out, vir_out,
    t_pair, t_out, t_far, v_pair, v_sum, v_side, v_line, v_chain, v_col, v_far,
    pair_send, pair_recv, t_send, t_recv, vp_send, vp_recv, x_send, x_recv, z_send, z_recv, y_send, y_recv,
):
    o = lax.axis_index("occ")
    s = lax.axis_index("aux")
    q, c = s // 2, s % 2
    z, low = o // 2, o % 2
    nz = n // 2
    chunks, chunk = v_pair.shape[0], v_pair.shape[-1]
    partner = (o, 2 * q + 1 - c)
    side = (2 * z + 1 - low, s)

    def cols(k):
        return pl.ds(k * chunk, chunk)

    def v_swap(k):
        return remote(vir.at[:, :, 1 - c, :, cols(k)], v_pair.at[k], vp_send.at[k], vp_recv.at[k], partner)

    def x_swap(k):
        return remote(v_sum.at[k, :, 1 - low], v_side.at[k], x_send.at[k], x_recv.at[k], side)

    def along(k, d):
        there = (z + d) % nz
        return remote(
            v_line.at[k, there], v_chain.at[k, d], z_send.at[k, d], z_recv.at[k, d], (2 * there + low, s)
        )

    def between(k, d):
        there = (q + d) % nq
        return remote(v_col.at[k, there], v_far.at[k, d], y_send.at[k, d], y_recv.at[k, d], (o, 2 * there + c))

    def swap(d):
        return remote(three.at[(q + d) % nq, 1 - c], t_pair.at[d], pair_send.at[d], pair_recv.at[d], partner)

    def spread(d):
        return remote(t_out.at[d], t_far.at[d], t_send.at[d], t_recv.at[d], (o, 2 * ((q + d) % nq) + c))

    order = list(range(1, nq)) + [0]

    def open_vir():
        for k in range(chunks):
            v_swap(k).start()

    def close():
        for d in order:
            swap(d).start()
        for k in range(chunks):
            v_swap(k).wait()
            v_sum[k] = (vir[:, :, c, :, cols(k)] + v_pair[k]).reshape(v_sum.shape[1:])
            x_swap(k).start()
        for d in order[:-1]:
            swap(d).wait()
            t_out[d] = three[(q + d) % nq, c] + t_pair[d]
            spread(d).start()
        for k in range(chunks):
            x_swap(k).wait()
            v_line[k] = v_sum[k, :, low] + v_side[k]
            for d in range(1, nz):
                along(k, d).start()
            if k == 0:
                swap(0).wait()
                near_out[...] = three[q, c] + t_pair[0]
        for k in range(chunks):
            held = v_line[k, z]
            for d in range(1, nz):
                along(k, d).wait()
                held += v_chain[k, d]
            v_col[k] = held
            for d in range(1, nq):
                between(k, d).start()
        for d in order[:-1]:
            spread(d).wait()
            far_out[...] = t_far[d] if d == 1 else far_out[...] + t_far[d]
        for k in range(chunks):
            rows = v_col[k, q]
            for d in range(1, nq):
                between(k, d).wait()
                rows += v_far[k, d]
            vir_out[:, cols(k)] = rows

    return open_vir, close


def amplitude_kernel(n, nq, *refs):
    make_densities(n, nq, *refs)()


def reduce_kernel(n, nq, *refs):
    greet(n, nq)()
    open_vir, close = reduction(n, nq, *refs)
    open_vir()
    close()


def whole_kernel(n, nq, inputs, outputs, count, *refs):
    operands, results, scratch = refs[:inputs], refs[inputs : inputs + outputs], refs[inputs + outputs :]
    three, vir, rest = scratch[0], scratch[1], scratch[2:]
    open_vir, close = reduction(n, nq, three, vir, *results, *rest[count:])
    finish = make_densities(n, nq, *operands, three, vir, *rest[:count], vir_done=open_vir)
    close()
    finish()


def paired_kernel(
    n, occ_e, half, coef, vir_e, three_out, vir_out,
    ints, raw, full, own, held, gift, cross, amps, vir,
    t_give, t_got, n_give, n_got, near_sum, v_pair, v_line, v_col,
    t_code, t_scale, t_code_in, t_scale_in, x_code, x_scale, x_code_in, x_scale_in,
    z_code, z_scale, z_code_in, z_scale_in, y_code, y_scale, y_code_in, y_scale_in, energies, levels,
    e_sems, i_sem, keep_sem, o_sem, raw_sems, c_recv, c_up, c_down, c_side, c_jump, cp_sems,
    pn_sems, pf_sems, f_recv, f_send, z_fwd, x_fwd, y_send, g_sems,
    t_send, t_recv, ts_send, ts_recv, n_sems, vp_send, vp_recv, x_send, x_recv, z_send, z_recv, yv_send, yv_recv,
):
    o = lax.axis_index("occ")
    s = lax.axis_index("aux")
    q, c = s // 2, s % 2
    z, low = o // 2, o % 2
    nz = n // 2
    far = 1 - q
    part, basis = coef.shape
    tile = raw.shape[0]
    virtuals = full.shape[0]
    width = virtuals // 4
    pieces = c_recv.shape[1]
    piece = basis // (2 * pieces)
    above, below, side = o + 2, o - 2, 2 * z + 1 - low
    other = 2 * q + 1 - c
    partner = (o, other)
    opposite = (o, 2 * far + c)

    def span(index, size):
        return pl.ds(pl.multiple_of(index * size, size), size)

    def start(copy):
        copy.start()

    def sent(copy):
        copy.wait_send()

    def nearest(k):
        return nearest_first(z, k, nz)

    barrier = pltpu.get_barrier_semaphore()
    peers = [partner, opposite, (o, 2 * far + 1 - c), (side, s), (side, other)]
    peers += [(2 * ((z + d) % nz) + low, t) for d in range(1, nz) for t in (s, other)]
    for peer in peers:
        pl.semaphore_signal(barrier, inc=1, device_id=peer, device_id_type=MESH)
    small = [pltpu.make_async_copy(occ_e, energies, e_sems.at[0]), pltpu.make_async_copy(vir_e, levels, e_sems.at[1])]
    fetch = pltpu.make_async_copy(half, ints, i_sem)
    fetch.start()
    keep = pltpu.make_async_copy(coef, full.at[span(o, part)], keep_sem)
    keep.start()
    for copy in small:
        copy.start()
    pl.semaphore_wait(barrier, len(peers))

    lend = remote(half.at[o], raw, raw_sems.at[0], raw_sems.at[1], opposite)
    lend.start()

    def coef_slot(block, core, h):
        return full.at[span(block, part), pl.ds(pl.multiple_of((pieces * core + h) * piece, piece), piece)]

    def coef_relay(chain, src, dst, recv, act):
        pl.when(jnp.logical_and(jnp.logical_and(chain <= z, chain > z - 2), z < nz - 1))(
            lambda: act(remote(src, dst, c_up.at[z - chain], recv, (above, s)))
        )
        pl.when(jnp.logical_and(jnp.logical_and(chain >= z, chain < z + 2), z > 0))(
            lambda: act(remote(src, dst, c_down.at[chain - z], recv, (below, s)))
        )
        act(remote(src, dst, c_side.at[chain], recv, (side, s)))

    def coef_across(block, h, core):
        ref = coef_slot(block, core, h)
        return remote(ref, ref, cp_sems.at[0], cp_sems.at[1], partner)

    def coef_wait(block, h):
        ref = coef_slot(block, c, h)
        remote(ref, ref, c_side.at[0], c_recv.at[block, h], (side, s)).wait_recv()

    def coef_own(h):
        return coef.at[:, pl.ds(pl.multiple_of((pieces * c + h) * piece, piece), piece)]

    def coef_far(src, dst, recv, act):
        for d in range(3, nz):
            pl.when(z + d < nz)(
                lambda: act(remote(src, dst, c_jump.at[0, d], recv, (o + 2 * d, s)))
            )
            pl.when(z >= d)(
                lambda: act(remote(src, dst, c_jump.at[1, d], recv, (o - 2 * d, s)))
            )

    for h in range(pieces):
        coef_far(coef_own(h), coef_slot(o, c, h), c_recv.at[o, h], start)
        coef_relay(z, coef_own(h), coef_slot(o, c, h), c_recv.at[o, h], start)
    for copy in small:
        copy.wait()
    row_e = levels[...].reshape(1, virtuals)
    here = lax.broadcasted_iota(jnp.int32, (width, virtuals), 0) + s * width
    there = lax.broadcasted_iota(jnp.int32, (width, virtuals), 1)
    col_e = jnp.sum(jnp.where(here == there, row_e, 0.0), axis=1, keepdims=True)

    def coef_beside(k):
        block = 2 * nearest(k) + 1 - low
        for h in range(pieces):
            coef_wait(block, h)
            coef_across(block, h, c).start()

    @pl.loop(1, nz)
    def _(k):
        chain = nearest(k)
        block = 2 * chain + low
        for h in range(pieces):
            coef_wait(block, h)
            coef_relay(chain, coef_slot(block, c, h), coef_slot(block, c, h), c_recv.at[block, h], start)
            coef_across(block, h, c).start()
        coef_beside(k - 1)

    coef_beside(nz - 1)

    def coef_halves(blocks):
        ref = full.at[: blocks * part, : basis // 2]
        return remote(ref, ref, cp_sems.at[0], cp_sems.at[1], partner)

    coef_halves(n - 1).wait_recv()

    keep.wait()
    fetch.wait()

    def transform(rows, source):
        return lax.dot_general(rows, source, (((1,), (1,)), ((), ())), preferred_element_type=F32).astype(jnp.bfloat16)

    def cols(group, core):
        return span(2 * group + core, tile)

    def lend_block(block, sem, act):
        for core in range(2):
            act(
                remote(
                    cross.at[block, pl.ds(core * width, width)], held.at[span(block, width), cols(q, c)],
                    y_send.at[sem], f_recv.at[block], (o, 2 * far + core),
                )
            )

    def distant(chain):
        return jnp.abs(chain - z) > 2

    def cross_over(block, sem):
        cross[block] = transform(full[span(far, 2 * width), :], ints[block])
        lend_block(block, sem, start)

    @pl.loop(2, nz)
    def _(k):
        chain = nearest(k)
        cross_over(2 * chain + 1 - low, 0)
        pl.when(distant(chain))(lambda: cross_over(2 * chain + low, k - 1))

    def own_part(group, core):
        return own.at[:, cols(group, core)]

    def near_part(core):
        ref = own_part(q, core)
        return remote(ref, ref, pn_sems.at[0], pn_sems.at[1], partner)

    def far_part(core):
        ref = own_part(far, core)
        return remote(ref, ref, pf_sems.at[0], pf_sems.at[1], partner)

    def hand_out(pairs, act):
        for core, src, dst in pairs:
            recv = f_recv.at[o]
            pl.when(z < nz - 1)(lambda: act(remote(src, dst, f_send.at[0], recv, (above, 2 * q + core))))
            pl.when(z > 0)(lambda: act(remote(src, dst, f_send.at[1], recv, (below, 2 * q + core))))
        for core, src, dst in pairs:
            act(remote(src, dst, f_send.at[2], f_recv.at[o], (side, 2 * q + core)))

    outgoing = [
        (core, own.at[span(2 * q + core, width), cols(far, c)], held.at[span(o, width), cols(far, c)])
        for core in range(2)
    ]

    lend.wait_recv()
    own[:, cols(far, c)] = transform(full[...], raw[...])
    hand_out(outgoing, start)
    far_part(c).start()
    own[:, cols(q, c)] = transform(full[...], ints[o])
    near_part(c).start()

    def give(block, core):
        return remote(
            gift.at[block], held.at[span(block, width), cols(q, core)], g_sems.at[0], g_sems.at[1], partner
        )

    @pl.loop(1, n)
    def _(d):
        block = (o + d) % n
        rows = jnp.concatenate([full[span(s, width), :], full[span(other, width), :]], axis=0)
        both = transform(rows, ints[block])
        held[span(block, width), cols(q, c)] = both[:width]
        gift[block] = both[width:]
        give(block, c).start()

    def given():
        ref = gift.at[: n - 1]
        return remote(ref, ref, g_sems.at[0], g_sems.at[1], partner)

    far_part(1 - c).wait_recv()
    near_part(1 - c).wait_recv()
    mine = pltpu.make_async_copy(own.at[span(s, width)], held.at[span(o, width)], o_sem)
    mine.start()

    def arrive(block):
        ref = held.at[span(block, width), span(far, 2 * tile)]
        remote(ref, ref, x_fwd, f_recv.at[block], (side, s)).wait_recv()

    def pass_on(chain, act):
        block = 2 * chain + low
        ref = held.at[span(block, width), span(far, 2 * tile)]
        recv = f_recv.at[block]
        pl.when(jnp.logical_and(chain < z, z < nz - 1))(lambda: act(remote(ref, ref, z_fwd.at[0], recv, (above, s))))
        pl.when(jnp.logical_and(chain > z, z > 0))(lambda: act(remote(ref, ref, z_fwd.at[1], recv, (below, s))))
        pl.when(chain == nearest(1))(lambda: act(remote(ref, ref, x_fwd, recv, (side, s))))

    def beside_each(act):
        pl.when(z > 0)(lambda: act(z - 1))
        pl.when(z < nz - 1)(lambda: act(z + 1))

    def take(chain):
        arrive(2 * chain + low)
        pass_on(chain, start)

    beside_each(take)
    given().wait_recv()
    mine.wait()

    def absorb(chain):
        rows = span(chain, 2 * width)
        coulomb = lax.dot_general(
            held[rows, :], own[...], (((1,), (1,)), ((), ())), preferred_element_type=F32
        )
        left = jnp.concatenate([energies[o] + energies[2 * chain + t] - col_e for t in range(2)], axis=0)
        amps[rows, :] = (coulomb / (left - row_e)).astype(jnp.bfloat16)

    @pl.loop(0, nz)
    def _(i):
        chain = nearest(jnp.where(i == 0, 0, jnp.where(i == nz - 1, 1, i + 1)))
        pl.when(jnp.abs(chain - z) > 1)(lambda: arrive(2 * chain + low))
        arrive(2 * chain + 1 - low)
        absorb(chain)

    contract = (((0,), (0,)), ((), ()))
    strips, strip = t_give.shape[0], t_give.shape[-1]
    rows = vir.shape[4]
    middle = virtuals // 2

    def wide(k):
        return pl.ds(k * strip, strip)

    def part_three(group, core, where):
        return lax.dot_general(
            held[:, cols(group, core)], amps[:, where], contract, preferred_element_type=F32
        )

    def far_swap(k):
        return remote(t_give.at[k], t_got.at[k], t_send, t_recv.at[k], partner)

    def coded_copies(code, scale, code_to, scale_to, sems, target):
        return (
            remote(code, code_to, sems[0].at[0], sems[1].at[0], target),
            remote(scale, scale_to, sems[0].at[1], sems[1].at[1], target),
        )

    def far_send(k):
        sems = (ts_send, ts_recv.at[k])
        return coded_copies(t_code.at[k], t_scale.at[k], t_code_in.at[k], t_scale_in.at[k], sems, opposite)

    def x_swap(chain):
        sems = (x_send, x_recv.at[chain])
        return coded_copies(
            x_code.at[chain], x_scale.at[chain], x_code_in.at[chain], x_scale_in.at[chain], sems, (side, s)
        )

    def along(to, sender):
        sems = (z_send, z_recv.at[sender])
        return coded_copies(
            z_code.at[to], z_scale.at[to], z_code_in.at[sender], z_scale_in.at[sender], sems, (2 * to + low, s)
        )

    def both_start(copies):
        for copy in copies:
            copy.start()

    def both_recv(copies):
        for copy in copies:
            copy.wait_recv()

    def both_sent(copies):
        for copy in copies:
            copy.wait_send()

    def encode(value, code, scale):
        parts = scale.shape[0]
        size = value.shape[0] // parts
        grouped = value.reshape(parts, size, value.shape[1])
        top = jnp.maximum(jnp.max(jnp.abs(grouped), axis=1, keepdims=True), TINY)
        scale[...] = top
        code[...] = jnp.exp(grouped * (SPAN / top)).astype(jnp.bfloat16).reshape(value.shape)

    def decode(code, scale):
        parts = scale.shape[0]
        words = jnp.log(code[...].astype(F32)).reshape(parts, code.shape[0] // parts, code.shape[1])
        return (words * (scale[...] * (1.0 / SPAN))).reshape(code.shape)

    def v_swap(chain):
        return remote(vir.at[chain, :, :, 1 - c], v_pair.at[chain], vp_send, vp_recv.at[chain], partner)

    def between():
        return coded_copies(y_code, y_scale, y_code_in, y_scale_in, (yv_send, yv_recv), opposite)

    near_swap = remote(n_give, n_got, n_sems.at[0], n_sems.at[1], partner)
    first = jnp.where(z < nz // 2, 1, 0)
    for half in (first, 1 - first):
        new = lax.dot_general(
            amps[:, span(half, middle)], amps[...], contract, preferred_element_type=F32
        )
        vir[pl.ds(half * (nz // 2), nz // 2)] = new.reshape((nz // 2,) + vir.shape[1:])
        for t in range(nz // 2):
            v_swap(half * (nz // 2) + t).start()

    def pair_sum(chain, across):
        return (vir[chain, across, :, c] + v_pair[chain, across]).reshape(2 * rows, virtuals)

    farthest = [nearest(k) for k in reversed(range(nz))]

    def add_pair(chain):
        v_swap(chain).wait_recv()
        encode(pair_sum(chain, 1 - low), x_code.at[chain], x_scale.at[chain])
        both_start(x_swap(chain))

    for k in range(max(strips, nz)):
        if k < strips:
            t_give[k] = part_three(far, 1 - c, wide(k))
            far_swap(k).start()
        if k < nz:
            add_pair(farthest[k])
    for k in range(strips):
        new = part_three(far, c, wide(k))
        far_swap(k).wait_recv()
        encode(new + t_got[k], t_code.at[k], t_scale.at[k])
        both_start(far_send(k))
    def add_beside(chain, last):
        both_recv(x_swap(chain))
        total = pair_sum(chain, low) + decode(x_code_in.at[chain], x_scale_in.at[chain])
        if last:
            v_line[...] = total
        else:
            encode(total, z_code.at[chain], z_scale.at[chain])
            both_start(along(chain, z))

    def near_give():
        n_give[...] = part_three(q, 1 - c, slice(None))
        near_swap.start()

    def near_keep():
        near_sum[...] = part_three(q, c, slice(None))

    fillers = [near_give, near_keep]
    for k in range(nz):
        add_beside(farthest[k], k == nz - 1)
        if k < len(fillers):
            fillers[k]()
    for filler in fillers[nz:]:
        filler()
    near_swap.wait_recv()
    near_sum[...] += n_got[...]
    for k in range(1, nz):
        sender = nearest(k)
        both_recv(along(sender, sender))
        v_line[...] += decode(z_code_in.at[sender], z_scale_in.at[sender])
    v_col[...] = v_line[...].reshape(v_col.shape)
    encode(v_col[far], y_code, y_scale)
    both_start(between())
    for k in range(strips):
        both_recv(far_send(k))
        near_sum[:, wide(k)] += decode(t_code_in.at[k], t_scale_in.at[k])
    three_out[...] = near_sum[...].reshape(three_out.shape)
    both_recv(between())
    vir_out[...] = (v_col[q] + decode(y_code_in, y_scale_in)) / (n * virtuals)

    lend.wait_send()

    half_block = full.at[:part, : basis // 2]

    @pl.loop(0, nz)
    def _(chain):
        coef_relay(chain, half_block, half_block, c_recv.at[0, 0], sent)

    coef_far(half_block, half_block, c_recv.at[0, 0], sent)
    coef_halves(n - 1).wait_send()
    given().wait_send()

    def lent(blocks, sem):
        ref = cross.at[:blocks]
        return remote(ref, ref, y_send.at[sem], f_recv.at[0], opposite)

    if nz > 2:
        lent(nz - 2, 0).wait_send()
    for k in range(2, nz):
        pl.when(distant(nearest(k)))(lambda: lent(1, k - 1).wait_send())

    both_rows = own.at[: 2 * width, :tile]
    hand_out([(0, both_rows, both_rows)], sent)
    far_part(c).wait_send()
    near_part(c).wait_send()
    beside_each(lambda chain: pass_on(chain, sent))
    near_swap.wait_send()
    remote(t_give, t_give, t_send, t_recv.at[0], partner).wait_send()
    both_sent(coded_copies(t_code, t_scale, t_code, t_scale, (ts_send, ts_recv.at[0]), opposite))
    whole = vir.at[:, :, :, 0]
    remote(whole, whole, vp_send, vp_recv.at[0], partner).wait_send()
    both_sent(coded_copies(x_code, x_scale, x_code, x_scale, (x_send, x_recv.at[0]), (side, s)))
    codes, scales = z_code.at[: nz - 1], z_scale.at[: nz - 1]
    both_sent(coded_copies(codes, scales, codes, scales, (z_send, z_recv.at[0]), (side, s)))
    both_sent(between())


def paired(n, half_integrals, coef, occ_energy, vir_energy):
    _, tile, basis = half_integrals.shape
    part = coef.shape[0]
    virtuals = part * n
    width, rows, nz = virtuals // 4, virtuals // (4 * n), n // 2
    pieces = PIECES if basis % (256 * PIECES) == 0 else 1
    vmem = pl.BlockSpec(memory_space=pltpu.VMEM)
    dma = pltpu.SemaphoreType.DMA
    lanes = 128
    chunks = virtuals // lanes
    strip = 2 * lanes if chunks % 2 == 0 else lanes
    strips = virtuals // strip

    def room(*shape):
        return pltpu.VMEM(shape, F32)

    def packed(*shape):
        return pltpu.VMEM(shape, jnp.bfloat16)

    scratch = [
        packed(n, tile, basis), packed(tile, basis), packed(virtuals, basis), packed(virtuals, 4 * tile),
        packed(n * width, 4 * tile), packed(n, width, tile), packed(n, 2 * width, tile), packed(n * width, virtuals),
        room(nz, 2, 2, 2, rows, virtuals),
        room(strips, tile, strip), room(strips, tile, strip), room(tile, virtuals), room(tile, virtuals),
        room(tile, virtuals), room(nz, 2, 2, rows, virtuals), room(2 * rows, virtuals), room(2, rows, virtuals),
    ]
    groups = tile // 32
    for _ in range(2):
        scratch += [packed(strips, tile, strip), room(strips, groups, 1, strip)]
    for _ in range(4):
        scratch += [packed(nz, 2 * rows, virtuals), room(nz, 2, 1, virtuals)]
    for _ in range(2):
        scratch += [packed(rows, virtuals), room(1, 1, virtuals)]
    scratch += [pltpu.SMEM((n,), F32), room(virtuals)]
    scratch += [
        dma((2,)), dma, dma, dma, dma((2,)), dma((n, pieces)), dma((2,)), dma((2,)), dma((nz,)), dma((2, nz)), dma((2,)),
        dma((2,)), dma((2,)), dma((n,)), dma((3,)), dma((2,)), dma, dma((nz,)), dma((2,)),
        dma, dma((strips,)), dma((2,)), dma((strips, 2)), dma((2,)), dma, dma((nz,)),
        dma((2,)), dma((nz, 2)), dma((2,)), dma((nz, 2)), dma((2,)), dma((2,)),
    ]
    return pl.pallas_call(
        functools.partial(paired_kernel, n),
        out_shape=(
            pltpu.VMEM((tile, 1, virtuals), F32), pltpu.VMEM((rows, virtuals), F32),
        ),
        in_specs=[pl.BlockSpec(memory_space=pl.ANY)] * 4,
        out_specs=(vmem, vmem),
        scratch_shapes=scratch,
        compiler_params=pltpu.CompilerParams(
            collective_id=0, has_side_effects=True, vmem_limit_bytes=LIMIT
        ),
        name="densities",
    )(occ_energy, half_integrals, coef, vir_energy)


def per_device(half_integrals, vir_coef, occ_energy, vir_energy):
    n, aux = lax.axis_size("occ"), lax.axis_size("aux")
    nz, nq = n // 2, aux // 2
    _, tile, basis = half_integrals.shape
    part = vir_coef.shape[1]
    virtuals = part * n
    if nq == 2 and n % 2 == 0 and nz > 1 and nz % 2 == 0 and virtuals % (32 * n) == 0 and virtuals % 256 == 0 and tile % 32 == 0:
        three, vir_rows = paired(n, half_integrals, vir_coef.T, occ_energy, vir_energy)
        return three, vir_rows
    width, rows = virtuals // aux, virtuals // (n * aux)
    vmem = pl.BlockSpec(memory_space=pltpu.VMEM)
    dma = pltpu.SemaphoreType.DMA
    half = jnp.bfloat16
    lanes = 128
    chunks = virtuals // lanes

    def room(*shape):
        return pltpu.VMEM(shape, F32)

    def result(*shape):
        return jax.ShapeDtypeStruct(shape, F32)

    def call(kernel, name, number, in_specs, out_shape, scratch, operands):
        return pl.pallas_call(
            kernel,
            out_shape=out_shape,
            in_specs=in_specs,
            out_specs=(vmem,) * len(out_shape),
            scratch_shapes=scratch,
            compiler_params=pltpu.CompilerParams(
                collective_id=number, has_side_effects=True, vmem_limit_bytes=LIMIT
            ),
            name=name,
        )(*operands)

    operands = (occ_energy, half_integrals, vir_coef.T, vir_energy)
    specs = [pl.BlockSpec(memory_space=pltpu.SMEM), pl.BlockSpec(memory_space=pl.ANY), vmem, vmem]
    make_scratch = [
        pltpu.VMEM(half_integrals.shape, half),
        pltpu.VMEM((2, virtuals, basis // 2), half),
        pltpu.VMEM((nq, 2, nq, 2 * width, tile), half),
        pltpu.VMEM((nq, 2, n * width, tile), half),
        pltpu.VMEM((n, width, tile), half),
        pltpu.VMEM((n * width, virtuals), half),
        dma, dma((2,)), dma, dma((n,)), dma((nz,)), dma((nz,)), dma((nz,)), dma((n,)), dma((n,)),
        dma((nq, nq)), dma((nq, nq)), dma((nq, nq)), dma((nq, nq)), dma((nq,)), dma((nq,)), dma((n,)), dma((n,)),
        dma((nq, n)), dma((nq, nz)), dma((nq, nz)), dma((nq, nz)),
    ]
    reduce_scratch = [
        room(nq, tile, virtuals), room(nq, tile, virtuals), room(nq, tile, virtuals),
        room(chunks, n, nq, rows, lanes), room(chunks, nz, 2, nq, rows, lanes),
        room(chunks, nz, nq, rows, lanes), room(chunks, nz, nq, rows, lanes), room(chunks, nz, nq, rows, lanes),
        room(chunks, nq, rows, lanes), room(chunks, nq, rows, lanes),
        dma((nq,)), dma((nq,)), dma((nq,)), dma((nq,)), dma((chunks,)), dma((chunks,)), dma((chunks,)), dma((chunks,)),
        dma((chunks, nz)), dma((chunks, nz)), dma((chunks, nq)), dma((chunks, nq)),
    ]
    sums = (nq, 2, tile, virtuals)
    groups = (n, nq, 2, rows, virtuals)
    finals = (result(tile, virtuals), result(tile, virtuals), result(rows, virtuals))
    if rows % 8 == 0:
        kernel = functools.partial(whole_kernel, n, nq, len(specs), len(finals), len(make_scratch))
        scratch = [room(*sums), room(*groups)] + make_scratch + reduce_scratch
        near, far, vir_rows = call(kernel, "densities", 0, specs, finals, scratch, operands)
    else:
        kernel = functools.partial(amplitude_kernel, n, nq)
        partials = (result(*sums), result(virtuals, virtuals))
        three, vir = call(kernel, "amplitude", 0, specs, partials, make_scratch, operands)
        kernel = functools.partial(reduce_kernel, n, nq)
        near, far, vir_rows = call(
            kernel, "reduce", 1, [vmem, vmem], finals, reduce_scratch, (three, vir.reshape(groups))
        )
    return (near + far)[:, None, :], vir_rows / (n * virtuals)


def solution(mesh):
    return jax.shard_map(
        per_device,
        mesh=mesh,
        in_specs=(P(None, "aux", None), P(None, "occ"), P(), P()),
        out_specs=(P("aux", "occ", None), P(("occ", "aux"), None)),
        check_vma=False,
    )
```

```python
import functools

import jax
import jax.numpy as jnp
from jax import lax
from jax.experimental import pallas as pl
from jax.experimental.pallas import tpu as pltpu
from jax.sharding import PartitionSpec as P

MESH = pl.DeviceIdType.MESH
F32 = jnp.float32
PIECES = 4
SPAN = 80.0
TINY = 1e-30
LIMIT = 56 * 1024 * 1024


def remote(src, dst, send, recv, target):
    return pltpu.make_async_remote_copy(
        src_ref=src, dst_ref=dst, send_sem=send, recv_sem=recv, device_id=target, device_id_type=MESH
    )


def nearest_first(z, k, count):
    near = jnp.minimum(z, count - 1 - z)
    step = (k + 1) // 2
    both = z + step * (2 * (k % 2) - 1)
    low = z < count - 1 - z
    return jnp.where(k <= 2 * near, both, jnp.where(low, k, count - 1 - k))


def greet(n, nq):
    o = lax.axis_index("occ")
    s = lax.axis_index("aux")
    q, c = s // 2, s % 2
    z, low = o // 2, o % 2
    nz = n // 2
    barrier = pltpu.get_barrier_semaphore()
    peers = [(2 * z + 1 - low, s), (o, 2 * q + 1 - c)]
    peers += [(o, 2 * ((q + d) % nq) + c) for d in range(1, nq)]
    peers += [(2 * ((z + d) % nz) + low, s) for d in range(1, nz)]
    for peer in peers:
        pl.semaphore_signal(barrier, inc=1, device_id=peer, device_id_type=MESH)
    return lambda: pl.semaphore_wait(barrier, len(peers))


def make_densities(
    n, nq, occ_e, half, coef, vir_e, three, vir,
    ints, full, own, held, gift, amps,
    i_sem, c_copy, o_copy, c_recv, c_up, c_down, c_side, cp_send, cp_recv,
    own_send, own_recv, fw_send, fw_recv, pr_send, pr_recv, g_send, g_recv,
    h_recv, h_up, h_down, h_side,
    vir_done=lambda: None,
):
    o = lax.axis_index("occ")
    s = lax.axis_index("aux")
    q, c = s // 2, s % 2
    z, low = o // 2, o % 2
    nz = n // 2
    width = amps.shape[0] // n
    part = coef.shape[0]
    cut = coef.shape[1] // 2
    virtuals = amps.shape[1]
    above, below, side = o + 2, o - 2, 2 * z + 1 - low
    partner = (o, 2 * q + 1 - c)
    entered = greet(n, nq)

    fetch = pltpu.make_async_copy(half, ints, i_sem)
    fetch.start()

    def span(index, size):
        return pl.ds(pl.multiple_of(index * size, size), size)

    def keep(h):
        return pltpu.make_async_copy(coef.at[:, h * cut : (h + 1) * cut], full.at[h, span(o, part)], c_copy.at[h])

    keep(0).start()
    keep(1).start()
    entered()

    def relay(chain, src, dst, up, down, across, recv, act):
        pl.when(jnp.logical_and(chain <= z, z < nz - 1))(lambda: act(remote(src, dst, up, recv, (above, s))))
        pl.when(jnp.logical_and(chain >= z, z > 0))(lambda: act(remote(src, dst, down, recv, (below, s))))
        act(remote(src, dst, across, recv, (side, s)))

    def start(copy):
        copy.start()

    def sent(copy):
        copy.wait_send()

    def coef_slot(block):
        return full.at[c, span(block, part)]

    def coef_relay(chain, src, act):
        block = 2 * chain + low
        relay(chain, src, coef_slot(block), c_up.at[chain], c_down.at[chain], c_side.at[chain], c_recv.at[block], act)

    def coef_across(block):
        return remote(coef_slot(block), coef_slot(block), cp_send.at[block], cp_recv.at[block], partner)

    def coef_arrived(block):
        remote(coef_slot(block), coef_slot(block), c_side.at[0], c_recv.at[block], (side, s)).wait_recv()
        coef_across(block).start()

    coef_relay(z, coef.at[:, span(c, cut)], start)
    three[...] = jnp.zeros_like(three)
    vir[...] = jnp.zeros_like(vir)
    row_e = vir_e[...].reshape(1, virtuals)
    here = lax.broadcasted_iota(jnp.int32, (width, virtuals), 0) + s * width
    there = lax.broadcasted_iota(jnp.int32, (width, virtuals), 1)
    col_e = jnp.sum(jnp.where(here == there, row_e, 0.0), axis=1, keepdims=True)

    @pl.loop(1, nz)
    def _(k):
        chain = nearest_first(z, k, nz)
        block = 2 * chain + low
        remote(coef_slot(block), coef_slot(block), c_side.at[0], c_recv.at[block], (side, s)).wait_recv()
        coef_relay(chain, coef_slot(block), start)
        coef_across(block).start()
        coef_arrived(2 * nearest_first(z, k - 1, nz) + 1 - low)

    coef_arrived(2 * nearest_first(z, nz - 1, nz) + 1 - low)

    @pl.loop(1, n)
    def _(d):
        block = (o + d) % n
        other = full.at[1 - c, span(block, part)]
        remote(other, other, cp_send.at[block], cp_recv.at[block], partner).wait_recv()

    keep(0).wait()
    keep(1).wait()
    fetch.wait()

    def transform(block, rows):
        contract = (((1,), (1,)), ((), ()))
        return sum(
            lax.dot_general(
                full[h, rows, :], ints[block, :, h * cut : (h + 1) * cut], contract, preferred_element_type=F32
            )
            for h in range(2)
        ).astype(jnp.bfloat16)

    order = list(range(1, nq)) + [0]

    def chunk(there, core, group):
        return own.at[there, core, group]

    def to_partner(r):
        ref = chunk(q, c, (q + r) % nq)
        return remote(ref, ref, pr_send.at[r], pr_recv.at[r], partner)

    def to_chip(d, r):
        ref = chunk(q, c, (q + r) % nq)
        return remote(ref, ref, own_send.at[d, r], own_recv.at[d, r], (o, 2 * ((q + d) % nq) + c))

    def onward(d, r, core):
        there = (q + nq - d) % nq
        ref = chunk(there, core, (there + r) % nq)
        return remote(ref, ref, fw_send.at[d, r], fw_recv.at[d, r], partner)

    def from_chip(d, r):
        there = (q + nq - d) % nq
        ref = chunk(there, c, (there + r) % nq)
        remote(ref, ref, own_send.at[d, r], own_recv.at[d, r], partner).wait_recv()
        onward(d, r, c).start()

    for r in order:
        group = (q + r) % nq
        own[q, c, group] = transform(o, span(group, 2 * width))
        for d in range(1, nq):
            to_chip(d, r).start()
        to_partner(r).start()

    def give(block, core):
        return remote(
            gift.at[block], held.at[q, core, span(block, width)], g_send.at[block], g_recv.at[block], partner
        )

    @pl.loop(1, n)
    def _(d):
        block = (o + d) % n
        gift[block] = transform(block, span(2 * q + 1 - c, width))
        give(block, c).start()
        held[q, c, span(block, width), :] = transform(block, span(s, width))

    def held_slot(d, block):
        return held.at[(q + nq - d) % nq, :, span(block, width)]

    def own_slot(d):
        return own.at[(q + nq - d) % nq, :, q, span(c, width)]

    def held_relay(d, chain, src, act):
        block = 2 * chain + low
        relay(
            chain, src, held_slot(d, block), h_up.at[d, chain], h_down.at[d, chain], h_side.at[d, chain],
            h_recv.at[d, block], act,
        )

    def arrived(block):
        for d in range(1, nq):
            ref = held_slot(d, block)
            remote(ref, ref, h_side.at[d, 0], h_recv.at[d, block], (side, s)).wait_recv()

    for d in range(1, nq):
        from_chip(d, d)
    for d in range(1, nq):
        onward(d, d, 1 - c).wait_recv()
        held_relay(d, z, own_slot(d), start)
    rest = [(d, r) for d in range(1, nq) for r in order if r != d]
    for d, r in rest:
        from_chip(d, r)
    for r in order:
        ref = chunk(q, 1 - c, (q + r) % nq)
        remote(ref, ref, pr_send.at[r], pr_recv.at[r], partner).wait_recv()

    @pl.loop(1, n)
    def _(d):
        give((o + d) % n, 1 - c).wait_recv()

    for d, r in rest:
        onward(d, r, 1 - c).wait_recv()
    mine = pltpu.make_async_copy(
        own.at[:, :, q, span(c, width)], held.at[:, :, span(o, width)], o_copy
    )
    mine.start()
    mine.wait()

    def absorb(block):
        rows = span(block, width)
        coulomb = sum(
            lax.dot_general(
                held[t // 2, t % 2, rows, :], own[t // 2, t % 2].reshape(virtuals, -1),
                (((1,), (1,)), ((), ())), preferred_element_type=F32,
            )
            for t in range(2 * nq)
        )
        denominator = occ_e[o] + occ_e[block] - col_e - row_e
        amps[rows, :] = (coulomb / denominator).astype(jnp.bfloat16)

    contract = (((0,), (0,)), ((), ()))
    piece = virtuals // 2 if len(vir.shape) > 2 else 256

    def add_vir(chain):
        rows = span(chain, 2 * width)

        @pl.loop(0, virtuals // piece)
        def _(t):
            new = lax.dot_general(
                amps[rows, span(t, piece)], amps[rows, :], contract, preferred_element_type=F32
            )
            where = span(t, vir.shape[0] * piece // virtuals)
            vir[where] += new.reshape((-1,) + vir.shape[1:])

    def add_three(chain):
        rows = span(chain, 2 * width)

        @pl.loop(0, 2 * nq)
        def _(t):
            three[t // 2, t % 2] += lax.dot_general(
                held[t // 2, t % 2, rows, :], amps[rows, :], contract, preferred_element_type=F32
            )

    def both(chain):
        absorb(2 * chain + low)
        arrived(2 * chain + 1 - low)
        absorb(2 * chain + 1 - low)

    @pl.loop(1, nz)
    def _(k):
        chain = nearest_first(z, k, nz)
        arrived(2 * chain + low)
        for d in range(1, nq):
            held_relay(d, chain, held_slot(d, 2 * chain + low), start)
        before = nearest_first(z, k - 1, nz)
        both(before)
        add_vir(before)
        add_three(before)

    last = nearest_first(z, nz - 1, nz)
    both(last)
    add_vir(last)
    vir_done()
    add_three(last)

    def finish():
        @pl.loop(0, nz)
        def _(chain):
            coef_relay(chain, coef_slot(2 * chain + low), sent)
            for d in range(1, nq):
                held_relay(d, chain, held_slot(d, 2 * chain + low), sent)

        @pl.loop(1, n)
        def _(d):
            block = (o + d) % n
            coef_across(block).wait_send()
            give(block, c).wait_send()

        for r in order:
            to_partner(r).wait_send()
            for d in range(1, nq):
                to_chip(d, r).wait_send()
                onward(d, r, c).wait_send()

    return finish


def reduction(
    n, nq, three, vir, near_out, far_out, vir_out,
    t_pair, t_out, t_far, v_pair, v_sum, v_side, v_line, v_chain, v_col, v_far,
    pair_send, pair_recv, t_send, t_recv, vp_send, vp_recv, x_send, x_recv, z_send, z_recv, y_send, y_recv,
):
    o = lax.axis_index("occ")
    s = lax.axis_index("aux")
    q, c = s // 2, s % 2
    z, low = o // 2, o % 2
    nz = n // 2
    chunks, chunk = v_pair.shape[0], v_pair.shape[-1]
    partner = (o, 2 * q + 1 - c)
    side = (2 * z + 1 - low, s)

    def cols(k):
        return pl.ds(k * chunk, chunk)

    def v_swap(k):
        return remote(vir.at[:, :, 1 - c, :, cols(k)], v_pair.at[k], vp_send.at[k], vp_recv.at[k], partner)

    def x_swap(k):
        return remote(v_sum.at[k, :, 1 - low], v_side.at[k], x_send.at[k], x_recv.at[k], side)

    def along(k, d):
        there = (z + d) % nz
        return remote(
            v_line.at[k, there], v_chain.at[k, d], z_send.at[k, d], z_recv.at[k, d], (2 * there + low, s)
        )

    def between(k, d):
        there = (q + d) % nq
        return remote(v_col.at[k, there], v_far.at[k, d], y_send.at[k, d], y_recv.at[k, d], (o, 2 * there + c))

    def swap(d):
        return remote(three.at[(q + d) % nq, 1 - c], t_pair.at[d], pair_send.at[d], pair_recv.at[d], partner)

    def spread(d):
        return remote(t_out.at[d], t_far.at[d], t_send.at[d], t_recv.at[d], (o, 2 * ((q + d) % nq) + c))

    order = list(range(1, nq)) + [0]

    def open_vir():
        for k in range(chunks):
            v_swap(k).start()

    def close():
        for d in order:
            swap(d).start()
        for k in range(chunks):
            v_swap(k).wait()
            v_sum[k] = (vir[:, :, c, :, cols(k)] + v_pair[k]).reshape(v_sum.shape[1:])
            x_swap(k).start()
        for d in order[:-1]:
            swap(d).wait()
            t_out[d] = three[(q + d) % nq, c] + t_pair[d]
            spread(d).start()
        for k in range(chunks):
            x_swap(k).wait()
            v_line[k] = v_sum[k, :, low] + v_side[k]
            for d in range(1, nz):
                along(k, d).start()
            if k == 0:
                swap(0).wait()
                near_out[...] = three[q, c] + t_pair[0]
        for k in range(chunks):
            held = v_line[k, z]
            for d in range(1, nz):
                along(k, d).wait()
                held += v_chain[k, d]
            v_col[k] = held
            for d in range(1, nq):
                between(k, d).start()
        for d in order[:-1]:
            spread(d).wait()
            far_out[...] = t_far[d] if d == 1 else far_out[...] + t_far[d]
        for k in range(chunks):
            rows = v_col[k, q]
            for d in range(1, nq):
                between(k, d).wait()
                rows += v_far[k, d]
            vir_out[:, cols(k)] = rows

    return open_vir, close


def amplitude_kernel(n, nq, *refs):
    make_densities(n, nq, *refs)()


def reduce_kernel(n, nq, *refs):
    greet(n, nq)()
    open_vir, close = reduction(n, nq, *refs)
    open_vir()
    close()


def whole_kernel(n, nq, inputs, outputs, count, *refs):
    operands, results, scratch = refs[:inputs], refs[inputs : inputs + outputs], refs[inputs + outputs :]
    three, vir, rest = scratch[0], scratch[1], scratch[2:]
    open_vir, close = reduction(n, nq, three, vir, *results, *rest[count:])
    finish = make_densities(n, nq, *operands, three, vir, *rest[:count], vir_done=open_vir)
    close()
    finish()


def paired_kernel(
    n, occ_e, half, coef, vir_e, three_out, vir_out,
    ints, raw, full, own, held, gift, cross, amps, vir,
    t_give, t_mine, t_got, n_give, n_got, near_sum, v_pair, v_line, v_col,
    t_code, t_scale, t_code_in, t_scale_in, x_code, x_scale, x_code_in, x_scale_in,
    z_code, z_scale, z_code_in, z_scale_in, y_code, y_scale, y_code_in, y_scale_in, energies, levels,
    e_sems, i_sem, keep_sem, o_sem, raw_sems, c_recv, c_up, c_down, c_side, c_jump, cp_sems,
    pn_sems, pf_sems, f_recv, f_send, z_fwd, x_fwd, y_send, g_sems,
    t_send, t_recv, ts_send, ts_recv, n_sems, vp_send, vp_recv, x_send, x_recv, z_send, z_recv, yv_send, yv_recv,
):
    o = lax.axis_index("occ")
    s = lax.axis_index("aux")
    q, c = s // 2, s % 2
    z, low = o // 2, o % 2
    nz = n // 2
    far = 1 - q
    part, basis = coef.shape
    tile = raw.shape[0]
    virtuals = full.shape[0]
    width = virtuals // 4
    pieces = c_recv.shape[1]
    piece = basis // (2 * pieces)
    above, below, side = o + 2, o - 2, 2 * z + 1 - low
    other = 2 * q + 1 - c
    partner = (o, other)
    opposite = (o, 2 * far + c)

    def span(index, size):
        return pl.ds(pl.multiple_of(index * size, size), size)

    def start(copy):
        copy.start()

    def sent(copy):
        copy.wait_send()

    def nearest(k):
        return nearest_first(z, k, nz)

    at_end = jnp.logical_or(z == 0, z == nz - 1)
    inner_order = [0] + list(range(2, nz)) + [1]
    end_order = [0, nz - 1] + list(range(1, nz - 1))
    order = [nearest(jnp.where(at_end, a, b)) for a, b in zip(end_order, inner_order)]

    barrier = pltpu.get_barrier_semaphore()
    peers = [partner, opposite, (o, 2 * far + 1 - c), (side, s), (side, other)]
    peers += [(2 * ((z + d) % nz) + low, t) for d in range(1, nz) for t in (s, other)]
    for peer in peers:
        pl.semaphore_signal(barrier, inc=1, device_id=peer, device_id_type=MESH)
    small = [pltpu.make_async_copy(occ_e, energies, e_sems.at[0]), pltpu.make_async_copy(vir_e, levels, e_sems.at[1])]
    fetch = pltpu.make_async_copy(half, ints, i_sem)
    fetch.start()
    keep = pltpu.make_async_copy(coef, full.at[span(o, part)], keep_sem)
    keep.start()
    for copy in small:
        copy.start()
    pl.semaphore_wait(barrier, len(peers))

    lend = remote(half.at[o], raw, raw_sems.at[0], raw_sems.at[1], opposite)
    lend.start()

    def coef_slot(block, core, h):
        return full.at[span(block, part), pl.ds(pl.multiple_of((pieces * core + h) * piece, piece), piece)]

    def coef_relay(chain, src, dst, recv, act):
        pl.when(jnp.logical_and(jnp.logical_and(chain <= z, chain > z - 2), z < nz - 1))(
            lambda: act(remote(src, dst, c_up.at[z - chain], recv, (above, s)))
        )
        pl.when(jnp.logical_and(jnp.logical_and(chain >= z, chain < z + 2), z > 0))(
            lambda: act(remote(src, dst, c_down.at[chain - z], recv, (below, s)))
        )
        act(remote(src, dst, c_side.at[chain], recv, (side, s)))

    def coef_across(block, h, core):
        ref = coef_slot(block, core, h)
        return remote(ref, ref, cp_sems.at[0], cp_sems.at[1], partner)

    def coef_wait(block, h):
        ref = coef_slot(block, c, h)
        remote(ref, ref, c_side.at[0], c_recv.at[block, h], (side, s)).wait_recv()

    def coef_own(h):
        return coef.at[:, pl.ds(pl.multiple_of((pieces * c + h) * piece, piece), piece)]

    def coef_far(src, dst, recv, act):
        for d in range(3, nz):
            pl.when(z + d < nz)(
                lambda: act(remote(src, dst, c_jump.at[0, d], recv, (o + 2 * d, s)))
            )
            pl.when(z >= d)(
                lambda: act(remote(src, dst, c_jump.at[1, d], recv, (o - 2 * d, s)))
            )

    for h in range(pieces):
        coef_relay(z, coef_own(h), coef_slot(o, c, h), c_recv.at[o, h], start)
    for h in range(pieces):
        coef_far(coef_own(h), coef_slot(o, c, h), c_recv.at[o, h], start)
    for copy in small:
        copy.wait()
    row_e = levels[...].reshape(1, virtuals)
    here = lax.broadcasted_iota(jnp.int32, (width, virtuals), 0) + s * width
    there = lax.broadcasted_iota(jnp.int32, (width, virtuals), 1)
    col_e = jnp.sum(jnp.where(here == there, row_e, 0.0), axis=1, keepdims=True)

    def each_at(d, act):
        pl.when(z + d < nz)(lambda: act(z + d))
        pl.when(z >= d)(lambda: act(z - d))

    def coef_beside(chain, h):
        block = 2 * chain + 1 - low
        coef_wait(block, h)
        coef_across(block, h, c).start()

    def coef_along(chain, h):
        block = 2 * chain + low
        slot = coef_slot(block, c, h)
        coef_wait(block, h)
        coef_relay(chain, slot, slot, c_recv.at[block, h], start)
        coef_across(block, h, c).start()

    for d in range(1, nz + 1):
        for h in range(pieces):
            if d < nz:
                each_at(d, lambda chain: coef_along(chain, h))
        for h in range(pieces):
            if d == 1:
                coef_beside(z, h)
            else:
                each_at(d - 1, lambda chain: coef_beside(chain, h))

    def coef_halves(blocks):
        ref = full.at[: blocks * part, : basis // 2]
        return remote(ref, ref, cp_sems.at[0], cp_sems.at[1], partner)

    coef_halves(n - 1).wait_recv()

    keep.wait()
    fetch.wait()

    def transform(rows, source):
        return lax.dot_general(rows, source, (((1,), (1,)), ((), ())), preferred_element_type=F32).astype(jnp.bfloat16)

    def cols(group, core):
        return span(2 * group + core, tile)

    def lend_block(block, sem, act):
        for core in range(2):
            act(
                remote(
                    cross.at[block, pl.ds(core * width, width)], held.at[span(block, width), cols(q, c)],
                    y_send.at[sem], f_recv.at[block, 0], (o, 2 * far + core),
                )
            )

    def distant(chain):
        return jnp.abs(chain - z) > 2

    def cross_over(block, sem):
        cross[block] = transform(full[span(far, 2 * width), :], ints[block])
        lend_block(block, sem, start)

    @pl.loop(2, nz)
    def _(k):
        chain = nearest(jnp.where(at_end, nz + 1 - k, k))
        cross_over(2 * chain + 1 - low, 0)
        pl.when(distant(chain))(lambda: cross_over(2 * chain + low, jnp.where(at_end, nz - k, k - 1)))

    def own_part(group, core):
        return own.at[:, cols(group, core)]

    def near_part(core):
        ref = own_part(q, core)
        return remote(ref, ref, pn_sems.at[0], pn_sems.at[1], partner)

    def far_part(core):
        ref = own_part(far, core)
        return remote(ref, ref, pf_sems.at[0], pf_sems.at[1], partner)

    def hand_out(parts, act):
        for core, t, src, dst in parts:
            recv = f_recv.at[o, t]
            to = 2 * q + core
            pl.when(z < nz - 1)(lambda: act(remote(src, dst, f_send.at[0], recv, (above, to))))
            pl.when(z > 0)(lambda: act(remote(src, dst, f_send.at[1], recv, (below, to))))
            act(remote(src, dst, f_send.at[2], recv, (side, to)))

    part_rows = width // 2

    def outgoing(core, t):
        rows = pl.ds(pl.multiple_of((2 * q + core) * width + t * part_rows, part_rows), part_rows)
        return core, t, own.at[rows, cols(far, c)], held.at[span(2 * o + t, part_rows), cols(far, c)]

    lend.wait_recv()
    own[:, cols(far, c)] = transform(full[...], raw[...])
    hand_out([outgoing(core, t) for t in range(2) for core in range(2)], start)
    far_part(c).start()
    own[:, cols(q, c)] = transform(full[...], ints[o])
    near_part(c).start()

    def give(block, core):
        return remote(
            gift.at[block], held.at[span(block, width), cols(q, core)], g_sems.at[0], g_sems.at[1], partner
        )

    @pl.loop(1, n)
    def _(d):
        block = (o + d) % n
        rows = jnp.concatenate([full[span(s, width), :], full[span(other, width), :]], axis=0)
        both = transform(rows, ints[block])
        held[span(block, width), cols(q, c)] = both[:width]
        gift[block] = both[width:]
        give(block, c).start()

    def given():
        ref = gift.at[: n - 1]
        return remote(ref, ref, g_sems.at[0], g_sems.at[1], partner)

    far_part(1 - c).wait_recv()
    near_part(1 - c).wait_recv()
    mine = pltpu.make_async_copy(own.at[span(s, width)], held.at[span(o, width)], o_sem)
    mine.start()

    def far_piece(block, t):
        return held.at[span(2 * block + t, part_rows), span(far, 2 * tile)]

    def arrive(block):
        ref = held.at[span(block, width), span(far, 2 * tile)]
        remote(ref, ref, x_fwd, f_recv.at[block, 0], (side, s)).wait_recv()

    def arrive_pieces(block):
        for t in range(2):
            ref = far_piece(block, t)
            remote(ref, ref, x_fwd, f_recv.at[block, t], (side, s)).wait_recv()

    def pass_on(chain, ref, recv, act):
        pl.when(jnp.logical_and(chain < z, z < nz - 1))(lambda: act(remote(ref, ref, z_fwd.at[0], recv, (above, s))))
        pl.when(jnp.logical_and(chain > z, z > 0))(lambda: act(remote(ref, ref, z_fwd.at[1], recv, (below, s))))
        pl.when(chain == nearest(1))(lambda: act(remote(ref, ref, x_fwd, recv, (side, s))))

    def take(chain, t):
        block = 2 * chain + low
        ref = far_piece(block, t)
        remote(ref, ref, x_fwd, f_recv.at[block, t], (side, s)).wait_recv()
        pass_on(chain, ref, f_recv.at[block, t], start)

    for t in range(2):
        each_at(1, lambda chain: take(chain, t))
    given().wait_recv()
    mine.wait()

    def absorb(slot, chain):
        coulomb = lax.dot_general(
            held[span(chain, 2 * width), :], own[...], (((1,), (1,)), ((), ())), preferred_element_type=F32
        )
        left = jnp.concatenate([energies[o] + energies[2 * chain + t] - col_e for t in range(2)], axis=0)
        amps[slot * 2 * width : (slot + 1) * 2 * width, :] = (coulomb / (left - row_e)).astype(jnp.bfloat16)

    contract = (((0,), (0,)), ((), ()))
    strips, strip = t_give.shape[0], t_give.shape[-1]
    rows = vir.shape[4]
    middle = virtuals // 2

    def wide(k):
        return pl.ds(k * strip, strip)

    early, late = range(nz // 2), range(nz // 2, nz)

    def amps_of(slots, where=slice(None)):
        return amps[slots[0] * 2 * width : (slots[-1] + 1) * 2 * width, where]

    def part_three(group, core, where, slots):
        rows = [held[span(order[i], 2 * width), cols(group, core)] for i in slots]
        return lax.dot_general(
            jnp.concatenate(rows, axis=0), amps_of(slots, where), contract, preferred_element_type=F32
        )

    def part_vir(half, slots):
        new = lax.dot_general(
            amps_of(slots, span(half, middle)), amps_of(slots), contract, preferred_element_type=F32
        )
        return new.reshape((nz // 2,) + vir.shape[1:])

    def admit(i):
        chain = order[i]
        pl.when(distant(chain))(lambda: arrive(2 * chain + low))
        pl.when(jnp.abs(chain - z) == 2)(lambda: arrive_pieces(2 * chain + low))
        passed = jnp.logical_or(chain == z, chain == nearest(1))
        pl.when(passed)(lambda: arrive_pieces(2 * chain + 1 - low))
        pl.when(jnp.logical_not(passed))(lambda: arrive(2 * chain + 1 - low))
        absorb(i, chain)

    for i in early:
        admit(i)
    for half in range(2):
        vir[pl.ds(half * (nz // 2), nz // 2)] = part_vir(half, early)
    for k in range(strips):
        t_give[k] = part_three(far, 1 - c, wide(k), early)
        t_mine[k] = part_three(far, c, wide(k), early)
    for i in late:
        admit(i)

    def far_swap(k):
        return remote(t_give.at[k], t_got.at[k], t_send, t_recv.at[k], partner)

    def coded_copies(code, scale, code_to, scale_to, sems, target):
        return (
            remote(code, code_to, sems[0].at[0], sems[1].at[0], target),
            remote(scale, scale_to, sems[0].at[1], sems[1].at[1], target),
        )

    def far_send(k):
        sems = (ts_send, ts_recv.at[k])
        return coded_copies(t_code.at[k], t_scale.at[k], t_code_in.at[k], t_scale_in.at[k], sems, opposite)

    def x_swap(chain):
        sems = (x_send, x_recv.at[chain])
        return coded_copies(
            x_code.at[chain], x_scale.at[chain], x_code_in.at[chain], x_scale_in.at[chain], sems, (side, s)
        )

    def along(to, sender):
        sems = (z_send, z_recv.at[sender])
        return coded_copies(
            z_code.at[to], z_scale.at[to], z_code_in.at[sender], z_scale_in.at[sender], sems, (2 * to + low, s)
        )

    def both_start(copies):
        for copy in copies:
            copy.start()

    def both_recv(copies):
        for copy in copies:
            copy.wait_recv()

    def both_sent(copies):
        for copy in copies:
            copy.wait_send()

    def encode(value, code, scale):
        parts = scale.shape[0]
        size = value.shape[0] // parts
        grouped = value.reshape(parts, size, value.shape[1])
        top = jnp.maximum(jnp.max(jnp.abs(grouped), axis=1, keepdims=True), TINY)
        scale[...] = top
        code[...] = jnp.exp(grouped * (SPAN / top)).astype(jnp.bfloat16).reshape(value.shape)

    def decode(code, scale):
        parts = scale.shape[0]
        words = jnp.log(code[...].astype(F32)).reshape(parts, code.shape[0] // parts, code.shape[1])
        return (words * (scale[...] * (1.0 / SPAN))).reshape(code.shape)

    def v_swap(chain):
        return remote(vir.at[chain, :, :, 1 - c], v_pair.at[chain], vp_send, vp_recv.at[chain], partner)

    def between():
        return coded_copies(y_code, y_scale, y_code_in, y_scale_in, (yv_send, yv_recv), opposite)

    near_swap = remote(n_give, n_got, n_sems.at[0], n_sems.at[1], partner)
    first = jnp.where(z < nz // 2, 1, 0)
    for half in (first, 1 - first):
        where = pl.ds(half * (nz // 2), nz // 2)
        vir[where] = vir[where] + part_vir(half, late)
        for t in range(nz // 2):
            v_swap(half * (nz // 2) + t).start()

    def pair_sum(chain, across):
        return (vir[chain, across, :, c] + v_pair[chain, across]).reshape(2 * rows, virtuals)

    farthest = [nearest(k) for k in reversed(range(nz))]

    def add_pair(chain):
        v_swap(chain).wait_recv()
        encode(pair_sum(chain, 1 - low), x_code.at[chain], x_scale.at[chain])
        both_start(x_swap(chain))

    for k in range(max(strips, nz)):
        if k < strips:
            t_give[k] += part_three(far, 1 - c, wide(k), late)
            far_swap(k).start()
        if k < nz:
            add_pair(farthest[k])
    for k in range(strips):
        new = t_mine[k] + part_three(far, c, wide(k), late)
        far_swap(k).wait_recv()
        encode(new + t_got[k], t_code.at[k], t_scale.at[k])
        both_start(far_send(k))
    def add_beside(chain, last):
        both_recv(x_swap(chain))
        total = pair_sum(chain, low) + decode(x_code_in.at[chain], x_scale_in.at[chain])
        if last:
            v_line[...] = total
        else:
            encode(total, z_code.at[chain], z_scale.at[chain])
            both_start(along(chain, z))

    def near_give():
        n_give[...] = part_three(q, 1 - c, slice(None), range(nz))
        near_swap.start()

    def near_keep():
        near_sum[...] = part_three(q, c, slice(None), range(nz))

    fillers = [near_give, near_keep]
    for k in range(nz):
        add_beside(farthest[k], k == nz - 1)
        if k < len(fillers):
            fillers[k]()
    for filler in fillers[nz:]:
        filler()
    near_swap.wait_recv()
    near_sum[...] += n_got[...]
    for k in range(1, nz):
        sender = nearest(k)
        both_recv(along(sender, sender))
        v_line[...] += decode(z_code_in.at[sender], z_scale_in.at[sender])
    v_col[...] = v_line[...].reshape(v_col.shape)
    encode(v_col[far], y_code, y_scale)
    both_start(between())
    for k in range(strips):
        both_recv(far_send(k))
        near_sum[:, wide(k)] += decode(t_code_in.at[k], t_scale_in.at[k])
    three_out[...] = near_sum[...].reshape(three_out.shape)
    both_recv(between())
    vir_out[...] = (v_col[q] + decode(y_code_in, y_scale_in)) / (n * virtuals)

    lend.wait_send()

    half_block = full.at[:part, : basis // 2]

    @pl.loop(0, nz)
    def _(chain):
        coef_relay(chain, half_block, half_block, c_recv.at[0, 0], sent)

    coef_far(half_block, half_block, c_recv.at[0, 0], sent)
    coef_halves(n - 1).wait_send()
    given().wait_send()

    def lent(blocks, sem):
        ref = cross.at[:blocks]
        return remote(ref, ref, y_send.at[sem], f_recv.at[0, 0], opposite)

    if nz > 2:
        lent(nz - 2, 0).wait_send()
    for k in range(2, nz):
        pl.when(distant(nearest(k)))(lambda: lent(1, k - 1).wait_send())

    both_rows = own.at[: 2 * width, :tile]
    hand_out([(0, 0, both_rows, both_rows)], sent)
    far_part(c).wait_send()
    near_part(c).wait_send()
    block_ref = held.at[:width, : 2 * tile]
    each_at(1, lambda chain: pass_on(chain, block_ref, f_recv.at[0, 0], sent))
    near_swap.wait_send()
    remote(t_give, t_give, t_send, t_recv.at[0], partner).wait_send()
    both_sent(coded_copies(t_code, t_scale, t_code, t_scale, (ts_send, ts_recv.at[0]), opposite))
    whole = vir.at[:, :, :, 0]
    remote(whole, whole, vp_send, vp_recv.at[0], partner).wait_send()
    both_sent(coded_copies(x_code, x_scale, x_code, x_scale, (x_send, x_recv.at[0]), (side, s)))
    codes, scales = z_code.at[: nz - 1], z_scale.at[: nz - 1]
    both_sent(coded_copies(codes, scales, codes, scales, (z_send, z_recv.at[0]), (side, s)))
    both_sent(between())


def paired(n, half_integrals, coef, occ_energy, vir_energy):
    _, tile, basis = half_integrals.shape
    part = coef.shape[0]
    virtuals = part * n
    width, rows, nz = virtuals // 4, virtuals // (4 * n), n // 2
    pieces = PIECES if basis % (256 * PIECES) == 0 else 1
    vmem = pl.BlockSpec(memory_space=pltpu.VMEM)
    dma = pltpu.SemaphoreType.DMA
    lanes = 128
    chunks = virtuals // lanes
    strip = 2 * lanes if chunks % 2 == 0 else lanes
    strips = virtuals // strip

    def room(*shape):
        return pltpu.VMEM(shape, F32)

    def packed(*shape):
        return pltpu.VMEM(shape, jnp.bfloat16)

    scratch = [
        packed(n, tile, basis), packed(tile, basis), packed(virtuals, basis), packed(virtuals, 4 * tile),
        packed(n * width, 4 * tile), packed(n, width, tile), packed(n, 2 * width, tile), packed(n * width, virtuals),
        room(nz, 2, 2, 2, rows, virtuals),
        room(strips, tile, strip), room(strips, tile, strip), room(strips, tile, strip), room(tile, virtuals), room(tile, virtuals),
        room(tile, virtuals), room(nz, 2, 2, rows, virtuals), room(2 * rows, virtuals), room(2, rows, virtuals),
    ]
    groups = tile // 32
    for _ in range(2):
        scratch += [packed(strips, tile, strip), room(strips, groups, 1, strip)]
    for _ in range(4):
        scratch += [packed(nz, 2 * rows, virtuals), room(nz, 2, 1, virtuals)]
    for _ in range(2):
        scratch += [packed(rows, virtuals), room(1, 1, virtuals)]
    scratch += [pltpu.SMEM((n,), F32), room(virtuals)]
    scratch += [
        dma((2,)), dma, dma, dma, dma((2,)), dma((n, pieces)), dma((2,)), dma((2,)), dma((nz,)), dma((2, nz)), dma((2,)),
        dma((2,)), dma((2,)), dma((n, 2)), dma((3,)), dma((2,)), dma, dma((nz,)), dma((2,)),
        dma, dma((strips,)), dma((2,)), dma((strips, 2)), dma((2,)), dma, dma((nz,)),
        dma((2,)), dma((nz, 2)), dma((2,)), dma((nz, 2)), dma((2,)), dma((2,)),
    ]
    return pl.pallas_call(
        functools.partial(paired_kernel, n),
        out_shape=(
            pltpu.VMEM((tile, 1, virtuals), F32), pltpu.VMEM((rows, virtuals), F32),
        ),
        in_specs=[pl.BlockSpec(memory_space=pl.ANY)] * 4,
        out_specs=(vmem, vmem),
        scratch_shapes=scratch,
        compiler_params=pltpu.CompilerParams(
            collective_id=0, has_side_effects=True, vmem_limit_bytes=LIMIT
        ),
        name="densities",
    )(occ_energy, half_integrals, coef, vir_energy)


def per_device(half_integrals, vir_coef, occ_energy, vir_energy):
    n, aux = lax.axis_size("occ"), lax.axis_size("aux")
    nz, nq = n // 2, aux // 2
    _, tile, basis = half_integrals.shape
    part = vir_coef.shape[1]
    virtuals = part * n
    if nq == 2 and n % 2 == 0 and nz > 1 and nz % 2 == 0 and virtuals % (32 * n) == 0 and virtuals % 256 == 0 and tile % 32 == 0:
        three, vir_rows = paired(n, half_integrals, vir_coef.T, occ_energy, vir_energy)
        return three, vir_rows
    width, rows = virtuals // aux, virtuals // (n * aux)
    vmem = pl.BlockSpec(memory_space=pltpu.VMEM)
    dma = pltpu.SemaphoreType.DMA
    half = jnp.bfloat16
    lanes = 128
    chunks = virtuals // lanes

    def room(*shape):
        return pltpu.VMEM(shape, F32)

    def result(*shape):
        return jax.ShapeDtypeStruct(shape, F32)

    def call(kernel, name, number, in_specs, out_shape, scratch, operands):
        return pl.pallas_call(
            kernel,
            out_shape=out_shape,
            in_specs=in_specs,
            out_specs=(vmem,) * len(out_shape),
            scratch_shapes=scratch,
            compiler_params=pltpu.CompilerParams(
                collective_id=number, has_side_effects=True, vmem_limit_bytes=LIMIT
            ),
            name=name,
        )(*operands)

    operands = (occ_energy, half_integrals, vir_coef.T, vir_energy)
    specs = [pl.BlockSpec(memory_space=pltpu.SMEM), pl.BlockSpec(memory_space=pl.ANY), vmem, vmem]
    make_scratch = [
        pltpu.VMEM(half_integrals.shape, half),
        pltpu.VMEM((2, virtuals, basis // 2), half),
        pltpu.VMEM((nq, 2, nq, 2 * width, tile), half),
        pltpu.VMEM((nq, 2, n * width, tile), half),
        pltpu.VMEM((n, width, tile), half),
        pltpu.VMEM((n * width, virtuals), half),
        dma, dma((2,)), dma, dma((n,)), dma((nz,)), dma((nz,)), dma((nz,)), dma((n,)), dma((n,)),
        dma((nq, nq)), dma((nq, nq)), dma((nq, nq)), dma((nq, nq)), dma((nq,)), dma((nq,)), dma((n,)), dma((n,)),
        dma((nq, n)), dma((nq, nz)), dma((nq, nz)), dma((nq, nz)),
    ]
    reduce_scratch = [
        room(nq, tile, virtuals), room(nq, tile, virtuals), room(nq, tile, virtuals),
        room(chunks, n, nq, rows, lanes), room(chunks, nz, 2, nq, rows, lanes),
        room(chunks, nz, nq, rows, lanes), room(chunks, nz, nq, rows, lanes), room(chunks, nz, nq, rows, lanes),
        room(chunks, nq, rows, lanes), room(chunks, nq, rows, lanes),
        dma((nq,)), dma((nq,)), dma((nq,)), dma((nq,)), dma((chunks,)), dma((chunks,)), dma((chunks,)), dma((chunks,)),
        dma((chunks, nz)), dma((chunks, nz)), dma((chunks, nq)), dma((chunks, nq)),
    ]
    sums = (nq, 2, tile, virtuals)
    groups = (n, nq, 2, rows, virtuals)
    finals = (result(tile, virtuals), result(tile, virtuals), result(rows, virtuals))
    if rows % 8 == 0:
        kernel = functools.partial(whole_kernel, n, nq, len(specs), len(finals), len(make_scratch))
        scratch = [room(*sums), room(*groups)] + make_scratch + reduce_scratch
        near, far, vir_rows = call(kernel, "densities", 0, specs, finals, scratch, operands)
    else:
        kernel = functools.partial(amplitude_kernel, n, nq)
        partials = (result(*sums), result(virtuals, virtuals))
        three, vir = call(kernel, "amplitude", 0, specs, partials, make_scratch, operands)
        kernel = functools.partial(reduce_kernel, n, nq)
        near, far, vir_rows = call(
            kernel, "reduce", 1, [vmem, vmem], finals, reduce_scratch, (three, vir.reshape(groups))
        )
    return (near + far)[:, None, :], vir_rows / (n * virtuals)


def solution(mesh):
    return jax.shard_map(
        per_device,
        mesh=mesh,
        in_specs=(P(None, "aux", None), P(None, "occ"), P(), P()),
        out_specs=(P("aux", "occ", None), P(("occ", "aux"), None)),
        check_vma=False,
    )
```

```python
import functools

import jax
import jax.numpy as jnp
from jax import lax
from jax.experimental import pallas as pl
from jax.experimental.pallas import tpu as pltpu
from jax.sharding import PartitionSpec as P

MESH = pl.DeviceIdType.MESH
F32 = jnp.float32
PIECES = 4
SPAN = 80.0
TINY = 1e-30
LIMIT = 56 * 1024 * 1024


def remote(src, dst, send, recv, target):
    return pltpu.make_async_remote_copy(
        src_ref=src, dst_ref=dst, send_sem=send, recv_sem=recv, device_id=target, device_id_type=MESH
    )


def nearest_first(z, k, count):
    near = jnp.minimum(z, count - 1 - z)
    step = (k + 1) // 2
    both = z + step * (2 * (k % 2) - 1)
    low = z < count - 1 - z
    return jnp.where(k <= 2 * near, both, jnp.where(low, k, count - 1 - k))


def greet(n, nq):
    o = lax.axis_index("occ")
    s = lax.axis_index("aux")
    q, c = s // 2, s % 2
    z, low = o // 2, o % 2
    nz = n // 2
    barrier = pltpu.get_barrier_semaphore()
    peers = [(2 * z + 1 - low, s), (o, 2 * q + 1 - c)]
    peers += [(o, 2 * ((q + d) % nq) + c) for d in range(1, nq)]
    peers += [(2 * ((z + d) % nz) + low, s) for d in range(1, nz)]
    for peer in peers:
        pl.semaphore_signal(barrier, inc=1, device_id=peer, device_id_type=MESH)
    return lambda: pl.semaphore_wait(barrier, len(peers))


def make_densities(
    n, nq, occ_e, half, coef, vir_e, three, vir,
    ints, full, own, held, gift, amps,
    i_sem, c_copy, o_copy, c_recv, c_up, c_down, c_side, cp_send, cp_recv,
    own_send, own_recv, fw_send, fw_recv, pr_send, pr_recv, g_send, g_recv,
    h_recv, h_up, h_down, h_side,
    vir_done=lambda: None,
):
    o = lax.axis_index("occ")
    s = lax.axis_index("aux")
    q, c = s // 2, s % 2
    z, low = o // 2, o % 2
    nz = n // 2
    width = amps.shape[0] // n
    part = coef.shape[0]
    cut = coef.shape[1] // 2
    virtuals = amps.shape[1]
    above, below, side = o + 2, o - 2, 2 * z + 1 - low
    partner = (o, 2 * q + 1 - c)
    entered = greet(n, nq)

    fetch = pltpu.make_async_copy(half, ints, i_sem)
    fetch.start()

    def span(index, size):
        return pl.ds(pl.multiple_of(index * size, size), size)

    def keep(h):
        return pltpu.make_async_copy(coef.at[:, h * cut : (h + 1) * cut], full.at[h, span(o, part)], c_copy.at[h])

    keep(0).start()
    keep(1).start()
    entered()

    def relay(chain, src, dst, up, down, across, recv, act):
        pl.when(jnp.logical_and(chain <= z, z < nz - 1))(lambda: act(remote(src, dst, up, recv, (above, s))))
        pl.when(jnp.logical_and(chain >= z, z > 0))(lambda: act(remote(src, dst, down, recv, (below, s))))
        act(remote(src, dst, across, recv, (side, s)))

    def start(copy):
        copy.start()

    def sent(copy):
        copy.wait_send()

    def coef_slot(block):
        return full.at[c, span(block, part)]

    def coef_relay(chain, src, act):
        block = 2 * chain + low
        relay(chain, src, coef_slot(block), c_up.at[chain], c_down.at[chain], c_side.at[chain], c_recv.at[block], act)

    def coef_across(block):
        return remote(coef_slot(block), coef_slot(block), cp_send.at[block], cp_recv.at[block], partner)

    def coef_arrived(block):
        remote(coef_slot(block), coef_slot(block), c_side.at[0], c_recv.at[block], (side, s)).wait_recv()
        coef_across(block).start()

    coef_relay(z, coef.at[:, span(c, cut)], start)
    three[...] = jnp.zeros_like(three)
    vir[...] = jnp.zeros_like(vir)
    row_e = vir_e[...].reshape(1, virtuals)
    here = lax.broadcasted_iota(jnp.int32, (width, virtuals), 0) + s * width
    there = lax.broadcasted_iota(jnp.int32, (width, virtuals), 1)
    col_e = jnp.sum(jnp.where(here == there, row_e, 0.0), axis=1, keepdims=True)

    @pl.loop(1, nz)
    def _(k):
        chain = nearest_first(z, k, nz)
        block = 2 * chain + low
        remote(coef_slot(block), coef_slot(block), c_side.at[0], c_recv.at[block], (side, s)).wait_recv()
        coef_relay(chain, coef_slot(block), start)
        coef_across(block).start()
        coef_arrived(2 * nearest_first(z, k - 1, nz) + 1 - low)

    coef_arrived(2 * nearest_first(z, nz - 1, nz) + 1 - low)

    @pl.loop(1, n)
    def _(d):
        block = (o + d) % n
        other = full.at[1 - c, span(block, part)]
        remote(other, other, cp_send.at[block], cp_recv.at[block], partner).wait_recv()

    keep(0).wait()
    keep(1).wait()
    fetch.wait()

    def transform(block, rows):
        contract = (((1,), (1,)), ((), ()))
        return sum(
            lax.dot_general(
                full[h, rows, :], ints[block, :, h * cut : (h + 1) * cut], contract, preferred_element_type=F32
            )
            for h in range(2)
        ).astype(jnp.bfloat16)

    order = list(range(1, nq)) + [0]

    def chunk(there, core, group):
        return own.at[there, core, group]

    def to_partner(r):
        ref = chunk(q, c, (q + r) % nq)
        return remote(ref, ref, pr_send.at[r], pr_recv.at[r], partner)

    def to_chip(d, r):
        ref = chunk(q, c, (q + r) % nq)
        return remote(ref, ref, own_send.at[d, r], own_recv.at[d, r], (o, 2 * ((q + d) % nq) + c))

    def onward(d, r, core):
        there = (q + nq - d) % nq
        ref = chunk(there, core, (there + r) % nq)
        return remote(ref, ref, fw_send.at[d, r], fw_recv.at[d, r], partner)

    def from_chip(d, r):
        there = (q + nq - d) % nq
        ref = chunk(there, c, (there + r) % nq)
        remote(ref, ref, own_send.at[d, r], own_recv.at[d, r], partner).wait_recv()
        onward(d, r, c).start()

    for r in order:
        group = (q + r) % nq
        own[q, c, group] = transform(o, span(group, 2 * width))
        for d in range(1, nq):
            to_chip(d, r).start()
        to_partner(r).start()

    def give(block, core):
        return remote(
            gift.at[block], held.at[q, core, span(block, width)], g_send.at[block], g_recv.at[block], partner
        )

    @pl.loop(1, n)
    def _(d):
        block = (o + d) % n
        gift[block] = transform(block, span(2 * q + 1 - c, width))
        give(block, c).start()
        held[q, c, span(block, width), :] = transform(block, span(s, width))

    def held_slot(d, block):
        return held.at[(q + nq - d) % nq, :, span(block, width)]

    def own_slot(d):
        return own.at[(q + nq - d) % nq, :, q, span(c, width)]

    def held_relay(d, chain, src, act):
        block = 2 * chain + low
        relay(
            chain, src, held_slot(d, block), h_up.at[d, chain], h_down.at[d, chain], h_side.at[d, chain],
            h_recv.at[d, block], act,
        )

    def arrived(block):
        for d in range(1, nq):
            ref = held_slot(d, block)
            remote(ref, ref, h_side.at[d, 0], h_recv.at[d, block], (side, s)).wait_recv()

    for d in range(1, nq):
        from_chip(d, d)
    for d in range(1, nq):
        onward(d, d, 1 - c).wait_recv()
        held_relay(d, z, own_slot(d), start)
    rest = [(d, r) for d in range(1, nq) for r in order if r != d]
    for d, r in rest:
        from_chip(d, r)
    for r in order:
        ref = chunk(q, 1 - c, (q + r) % nq)
        remote(ref, ref, pr_send.at[r], pr_recv.at[r], partner).wait_recv()

    @pl.loop(1, n)
    def _(d):
        give((o + d) % n, 1 - c).wait_recv()

    for d, r in rest:
        onward(d, r, 1 - c).wait_recv()
    mine = pltpu.make_async_copy(
        own.at[:, :, q, span(c, width)], held.at[:, :, span(o, width)], o_copy
    )
    mine.start()
    mine.wait()

    def absorb(block):
        rows = span(block, width)
        coulomb = sum(
            lax.dot_general(
                held[t // 2, t % 2, rows, :], own[t // 2, t % 2].reshape(virtuals, -1),
                (((1,), (1,)), ((), ())), preferred_element_type=F32,
            )
            for t in range(2 * nq)
        )
        denominator = occ_e[o] + occ_e[block] - col_e - row_e
        amps[rows, :] = (coulomb / denominator).astype(jnp.bfloat16)

    contract = (((0,), (0,)), ((), ()))
    piece = virtuals // 2 if len(vir.shape) > 2 else 256

    def add_vir(chain):
        rows = span(chain, 2 * width)

        @pl.loop(0, virtuals // piece)
        def _(t):
            new = lax.dot_general(
                amps[rows, span(t, piece)], amps[rows, :], contract, preferred_element_type=F32
            )
            where = span(t, vir.shape[0] * piece // virtuals)
            vir[where] += new.reshape((-1,) + vir.shape[1:])

    def add_three(chain):
        rows = span(chain, 2 * width)

        @pl.loop(0, 2 * nq)
        def _(t):
            three[t // 2, t % 2] += lax.dot_general(
                held[t // 2, t % 2, rows, :], amps[rows, :], contract, preferred_element_type=F32
            )

    def both(chain):
        absorb(2 * chain + low)
        arrived(2 * chain + 1 - low)
        absorb(2 * chain + 1 - low)

    @pl.loop(1, nz)
    def _(k):
        chain = nearest_first(z, k, nz)
        arrived(2 * chain + low)
        for d in range(1, nq):
            held_relay(d, chain, held_slot(d, 2 * chain + low), start)
        before = nearest_first(z, k - 1, nz)
        both(before)
        add_vir(before)
        add_three(before)

    last = nearest_first(z, nz - 1, nz)
    both(last)
    add_vir(last)
    vir_done()
    add_three(last)

    def finish():
        @pl.loop(0, nz)
        def _(chain):
            coef_relay(chain, coef_slot(2 * chain + low), sent)
            for d in range(1, nq):
                held_relay(d, chain, held_slot(d, 2 * chain + low), sent)

        @pl.loop(1, n)
        def _(d):
            block = (o + d) % n
            coef_across(block).wait_send()
            give(block, c).wait_send()

        for r in order:
            to_partner(r).wait_send()
            for d in range(1, nq):
                to_chip(d, r).wait_send()
                onward(d, r, c).wait_send()

    return finish


def reduction(
    n, nq, three, vir, near_out, far_out, vir_out,
    t_pair, t_out, t_far, v_pair, v_sum, v_side, v_line, v_chain, v_col, v_far,
    pair_send, pair_recv, t_send, t_recv, vp_send, vp_recv, x_send, x_recv, z_send, z_recv, y_send, y_recv,
):
    o = lax.axis_index("occ")
    s = lax.axis_index("aux")
    q, c = s // 2, s % 2
    z, low = o // 2, o % 2
    nz = n // 2
    chunks, chunk = v_pair.shape[0], v_pair.shape[-1]
    partner = (o, 2 * q + 1 - c)
    side = (2 * z + 1 - low, s)

    def cols(k):
        return pl.ds(k * chunk, chunk)

    def v_swap(k):
        return remote(vir.at[:, :, 1 - c, :, cols(k)], v_pair.at[k], vp_send.at[k], vp_recv.at[k], partner)

    def x_swap(k):
        return remote(v_sum.at[k, :, 1 - low], v_side.at[k], x_send.at[k], x_recv.at[k], side)

    def along(k, d):
        there = (z + d) % nz
        return remote(
            v_line.at[k, there], v_chain.at[k, d], z_send.at[k, d], z_recv.at[k, d], (2 * there + low, s)
        )

    def between(k, d):
        there = (q + d) % nq
        return remote(v_col.at[k, there], v_far.at[k, d], y_send.at[k, d], y_recv.at[k, d], (o, 2 * there + c))

    def swap(d):
        return remote(three.at[(q + d) % nq, 1 - c], t_pair.at[d], pair_send.at[d], pair_recv.at[d], partner)

    def spread(d):
        return remote(t_out.at[d], t_far.at[d], t_send.at[d], t_recv.at[d], (o, 2 * ((q + d) % nq) + c))

    order = list(range(1, nq)) + [0]

    def open_vir():
        for k in range(chunks):
            v_swap(k).start()

    def close():
        for d in order:
            swap(d).start()
        for k in range(chunks):
            v_swap(k).wait()
            v_sum[k] = (vir[:, :, c, :, cols(k)] + v_pair[k]).reshape(v_sum.shape[1:])
            x_swap(k).start()
        for d in order[:-1]:
            swap(d).wait()
            t_out[d] = three[(q + d) % nq, c] + t_pair[d]
            spread(d).start()
        for k in range(chunks):
            x_swap(k).wait()
            v_line[k] = v_sum[k, :, low] + v_side[k]
            for d in range(1, nz):
                along(k, d).start()
            if k == 0:
                swap(0).wait()
                near_out[...] = three[q, c] + t_pair[0]
        for k in range(chunks):
            held = v_line[k, z]
            for d in range(1, nz):
                along(k, d).wait()
                held += v_chain[k, d]
            v_col[k] = held
            for d in range(1, nq):
                between(k, d).start()
        for d in order[:-1]:
            spread(d).wait()
            far_out[...] = t_far[d] if d == 1 else far_out[...] + t_far[d]
        for k in range(chunks):
            rows = v_col[k, q]
            for d in range(1, nq):
                between(k, d).wait()
                rows += v_far[k, d]
            vir_out[:, cols(k)] = rows

    return open_vir, close


def amplitude_kernel(n, nq, *refs):
    make_densities(n, nq, *refs)()


def reduce_kernel(n, nq, *refs):
    greet(n, nq)()
    open_vir, close = reduction(n, nq, *refs)
    open_vir()
    close()


def whole_kernel(n, nq, inputs, outputs, count, *refs):
    operands, results, scratch = refs[:inputs], refs[inputs : inputs + outputs], refs[inputs + outputs :]
    three, vir, rest = scratch[0], scratch[1], scratch[2:]
    open_vir, close = reduction(n, nq, three, vir, *results, *rest[count:])
    finish = make_densities(n, nq, *operands, three, vir, *rest[:count], vir_done=open_vir)
    close()
    finish()


def paired_kernel(
    n, occ_e, half, coef, vir_e, three_out, vir_out,
    ints, raw, full, own, held, gift, cross, amps, vir,
    t_give, t_mine, t_got, n_give, n_got, near_sum, v_pair, v_line, v_col,
    t_code, t_scale, t_code_in, t_scale_in, x_code, x_scale, x_code_in, x_scale_in,
    z_code, z_scale, z_code_in, z_scale_in, y_code, y_scale, y_code_in, y_scale_in, energies, levels,
    e_sems, i_sem, keep_sem, o_sem, raw_sems, c_recv, c_up, c_down, c_side, c_jump, cp_sems,
    pn_sems, pf_sems, f_recv, f_send, z_fwd, x_fwd, y_send, g_sems,
    t_send, t_recv, ts_send, ts_recv, n_sems, vp_send, vp_recv, x_send, x_recv, z_send, z_recv, yv_send, yv_recv,
):
    o = lax.axis_index("occ")
    s = lax.axis_index("aux")
    q, c = s // 2, s % 2
    z, low = o // 2, o % 2
    nz = n // 2
    far = 1 - q
    part, basis = coef.shape
    tile = raw.shape[0]
    virtuals = full.shape[0]
    width = virtuals // 4
    pieces = c_recv.shape[1]
    piece = basis // (2 * pieces)
    above, below, side = o + 2, o - 2, 2 * z + 1 - low
    other = 2 * q + 1 - c
    partner = (o, other)
    opposite = (o, 2 * far + c)

    def span(index, size):
        return pl.ds(pl.multiple_of(index * size, size), size)

    def start(copy):
        copy.start()

    def sent(copy):
        copy.wait_send()

    def nearest(k):
        return nearest_first(z, k, nz)

    at_end = jnp.logical_or(z == 0, z == nz - 1)
    inner_order = [0] + list(range(2, nz)) + [1]
    end_order = [0, nz - 1] + list(range(1, nz - 1))
    order = [nearest(jnp.where(at_end, a, b)) for a, b in zip(end_order, inner_order)]

    barrier = pltpu.get_barrier_semaphore()
    peers = [partner, opposite, (o, 2 * far + 1 - c), (side, s), (side, other)]
    peers += [(2 * ((z + d) % nz) + low, t) for d in range(1, nz) for t in (s, other)]
    for peer in peers:
        pl.semaphore_signal(barrier, inc=1, device_id=peer, device_id_type=MESH)
    small = [pltpu.make_async_copy(occ_e, energies, e_sems.at[0]), pltpu.make_async_copy(vir_e, levels, e_sems.at[1])]
    fetch = pltpu.make_async_copy(half, ints, i_sem)
    fetch.start()
    keep = pltpu.make_async_copy(coef, full.at[span(o, part)], keep_sem)
    keep.start()
    for copy in small:
        copy.start()
    pl.semaphore_wait(barrier, len(peers))

    lend = remote(half.at[o], raw, raw_sems.at[0], raw_sems.at[1], opposite)

    def coef_slot(block, core, h):
        return full.at[span(block, part), pl.ds(pl.multiple_of((pieces * core + h) * piece, piece), piece)]

    def coef_relay(chain, src, dst, recv, act):
        pl.when(jnp.logical_and(jnp.logical_and(chain <= z, chain > z - 2), z < nz - 1))(
            lambda: act(remote(src, dst, c_up.at[z - chain], recv, (above, s)))
        )
        pl.when(jnp.logical_and(jnp.logical_and(chain >= z, chain < z + 2), z > 0))(
            lambda: act(remote(src, dst, c_down.at[chain - z], recv, (below, s)))
        )
        act(remote(src, dst, c_side.at[chain], recv, (side, s)))

    def coef_across(block, h, core):
        ref = coef_slot(block, core, h)
        return remote(ref, ref, cp_sems.at[0], cp_sems.at[1], partner)

    def coef_wait(block, h):
        ref = coef_slot(block, c, h)
        remote(ref, ref, c_side.at[0], c_recv.at[block, h], (side, s)).wait_recv()

    def coef_own(h):
        return coef.at[:, pl.ds(pl.multiple_of((pieces * c + h) * piece, piece), piece)]

    def coef_far(src, dst, recv, act):
        for d in range(3, nz):
            pl.when(z + d < nz)(
                lambda: act(remote(src, dst, c_jump.at[0, d], recv, (o + 2 * d, s)))
            )
            pl.when(z >= d)(
                lambda: act(remote(src, dst, c_jump.at[1, d], recv, (o - 2 * d, s)))
            )

    for h in range(pieces):
        coef_relay(z, coef_own(h), coef_slot(o, c, h), c_recv.at[o, h], start)
    for h in range(pieces):
        coef_far(coef_own(h), coef_slot(o, c, h), c_recv.at[o, h], start)
    lend.start()
    for copy in small:
        copy.wait()
    row_e = levels[...].reshape(1, virtuals)
    here = lax.broadcasted_iota(jnp.int32, (width, virtuals), 0) + s * width
    there = lax.broadcasted_iota(jnp.int32, (width, virtuals), 1)
    col_e = jnp.sum(jnp.where(here == there, row_e, 0.0), axis=1, keepdims=True)

    def each_at(d, act):
        pl.when(z + d < nz)(lambda: act(z + d))
        pl.when(z >= d)(lambda: act(z - d))

    def coef_beside(chain, h):
        block = 2 * chain + 1 - low
        coef_wait(block, h)
        coef_across(block, h, c).start()

    def coef_along(chain, h):
        block = 2 * chain + low
        slot = coef_slot(block, c, h)
        coef_wait(block, h)
        coef_relay(chain, slot, slot, c_recv.at[block, h], start)
        coef_across(block, h, c).start()

    for h in range(pieces):
        each_at(1, lambda chain: coef_along(chain, h))
    for h in range(pieces):
        coef_beside(z, h)
        for d in list(range(3, nz)) + [2]:
            each_at(d, lambda chain: coef_along(chain, h))
    for d in [1] + list(range(3, nz)) + [2]:
        for h in range(pieces):
            each_at(d, lambda chain: coef_beside(chain, h))

    def coef_halves(blocks):
        ref = full.at[: blocks * part, : basis // 2]
        return remote(ref, ref, cp_sems.at[0], cp_sems.at[1], partner)

    coef_halves(n - 1).wait_recv()

    keep.wait()
    fetch.wait()

    def transform(rows, source):
        return lax.dot_general(rows, source, (((1,), (1,)), ((), ())), preferred_element_type=F32).astype(jnp.bfloat16)

    def cols(group, core):
        return span(2 * group + core, tile)

    def lend_block(block, sem, act):
        for core in range(2):
            act(
                remote(
                    cross.at[block, pl.ds(core * width, width)], held.at[span(block, width), cols(q, c)],
                    y_send.at[sem], f_recv.at[block, 0], (o, 2 * far + core),
                )
            )

    def distant(chain):
        return jnp.abs(chain - z) > 2

    def cross_over(block, sem):
        cross[block] = transform(full[span(far, 2 * width), :], ints[block])
        lend_block(block, sem, start)

    @pl.loop(2, nz)
    def _(k):
        chain = nearest(jnp.where(at_end, nz + 1 - k, k))
        cross_over(2 * chain + 1 - low, 0)
        pl.when(distant(chain))(lambda: cross_over(2 * chain + low, jnp.where(at_end, nz - k, k - 1)))

    def own_part(group, core):
        return own.at[:, cols(group, core)]

    def near_part(core):
        ref = own_part(q, core)
        return remote(ref, ref, pn_sems.at[0], pn_sems.at[1], partner)

    def far_part(core):
        ref = own_part(far, core)
        return remote(ref, ref, pf_sems.at[0], pf_sems.at[1], partner)

    def hand_out(parts, act):
        for core, t, src, dst in parts:
            recv = f_recv.at[o, t]
            to = 2 * q + core
            pl.when(z < nz - 1)(lambda: act(remote(src, dst, f_send.at[0], recv, (above, to))))
            pl.when(z > 0)(lambda: act(remote(src, dst, f_send.at[1], recv, (below, to))))
            act(remote(src, dst, f_send.at[2], recv, (side, to)))

    part_rows = width // 2

    def outgoing(core, t):
        rows = pl.ds(pl.multiple_of((2 * q + core) * width + t * part_rows, part_rows), part_rows)
        return core, t, own.at[rows, cols(far, c)], held.at[span(2 * o + t, part_rows), cols(far, c)]

    lend.wait_recv()
    own[:, cols(far, c)] = transform(full[...], raw[...])
    hand_out([outgoing(core, t) for t in range(2) for core in range(2)], start)
    far_part(c).start()
    own[:, cols(q, c)] = transform(full[...], ints[o])
    near_part(c).start()

    def give(block, core):
        return remote(
            gift.at[block], held.at[span(block, width), cols(q, core)], g_sems.at[0], g_sems.at[1], partner
        )

    @pl.loop(1, n)
    def _(d):
        block = (o + d) % n
        rows = jnp.concatenate([full[span(s, width), :], full[span(other, width), :]], axis=0)
        both = transform(rows, ints[block])
        held[span(block, width), cols(q, c)] = both[:width]
        gift[block] = both[width:]
        give(block, c).start()

    def given():
        ref = gift.at[: n - 1]
        return remote(ref, ref, g_sems.at[0], g_sems.at[1], partner)

    far_part(1 - c).wait_recv()
    near_part(1 - c).wait_recv()
    mine = pltpu.make_async_copy(own.at[span(s, width)], held.at[span(o, width)], o_sem)
    mine.start()

    def far_piece(block, t):
        return held.at[span(2 * block + t, part_rows), span(far, 2 * tile)]

    def arrive(block):
        ref = held.at[span(block, width), span(far, 2 * tile)]
        remote(ref, ref, x_fwd, f_recv.at[block, 0], (side, s)).wait_recv()

    def arrive_pieces(block):
        for t in range(2):
            ref = far_piece(block, t)
            remote(ref, ref, x_fwd, f_recv.at[block, t], (side, s)).wait_recv()

    def pass_on(chain, ref, recv, act):
        pl.when(jnp.logical_and(chain < z, z < nz - 1))(lambda: act(remote(ref, ref, z_fwd.at[0], recv, (above, s))))
        pl.when(jnp.logical_and(chain > z, z > 0))(lambda: act(remote(ref, ref, z_fwd.at[1], recv, (below, s))))
        pl.when(chain == nearest(1))(lambda: act(remote(ref, ref, x_fwd, recv, (side, s))))

    def take(chain, t):
        block = 2 * chain + low
        ref = far_piece(block, t)
        remote(ref, ref, x_fwd, f_recv.at[block, t], (side, s)).wait_recv()
        pass_on(chain, ref, f_recv.at[block, t], start)

    for t in range(2):
        each_at(1, lambda chain: take(chain, t))
    given().wait_recv()
    mine.wait()

    def absorb(slot, chain):
        coulomb = lax.dot_general(
            held[span(chain, 2 * width), :], own[...], (((1,), (1,)), ((), ())), preferred_element_type=F32
        )
        left = jnp.concatenate([energies[o] + energies[2 * chain + t] - col_e for t in range(2)], axis=0)
        amps[slot * 2 * width : (slot + 1) * 2 * width, :] = (coulomb / (left - row_e)).astype(jnp.bfloat16)

    contract = (((0,), (0,)), ((), ()))
    strips, strip = t_give.shape[0], t_give.shape[-1]
    rows = vir.shape[4]
    middle = virtuals // 2

    def wide(k):
        return pl.ds(k * strip, strip)

    early, late = range(nz // 2), range(nz // 2, nz)

    def amps_of(slots, where=slice(None)):
        return amps[slots[0] * 2 * width : (slots[-1] + 1) * 2 * width, where]

    def part_three(group, core, where, slots):
        rows = [held[span(order[i], 2 * width), cols(group, core)] for i in slots]
        return lax.dot_general(
            jnp.concatenate(rows, axis=0), amps_of(slots, where), contract, preferred_element_type=F32
        )

    def part_vir(half, slots):
        new = lax.dot_general(
            amps_of(slots, span(half, middle)), amps_of(slots), contract, preferred_element_type=F32
        )
        return new.reshape((nz // 2,) + vir.shape[1:])

    def admit(i):
        chain = order[i]
        pl.when(distant(chain))(lambda: arrive(2 * chain + low))
        pl.when(jnp.abs(chain - z) == 2)(lambda: arrive_pieces(2 * chain + low))
        passed = jnp.logical_or(chain == z, chain == nearest(1))
        pl.when(passed)(lambda: arrive_pieces(2 * chain + 1 - low))
        pl.when(jnp.logical_not(passed))(lambda: arrive(2 * chain + 1 - low))
        absorb(i, chain)

    for i in early:
        admit(i)
    for half in range(2):
        vir[pl.ds(half * (nz // 2), nz // 2)] = part_vir(half, early)
    for k in range(strips):
        t_give[k] = part_three(far, 1 - c, wide(k), early)
        t_mine[k] = part_three(far, c, wide(k), early)
    for i in late:
        admit(i)

    def far_swap(k):
        return remote(t_give.at[k], t_got.at[k], t_send, t_recv.at[k], partner)

    def coded_copies(code, scale, code_to, scale_to, sems, target):
        return (
            remote(code, code_to, sems[0].at[0], sems[1].at[0], target),
            remote(scale, scale_to, sems[0].at[1], sems[1].at[1], target),
        )

    def far_send(k):
        sems = (ts_send, ts_recv.at[k])
        return coded_copies(t_code.at[k], t_scale.at[k], t_code_in.at[k], t_scale_in.at[k], sems, opposite)

    def x_swap(chain):
        sems = (x_send, x_recv.at[chain])
        return coded_copies(
            x_code.at[chain], x_scale.at[chain], x_code_in.at[chain], x_scale_in.at[chain], sems, (side, s)
        )

    def along(to, sender):
        sems = (z_send, z_recv.at[sender])
        return coded_copies(
            z_code.at[to], z_scale.at[to], z_code_in.at[sender], z_scale_in.at[sender], sems, (2 * to + low, s)
        )

    def both_start(copies):
        for copy in copies:
            copy.start()

    def both_recv(copies):
        for copy in copies:
            copy.wait_recv()

    def both_sent(copies):
        for copy in copies:
            copy.wait_send()

    def encode(value, code, scale):
        parts = scale.shape[0]
        size = value.shape[0] // parts
        grouped = value.reshape(parts, size, value.shape[1])
        top = jnp.maximum(jnp.max(jnp.abs(grouped), axis=1, keepdims=True), TINY)
        scale[...] = top
        code[...] = jnp.exp(grouped * (SPAN / top)).astype(jnp.bfloat16).reshape(value.shape)

    def decode(code, scale):
        parts = scale.shape[0]
        words = jnp.log(code[...].astype(F32)).reshape(parts, code.shape[0] // parts, code.shape[1])
        return (words * (scale[...] * (1.0 / SPAN))).reshape(code.shape)

    def v_swap(chain):
        return remote(vir.at[chain, :, :, 1 - c], v_pair.at[chain], vp_send, vp_recv.at[chain], partner)

    def between():
        return coded_copies(y_code, y_scale, y_code_in, y_scale_in, (yv_send, yv_recv), opposite)

    near_swap = remote(n_give, n_got, n_sems.at[0], n_sems.at[1], partner)
    first = jnp.where(z < nz // 2, 1, 0)
    for half in (first, 1 - first):
        where = pl.ds(half * (nz // 2), nz // 2)
        vir[where] = vir[where] + part_vir(half, late)
        for t in range(nz // 2):
            v_swap(half * (nz // 2) + t).start()

    def pair_sum(chain, across):
        return (vir[chain, across, :, c] + v_pair[chain, across]).reshape(2 * rows, virtuals)

    farthest = [nearest(k) for k in reversed(range(nz))]

    def add_pair(chain):
        v_swap(chain).wait_recv()
        encode(pair_sum(chain, 1 - low), x_code.at[chain], x_scale.at[chain])
        both_start(x_swap(chain))

    for k in range(max(strips, nz)):
        if k < strips:
            t_give[k] += part_three(far, 1 - c, wide(k), late)
            far_swap(k).start()
        if k < nz:
            add_pair(farthest[k])
    for k in range(strips):
        new = t_mine[k] + part_three(far, c, wide(k), late)
        far_swap(k).wait_recv()
        encode(new + t_got[k], t_code.at[k], t_scale.at[k])
        both_start(far_send(k))
    def add_beside(chain, last):
        both_recv(x_swap(chain))
        total = pair_sum(chain, low) + decode(x_code_in.at[chain], x_scale_in.at[chain])
        if last:
            v_line[...] = total
        else:
            encode(total, z_code.at[chain], z_scale.at[chain])
            both_start(along(chain, z))

    def near_give():
        n_give[...] = part_three(q, 1 - c, slice(None), range(nz))
        near_swap.start()

    def near_keep():
        near_sum[...] = part_three(q, c, slice(None), range(nz))

    fillers = [near_give, near_keep]
    for k in range(nz):
        add_beside(farthest[k], k == nz - 1)
        if k < len(fillers):
            fillers[k]()
    for filler in fillers[nz:]:
        filler()
    near_swap.wait_recv()
    near_sum[...] += n_got[...]
    for k in range(1, nz):
        sender = nearest(k)
        both_recv(along(sender, sender))
        v_line[...] += decode(z_code_in.at[sender], z_scale_in.at[sender])
    v_col[...] = v_line[...].reshape(v_col.shape)
    encode(v_col[far], y_code, y_scale)
    both_start(between())
    for k in range(strips):
        both_recv(far_send(k))
        near_sum[:, wide(k)] += decode(t_code_in.at[k], t_scale_in.at[k])
    three_out[...] = near_sum[...].reshape(three_out.shape)
    both_recv(between())
    vir_out[...] = (v_col[q] + decode(y_code_in, y_scale_in)) / (n * virtuals)

    lend.wait_send()

    half_block = full.at[:part, : basis // 2]

    @pl.loop(0, nz)
    def _(chain):
        coef_relay(chain, half_block, half_block, c_recv.at[0, 0], sent)

    coef_far(half_block, half_block, c_recv.at[0, 0], sent)
    coef_halves(n - 1).wait_send()
    given().wait_send()

    def lent(blocks, sem):
        ref = cross.at[:blocks]
        return remote(ref, ref, y_send.at[sem], f_recv.at[0, 0], opposite)

    if nz > 2:
        lent(nz - 2, 0).wait_send()
    for k in range(2, nz):
        pl.when(distant(nearest(k)))(lambda: lent(1, k - 1).wait_send())

    both_rows = own.at[: 2 * width, :tile]
    hand_out([(0, 0, both_rows, both_rows)], sent)
    far_part(c).wait_send()
    near_part(c).wait_send()
    block_ref = held.at[:width, : 2 * tile]
    each_at(1, lambda chain: pass_on(chain, block_ref, f_recv.at[0, 0], sent))
    near_swap.wait_send()
    remote(t_give, t_give, t_send, t_recv.at[0], partner).wait_send()
    both_sent(coded_copies(t_code, t_scale, t_code, t_scale, (ts_send, ts_recv.at[0]), opposite))
    whole = vir.at[:, :, :, 0]
    remote(whole, whole, vp_send, vp_recv.at[0], partner).wait_send()
    both_sent(coded_copies(x_code, x_scale, x_code, x_scale, (x_send, x_recv.at[0]), (side, s)))
    codes, scales = z_code.at[: nz - 1], z_scale.at[: nz - 1]
    both_sent(coded_copies(codes, scales, codes, scales, (z_send, z_recv.at[0]), (side, s)))
    both_sent(between())


def paired(n, half_integrals, coef, occ_energy, vir_energy):
    _, tile, basis = half_integrals.shape
    part = coef.shape[0]
    virtuals = part * n
    width, rows, nz = virtuals // 4, virtuals // (4 * n), n // 2
    pieces = PIECES if basis % (256 * PIECES) == 0 else 1
    vmem = pl.BlockSpec(memory_space=pltpu.VMEM)
    dma = pltpu.SemaphoreType.DMA
    lanes = 128
    chunks = virtuals // lanes
    strip = 2 * lanes if chunks % 2 == 0 else lanes
    strips = virtuals // strip

    def room(*shape):
        return pltpu.VMEM(shape, F32)

    def packed(*shape):
        return pltpu.VMEM(shape, jnp.bfloat16)

    scratch = [
        packed(n, tile, basis), packed(tile, basis), packed(virtuals, basis), packed(virtuals, 4 * tile),
        packed(n * width, 4 * tile), packed(n, width, tile), packed(n, 2 * width, tile), packed(n * width, virtuals),
        room(nz, 2, 2, 2, rows, virtuals),
        room(strips, tile, strip), room(strips, tile, strip), room(strips, tile, strip), room(tile, virtuals), room(tile, virtuals),
        room(tile, virtuals), room(nz, 2, 2, rows, virtuals), room(2 * rows, virtuals), room(2, rows, virtuals),
    ]
    groups = tile // 32
    for _ in range(2):
        scratch += [packed(strips, tile, strip), room(strips, groups, 1, strip)]
    for _ in range(4):
        scratch += [packed(nz, 2 * rows, virtuals), room(nz, 2, 1, virtuals)]
    for _ in range(2):
        scratch += [packed(rows, virtuals), room(1, 1, virtuals)]
    scratch += [pltpu.SMEM((n,), F32), room(virtuals)]
    scratch += [
        dma((2,)), dma, dma, dma, dma((2,)), dma((n, pieces)), dma((2,)), dma((2,)), dma((nz,)), dma((2, nz)), dma((2,)),
        dma((2,)), dma((2,)), dma((n, 2)), dma((3,)), dma((2,)), dma, dma((nz,)), dma((2,)),
        dma, dma((strips,)), dma((2,)), dma((strips, 2)), dma((2,)), dma, dma((nz,)),
        dma((2,)), dma((nz, 2)), dma((2,)), dma((nz, 2)), dma((2,)), dma((2,)),
    ]
    return pl.pallas_call(
        functools.partial(paired_kernel, n),
        out_shape=(
            pltpu.VMEM((tile, 1, virtuals), F32), pltpu.VMEM((rows, virtuals), F32),
        ),
        in_specs=[pl.BlockSpec(memory_space=pl.ANY)] * 4,
        out_specs=(vmem, vmem),
        scratch_shapes=scratch,
        compiler_params=pltpu.CompilerParams(
            collective_id=0, has_side_effects=True, vmem_limit_bytes=LIMIT
        ),
        name="densities",
    )(occ_energy, half_integrals, coef, vir_energy)


def per_device(half_integrals, vir_coef, occ_energy, vir_energy):
    n, aux = lax.axis_size("occ"), lax.axis_size("aux")
    nz, nq = n // 2, aux // 2
    _, tile, basis = half_integrals.shape
    part = vir_coef.shape[1]
    virtuals = part * n
    if nq == 2 and n % 2 == 0 and nz > 1 and nz % 2 == 0 and virtuals % (32 * n) == 0 and virtuals % 256 == 0 and tile % 32 == 0:
        three, vir_rows = paired(n, half_integrals, vir_coef.T, occ_energy, vir_energy)
        return three, vir_rows
    width, rows = virtuals // aux, virtuals // (n * aux)
    vmem = pl.BlockSpec(memory_space=pltpu.VMEM)
    dma = pltpu.SemaphoreType.DMA
    half = jnp.bfloat16
    lanes = 128
    chunks = virtuals // lanes

    def room(*shape):
        return pltpu.VMEM(shape, F32)

    def result(*shape):
        return jax.ShapeDtypeStruct(shape, F32)

    def call(kernel, name, number, in_specs, out_shape, scratch, operands):
        return pl.pallas_call(
            kernel,
            out_shape=out_shape,
            in_specs=in_specs,
            out_specs=(vmem,) * len(out_shape),
            scratch_shapes=scratch,
            compiler_params=pltpu.CompilerParams(
                collective_id=number, has_side_effects=True, vmem_limit_bytes=LIMIT
            ),
            name=name,
        )(*operands)

    operands = (occ_energy, half_integrals, vir_coef.T, vir_energy)
    specs = [pl.BlockSpec(memory_space=pltpu.SMEM), pl.BlockSpec(memory_space=pl.ANY), vmem, vmem]
    make_scratch = [
        pltpu.VMEM(half_integrals.shape, half),
        pltpu.VMEM((2, virtuals, basis // 2), half),
        pltpu.VMEM((nq, 2, nq, 2 * width, tile), half),
        pltpu.VMEM((nq, 2, n * width, tile), half),
        pltpu.VMEM((n, width, tile), half),
        pltpu.VMEM((n * width, virtuals), half),
        dma, dma((2,)), dma, dma((n,)), dma((nz,)), dma((nz,)), dma((nz,)), dma((n,)), dma((n,)),
        dma((nq, nq)), dma((nq, nq)), dma((nq, nq)), dma((nq, nq)), dma((nq,)), dma((nq,)), dma((n,)), dma((n,)),
        dma((nq, n)), dma((nq, nz)), dma((nq, nz)), dma((nq, nz)),
    ]
    reduce_scratch = [
        room(nq, tile, virtuals), room(nq, tile, virtuals), room(nq, tile, virtuals),
        room(chunks, n, nq, rows, lanes), room(chunks, nz, 2, nq, rows, lanes),
        room(chunks, nz, nq, rows, lanes), room(chunks, nz, nq, rows, lanes), room(chunks, nz, nq, rows, lanes),
        room(chunks, nq, rows, lanes), room(chunks, nq, rows, lanes),
        dma((nq,)), dma((nq,)), dma((nq,)), dma((nq,)), dma((chunks,)), dma((chunks,)), dma((chunks,)), dma((chunks,)),
        dma((chunks, nz)), dma((chunks, nz)), dma((chunks, nq)), dma((chunks, nq)),
    ]
    sums = (nq, 2, tile, virtuals)
    groups = (n, nq, 2, rows, virtuals)
    finals = (result(tile, virtuals), result(tile, virtuals), result(rows, virtuals))
    if rows % 8 == 0:
        kernel = functools.partial(whole_kernel, n, nq, len(specs), len(finals), len(make_scratch))
        scratch = [room(*sums), room(*groups)] + make_scratch + reduce_scratch
        near, far, vir_rows = call(kernel, "densities", 0, specs, finals, scratch, operands)
    else:
        kernel = functools.partial(amplitude_kernel, n, nq)
        partials = (result(*sums), result(virtuals, virtuals))
        three, vir = call(kernel, "amplitude", 0, specs, partials, make_scratch, operands)
        kernel = functools.partial(reduce_kernel, n, nq)
        near, far, vir_rows = call(
            kernel, "reduce", 1, [vmem, vmem], finals, reduce_scratch, (three, vir.reshape(groups))
        )
    return (near + far)[:, None, :], vir_rows / (n * virtuals)


def solution(mesh):
    return jax.shard_map(
        per_device,
        mesh=mesh,
        in_specs=(P(None, "aux", None), P(None, "occ"), P(), P()),
        out_specs=(P("aux", "occ", None), P(("occ", "aux"), None)),
        check_vma=False,
    )
```

```python
import functools

import jax
import jax.numpy as jnp
from jax import lax
from jax.experimental import pallas as pl
from jax.experimental.pallas import tpu as pltpu
from jax.sharding import PartitionSpec as P

MESH = pl.DeviceIdType.MESH
F32 = jnp.float32
PIECES = 4
SPAN = 80.0
TINY = 1e-30
LIMIT = 56 * 1024 * 1024


def remote(src, dst, send, recv, target):
    return pltpu.make_async_remote_copy(
        src_ref=src, dst_ref=dst, send_sem=send, recv_sem=recv, device_id=target, device_id_type=MESH
    )


def nearest_first(z, k, count):
    near = jnp.minimum(z, count - 1 - z)
    step = (k + 1) // 2
    both = z + step * (2 * (k % 2) - 1)
    low = z < count - 1 - z
    return jnp.where(k <= 2 * near, both, jnp.where(low, k, count - 1 - k))


def greet(n, nq):
    o = lax.axis_index("occ")
    s = lax.axis_index("aux")
    q, c = s // 2, s % 2
    z, low = o // 2, o % 2
    nz = n // 2
    barrier = pltpu.get_barrier_semaphore()
    peers = [(2 * z + 1 - low, s), (o, 2 * q + 1 - c)]
    peers += [(o, 2 * ((q + d) % nq) + c) for d in range(1, nq)]
    peers += [(2 * ((z + d) % nz) + low, s) for d in range(1, nz)]
    for peer in peers:
        pl.semaphore_signal(barrier, inc=1, device_id=peer, device_id_type=MESH)
    return lambda: pl.semaphore_wait(barrier, len(peers))


def make_densities(
    n, nq, occ_e, half, coef, vir_e, three, vir,
    ints, full, own, held, gift, amps,
    i_sem, c_copy, o_copy, c_recv, c_up, c_down, c_side, cp_send, cp_recv,
    own_send, own_recv, fw_send, fw_recv, pr_send, pr_recv, g_send, g_recv,
    h_recv, h_up, h_down, h_side,
    vir_done=lambda: None,
):
    o = lax.axis_index("occ")
    s = lax.axis_index("aux")
    q, c = s // 2, s % 2
    z, low = o // 2, o % 2
    nz = n // 2
    width = amps.shape[0] // n
    part = coef.shape[0]
    cut = coef.shape[1] // 2
    virtuals = amps.shape[1]
    above, below, side = o + 2, o - 2, 2 * z + 1 - low
    partner = (o, 2 * q + 1 - c)
    entered = greet(n, nq)

    fetch = pltpu.make_async_copy(half, ints, i_sem)
    fetch.start()

    def span(index, size):
        return pl.ds(pl.multiple_of(index * size, size), size)

    def keep(h):
        return pltpu.make_async_copy(coef.at[:, h * cut : (h + 1) * cut], full.at[h, span(o, part)], c_copy.at[h])

    keep(0).start()
    keep(1).start()
    entered()

    def relay(chain, src, dst, up, down, across, recv, act):
        pl.when(jnp.logical_and(chain <= z, z < nz - 1))(lambda: act(remote(src, dst, up, recv, (above, s))))
        pl.when(jnp.logical_and(chain >= z, z > 0))(lambda: act(remote(src, dst, down, recv, (below, s))))
        act(remote(src, dst, across, recv, (side, s)))

    def start(copy):
        copy.start()

    def sent(copy):
        copy.wait_send()

    def coef_slot(block):
        return full.at[c, span(block, part)]

    def coef_relay(chain, src, act):
        block = 2 * chain + low
        relay(chain, src, coef_slot(block), c_up.at[chain], c_down.at[chain], c_side.at[chain], c_recv.at[block], act)

    def coef_across(block):
        return remote(coef_slot(block), coef_slot(block), cp_send.at[block], cp_recv.at[block], partner)

    def coef_arrived(block):
        remote(coef_slot(block), coef_slot(block), c_side.at[0], c_recv.at[block], (side, s)).wait_recv()
        coef_across(block).start()

    coef_relay(z, coef.at[:, span(c, cut)], start)
    three[...] = jnp.zeros_like(three)
    vir[...] = jnp.zeros_like(vir)
    row_e = vir_e[...].reshape(1, virtuals)
    here = lax.broadcasted_iota(jnp.int32, (width, virtuals), 0) + s * width
    there = lax.broadcasted_iota(jnp.int32, (width, virtuals), 1)
    col_e = jnp.sum(jnp.where(here == there, row_e, 0.0), axis=1, keepdims=True)

    @pl.loop(1, nz)
    def _(k):
        chain = nearest_first(z, k, nz)
        block = 2 * chain + low
        remote(coef_slot(block), coef_slot(block), c_side.at[0], c_recv.at[block], (side, s)).wait_recv()
        coef_relay(chain, coef_slot(block), start)
        coef_across(block).start()
        coef_arrived(2 * nearest_first(z, k - 1, nz) + 1 - low)

    coef_arrived(2 * nearest_first(z, nz - 1, nz) + 1 - low)

    @pl.loop(1, n)
    def _(d):
        block = (o + d) % n
        other = full.at[1 - c, span(block, part)]
        remote(other, other, cp_send.at[block], cp_recv.at[block], partner).wait_recv()

    keep(0).wait()
    keep(1).wait()
    fetch.wait()

    def transform(block, rows):
        contract = (((1,), (1,)), ((), ()))
        return sum(
            lax.dot_general(
                full[h, rows, :], ints[block, :, h * cut : (h + 1) * cut], contract, preferred_element_type=F32
            )
            for h in range(2)
        ).astype(jnp.bfloat16)

    order = list(range(1, nq)) + [0]

    def chunk(there, core, group):
        return own.at[there, core, group]

    def to_partner(r):
        ref = chunk(q, c, (q + r) % nq)
        return remote(ref, ref, pr_send.at[r], pr_recv.at[r], partner)

    def to_chip(d, r):
        ref = chunk(q, c, (q + r) % nq)
        return remote(ref, ref, own_send.at[d, r], own_recv.at[d, r], (o, 2 * ((q + d) % nq) + c))

    def onward(d, r, core):
        there = (q + nq - d) % nq
        ref = chunk(there, core, (there + r) % nq)
        return remote(ref, ref, fw_send.at[d, r], fw_recv.at[d, r], partner)

    def from_chip(d, r):
        there = (q + nq - d) % nq
        ref = chunk(there, c, (there + r) % nq)
        remote(ref, ref, own_send.at[d, r], own_recv.at[d, r], partner).wait_recv()
        onward(d, r, c).start()

    for r in order:
        group = (q + r) % nq
        own[q, c, group] = transform(o, span(group, 2 * width))
        for d in range(1, nq):
            to_chip(d, r).start()
        to_partner(r).start()

    def give(block, core):
        return remote(
            gift.at[block], held.at[q, core, span(block, width)], g_send.at[block], g_recv.at[block], partner
        )

    @pl.loop(1, n)
    def _(d):
        block = (o + d) % n
        gift[block] = transform(block, span(2 * q + 1 - c, width))
        give(block, c).start()
        held[q, c, span(block, width), :] = transform(block, span(s, width))

    def held_slot(d, block):
        return held.at[(q + nq - d) % nq, :, span(block, width)]

    def own_slot(d):
        return own.at[(q + nq - d) % nq, :, q, span(c, width)]

    def held_relay(d, chain, src, act):
        block = 2 * chain + low
        relay(
            chain, src, held_slot(d, block), h_up.at[d, chain], h_down.at[d, chain], h_side.at[d, chain],
            h_recv.at[d, block], act,
        )

    def arrived(block):
        for d in range(1, nq):
            ref = held_slot(d, block)
            remote(ref, ref, h_side.at[d, 0], h_recv.at[d, block], (side, s)).wait_recv()

    for d in range(1, nq):
        from_chip(d, d)
    for d in range(1, nq):
        onward(d, d, 1 - c).wait_recv()
        held_relay(d, z, own_slot(d), start)
    rest = [(d, r) for d in range(1, nq) for r in order if r != d]
    for d, r in rest:
        from_chip(d, r)
    for r in order:
        ref = chunk(q, 1 - c, (q + r) % nq)
        remote(ref, ref, pr_send.at[r], pr_recv.at[r], partner).wait_recv()

    @pl.loop(1, n)
    def _(d):
        give((o + d) % n, 1 - c).wait_recv()

    for d, r in rest:
        onward(d, r, 1 - c).wait_recv()
    mine = pltpu.make_async_copy(
        own.at[:, :, q, span(c, width)], held.at[:, :, span(o, width)], o_copy
    )
    mine.start()
    mine.wait()

    def absorb(block):
        rows = span(block, width)
        coulomb = sum(
            lax.dot_general(
                held[t // 2, t % 2, rows, :], own[t // 2, t % 2].reshape(virtuals, -1),
                (((1,), (1,)), ((), ())), preferred_element_type=F32,
            )
            for t in range(2 * nq)
        )
        denominator = occ_e[o] + occ_e[block] - col_e - row_e
        amps[rows, :] = (coulomb / denominator).astype(jnp.bfloat16)

    contract = (((0,), (0,)), ((), ()))
    piece = virtuals // 2 if len(vir.shape) > 2 else 256

    def add_vir(chain):
        rows = span(chain, 2 * width)

        @pl.loop(0, virtuals // piece)
        def _(t):
            new = lax.dot_general(
                amps[rows, span(t, piece)], amps[rows, :], contract, preferred_element_type=F32
            )
            where = span(t, vir.shape[0] * piece // virtuals)
            vir[where] += new.reshape((-1,) + vir.shape[1:])

    def add_three(chain):
        rows = span(chain, 2 * width)

        @pl.loop(0, 2 * nq)
        def _(t):
            three[t // 2, t % 2] += lax.dot_general(
                held[t // 2, t % 2, rows, :], amps[rows, :], contract, preferred_element_type=F32
            )

    def both(chain):
        absorb(2 * chain + low)
        arrived(2 * chain + 1 - low)
        absorb(2 * chain + 1 - low)

    @pl.loop(1, nz)
    def _(k):
        chain = nearest_first(z, k, nz)
        arrived(2 * chain + low)
        for d in range(1, nq):
            held_relay(d, chain, held_slot(d, 2 * chain + low), start)
        before = nearest_first(z, k - 1, nz)
        both(before)
        add_vir(before)
        add_three(before)

    last = nearest_first(z, nz - 1, nz)
    both(last)
    add_vir(last)
    vir_done()
    add_three(last)

    def finish():
        @pl.loop(0, nz)
        def _(chain):
            coef_relay(chain, coef_slot(2 * chain + low), sent)
            for d in range(1, nq):
                held_relay(d, chain, held_slot(d, 2 * chain + low), sent)

        @pl.loop(1, n)
        def _(d):
            block = (o + d) % n
            coef_across(block).wait_send()
            give(block, c).wait_send()

        for r in order:
            to_partner(r).wait_send()
            for d in range(1, nq):
                to_chip(d, r).wait_send()
                onward(d, r, c).wait_send()

    return finish


def reduction(
    n, nq, three, vir, near_out, far_out, vir_out,
    t_pair, t_out, t_far, v_pair, v_sum, v_side, v_line, v_chain, v_col, v_far,
    pair_send, pair_recv, t_send, t_recv, vp_send, vp_recv, x_send, x_recv, z_send, z_recv, y_send, y_recv,
):
    o = lax.axis_index("occ")
    s = lax.axis_index("aux")
    q, c = s // 2, s % 2
    z, low = o // 2, o % 2
    nz = n // 2
    chunks, chunk = v_pair.shape[0], v_pair.shape[-1]
    partner = (o, 2 * q + 1 - c)
    side = (2 * z + 1 - low, s)

    def cols(k):
        return pl.ds(k * chunk, chunk)

    def v_swap(k):
        return remote(vir.at[:, :, 1 - c, :, cols(k)], v_pair.at[k], vp_send.at[k], vp_recv.at[k], partner)

    def x_swap(k):
        return remote(v_sum.at[k, :, 1 - low], v_side.at[k], x_send.at[k], x_recv.at[k], side)

    def along(k, d):
        there = (z + d) % nz
        return remote(
            v_line.at[k, there], v_chain.at[k, d], z_send.at[k, d], z_recv.at[k, d], (2 * there + low, s)
        )

    def between(k, d):
        there = (q + d) % nq
        return remote(v_col.at[k, there], v_far.at[k, d], y_send.at[k, d], y_recv.at[k, d], (o, 2 * there + c))

    def swap(d):
        return remote(three.at[(q + d) % nq, 1 - c], t_pair.at[d], pair_send.at[d], pair_recv.at[d], partner)

    def spread(d):
        return remote(t_out.at[d], t_far.at[d], t_send.at[d], t_recv.at[d], (o, 2 * ((q + d) % nq) + c))

    order = list(range(1, nq)) + [0]

    def open_vir():
        for k in range(chunks):
            v_swap(k).start()

    def close():
        for d in order:
            swap(d).start()
        for k in range(chunks):
            v_swap(k).wait()
            v_sum[k] = (vir[:, :, c, :, cols(k)] + v_pair[k]).reshape(v_sum.shape[1:])
            x_swap(k).start()
        for d in order[:-1]:
            swap(d).wait()
            t_out[d] = three[(q + d) % nq, c] + t_pair[d]
            spread(d).start()
        for k in range(chunks):
            x_swap(k).wait()
            v_line[k] = v_sum[k, :, low] + v_side[k]
            for d in range(1, nz):
                along(k, d).start()
            if k == 0:
                swap(0).wait()
                near_out[...] = three[q, c] + t_pair[0]
        for k in range(chunks):
            held = v_line[k, z]
            for d in range(1, nz):
                along(k, d).wait()
                held += v_chain[k, d]
            v_col[k] = held
            for d in range(1, nq):
                between(k, d).start()
        for d in order[:-1]:
            spread(d).wait()
            far_out[...] = t_far[d] if d == 1 else far_out[...] + t_far[d]
        for k in range(chunks):
            rows = v_col[k, q]
            for d in range(1, nq):
                between(k, d).wait()
                rows += v_far[k, d]
            vir_out[:, cols(k)] = rows

    return open_vir, close


def amplitude_kernel(n, nq, *refs):
    make_densities(n, nq, *refs)()


def reduce_kernel(n, nq, *refs):
    greet(n, nq)()
    open_vir, close = reduction(n, nq, *refs)
    open_vir()
    close()


def whole_kernel(n, nq, inputs, outputs, count, *refs):
    operands, results, scratch = refs[:inputs], refs[inputs : inputs + outputs], refs[inputs + outputs :]
    three, vir, rest = scratch[0], scratch[1], scratch[2:]
    open_vir, close = reduction(n, nq, three, vir, *results, *rest[count:])
    finish = make_densities(n, nq, *operands, three, vir, *rest[:count], vir_done=open_vir)
    close()
    finish()


def paired_kernel(
    n, occ_e, half, coef, vir_e, three_out, vir_out,
    ints, raw, full, own, held, gift, cross, amps, base, vir,
    t_give, t_mine, t_got, n_give, n_got, near_sum, v_pair, v_line, v_col,
    t_code, t_scale, t_code_in, t_scale_in, x_code, x_scale, x_code_in, x_scale_in,
    z_code, z_scale, z_code_in, z_scale_in, y_code, y_scale, y_code_in, y_scale_in, energies, levels,
    e_sems, i_sem, keep_sem, o_sem, raw_sems, c_recv, c_up, c_down, c_side, c_jump, cp_sems,
    pn_sems, pf_sems, f_recv, f_send, z_fwd, x_fwd, y_send, g_sems,
    t_send, t_recv, ts_send, ts_recv, n_sems, vp_send, vp_recv, x_send, x_recv, z_send, z_recv, yv_send, yv_recv,
):
    o = lax.axis_index("occ")
    s = lax.axis_index("aux")
    q, c = s // 2, s % 2
    z, low = o // 2, o % 2
    nz = n // 2
    far = 1 - q
    part, basis = coef.shape
    tile = raw.shape[0]
    virtuals = full.shape[0]
    width = virtuals // 4
    pieces = c_recv.shape[1]
    piece = basis // (2 * pieces)
    above, below, side = o + 2, o - 2, 2 * z + 1 - low
    other = 2 * q + 1 - c
    partner = (o, other)
    opposite = (o, 2 * far + c)

    def span(index, size):
        return pl.ds(pl.multiple_of(index * size, size), size)

    def start(copy):
        copy.start()

    def sent(copy):
        copy.wait_send()

    def nearest(k):
        return nearest_first(z, k, nz)

    at_end = jnp.logical_or(z == 0, z == nz - 1)
    inner_order = [0] + list(range(2, nz)) + [1]
    end_order = [0, nz - 1] + list(range(1, nz - 1))
    order = [nearest(jnp.where(at_end, a, b)) for a, b in zip(end_order, inner_order)]

    barrier = pltpu.get_barrier_semaphore()
    peers = [partner, opposite, (o, 2 * far + 1 - c), (side, s), (side, other)]
    peers += [(2 * ((z + d) % nz) + low, t) for d in range(1, nz) for t in (s, other)]
    for peer in peers:
        pl.semaphore_signal(barrier, inc=1, device_id=peer, device_id_type=MESH)
    small = [pltpu.make_async_copy(occ_e, energies, e_sems.at[0]), pltpu.make_async_copy(vir_e, levels, e_sems.at[1])]
    fetch = pltpu.make_async_copy(half, ints, i_sem)
    fetch.start()
    keep = pltpu.make_async_copy(coef, full.at[span(o, part)], keep_sem)
    keep.start()
    for copy in small:
        copy.start()
    pl.semaphore_wait(barrier, len(peers))

    lend = remote(half.at[o], raw, raw_sems.at[0], raw_sems.at[1], opposite)

    def coef_slot(block, core, h):
        return full.at[span(block, part), pl.ds(pl.multiple_of((pieces * core + h) * piece, piece), piece)]

    def coef_relay(chain, src, dst, recv, act):
        pl.when(jnp.logical_and(jnp.logical_and(chain <= z, chain > z - 2), z < nz - 1))(
            lambda: act(remote(src, dst, c_up.at[z - chain], recv, (above, s)))
        )
        pl.when(jnp.logical_and(jnp.logical_and(chain >= z, chain < z + 2), z > 0))(
            lambda: act(remote(src, dst, c_down.at[chain - z], recv, (below, s)))
        )
        act(remote(src, dst, c_side.at[chain], recv, (side, s)))

    def coef_across(block, h, core):
        ref = coef_slot(block, core, h)
        return remote(ref, ref, cp_sems.at[0], cp_sems.at[1], partner)

    def coef_wait(block, h):
        ref = coef_slot(block, c, h)
        remote(ref, ref, c_side.at[0], c_recv.at[block, h], (side, s)).wait_recv()

    def coef_own(h):
        return coef.at[:, pl.ds(pl.multiple_of((pieces * c + h) * piece, piece), piece)]

    def coef_far(src, dst, recv, act):
        for d in range(3, nz):
            pl.when(z + d < nz)(
                lambda: act(remote(src, dst, c_jump.at[0, d - 3], recv, (o + 2 * d, s)))
            )
            pl.when(z >= d)(
                lambda: act(remote(src, dst, c_jump.at[1, d - 3], recv, (o - 2 * d, s)))
            )

    for h in range(pieces):
        coef_relay(z, coef_own(h), coef_slot(o, c, h), c_recv.at[o, h], start)
    for h in range(pieces):
        coef_far(coef_own(h), coef_slot(o, c, h), c_recv.at[o, h], start)
    lend.start()
    for copy in small:
        copy.wait()
    row_e = levels[...].reshape(1, virtuals)
    here = lax.broadcasted_iota(jnp.int32, (width, virtuals), 0) + s * width
    there = lax.broadcasted_iota(jnp.int32, (width, virtuals), 1)
    col_e = jnp.sum(jnp.where(here == there, row_e, 0.0), axis=1, keepdims=True)

    def each_at(d, act):
        pl.when(z + d < nz)(lambda: act(z + d))
        pl.when(z >= d)(lambda: act(z - d))

    def coef_beside(chain, h):
        block = 2 * chain + 1 - low
        coef_wait(block, h)
        coef_across(block, h, c).start()

    def coef_along(chain, h):
        block = 2 * chain + low
        slot = coef_slot(block, c, h)
        coef_wait(block, h)
        coef_relay(chain, slot, slot, c_recv.at[block, h], start)
        coef_across(block, h, c).start()

    for h in range(pieces):
        each_at(1, lambda chain: coef_along(chain, h))
    for h in range(pieces):
        coef_beside(z, h)
        for d in list(range(3, nz)) + [2]:
            each_at(d, lambda chain: coef_along(chain, h))
    for d in [1] + list(range(3, nz)) + [2]:
        for h in range(pieces):
            each_at(d, lambda chain: coef_beside(chain, h))

    def coef_halves(blocks):
        ref = full.at[: blocks * part, : basis // 2]
        return remote(ref, ref, cp_sems.at[0], cp_sems.at[1], partner)

    coef_halves(n - 1).wait_recv()

    keep.wait()
    fetch.wait()

    def transform(rows, source):
        return lax.dot_general(rows, source, (((1,), (1,)), ((), ())), preferred_element_type=F32).astype(jnp.bfloat16)

    def cols(group, core):
        return span(2 * group + core, tile)

    def lend_block(block, sem, act):
        for core in range(2):
            act(
                remote(
                    cross.at[block, pl.ds(core * width, width)], held.at[span(block, width), cols(q, c)],
                    y_send.at[sem], f_recv.at[block, 0], (o, 2 * far + core),
                )
            )

    def distant(chain):
        return jnp.abs(chain - z) > 2

    def cross_over(block, sem):
        cross[block] = transform(full[span(far, 2 * width), :], ints[block])
        lend_block(block, sem, start)

    @pl.loop(2, nz)
    def _(k):
        chain = nearest(jnp.where(at_end, nz + 1 - k, k))
        cross_over(2 * chain + 1 - low, 0)
        pl.when(distant(chain))(lambda: cross_over(2 * chain + low, jnp.where(at_end, nz - k, k - 1)))

    def own_part(group, core):
        return own.at[:, cols(group, core)]

    def near_part(core):
        ref = own_part(q, core)
        return remote(ref, ref, pn_sems.at[0], pn_sems.at[1], partner)

    def far_part(core):
        ref = own_part(far, core)
        return remote(ref, ref, pf_sems.at[0], pf_sems.at[1], partner)

    def hand_out(parts, act):
        for core, t, src, dst in parts:
            recv = f_recv.at[o, t]
            to = 2 * q + core
            pl.when(z < nz - 1)(lambda: act(remote(src, dst, f_send.at[0], recv, (above, to))))
            pl.when(z > 0)(lambda: act(remote(src, dst, f_send.at[1], recv, (below, to))))
            act(remote(src, dst, f_send.at[2], recv, (side, to)))

    part_rows = width // 2

    def outgoing(core, t):
        rows = pl.ds(pl.multiple_of((2 * q + core) * width + t * part_rows, part_rows), part_rows)
        return core, t, own.at[rows, cols(far, c)], held.at[span(2 * o + t, part_rows), cols(far, c)]

    lend.wait_recv()
    own[:, cols(far, c)] = transform(full[...], raw[...])
    hand_out([outgoing(core, t) for t in range(2) for core in range(2)], start)
    far_part(c).start()
    own[:, cols(q, c)] = transform(full[...], ints[o])
    near_part(c).start()

    def give(block, core):
        return remote(
            gift.at[block], held.at[span(block, width), cols(q, core)], g_sems.at[0], g_sems.at[1], partner
        )

    @pl.loop(1, n)
    def _(d):
        block = (o + d) % n
        rows = jnp.concatenate([full[span(s, width), :], full[span(other, width), :]], axis=0)
        both = transform(rows, ints[block])
        held[span(block, width), cols(q, c)] = both[:width]
        gift[block] = both[width:]
        give(block, c).start()

    def given():
        ref = gift.at[: n - 1]
        return remote(ref, ref, g_sems.at[0], g_sems.at[1], partner)

    far_part(1 - c).wait_recv()
    near_part(1 - c).wait_recv()
    mine = pltpu.make_async_copy(own.at[span(s, width)], held.at[span(o, width)], o_sem)
    mine.start()

    def far_piece(block, t):
        return held.at[span(2 * block + t, part_rows), span(far, 2 * tile)]

    def arrive(block):
        ref = held.at[span(block, width), span(far, 2 * tile)]
        remote(ref, ref, x_fwd, f_recv.at[block, 0], (side, s)).wait_recv()

    def arrive_pieces(block):
        for t in range(2):
            ref = far_piece(block, t)
            remote(ref, ref, x_fwd, f_recv.at[block, t], (side, s)).wait_recv()

    def pass_on(chain, ref, recv, act):
        pl.when(jnp.logical_and(chain < z, z < nz - 1))(lambda: act(remote(ref, ref, z_fwd.at[0], recv, (above, s))))
        pl.when(jnp.logical_and(chain > z, z > 0))(lambda: act(remote(ref, ref, z_fwd.at[1], recv, (below, s))))
        pl.when(chain == nearest(1))(lambda: act(remote(ref, ref, x_fwd, recv, (side, s))))

    def take(chain, t):
        block = 2 * chain + low
        ref = far_piece(block, t)
        remote(ref, ref, x_fwd, f_recv.at[block, t], (side, s)).wait_recv()
        pass_on(chain, ref, f_recv.at[block, t], start)

    for t in range(2):
        each_at(1, lambda chain: take(chain, t))
    given().wait_recv()
    mine.wait()

    def overlap(chain, group):
        where = span(group, 2 * tile)
        return lax.dot_general(
            held[span(chain, 2 * width), where], own[:, where], (((1,), (1,)), ((), ())), preferred_element_type=F32
        )

    def absorb(slot, chain):
        if slot:
            coulomb = base[slot - 1] + overlap(chain, far)
        else:
            coulomb = lax.dot_general(
                held[span(chain, 2 * width), :], own[...], (((1,), (1,)), ((), ())), preferred_element_type=F32
            )
        left = jnp.concatenate([energies[o] + energies[2 * chain + t] - col_e for t in range(2)], axis=0)
        amps[slot * 2 * width : (slot + 1) * 2 * width, :] = (coulomb / (left - row_e)).astype(jnp.bfloat16)

    contract = (((0,), (0,)), ((), ()))
    strips, strip = t_give.shape[0], t_give.shape[-1]
    rows = vir.shape[4]
    middle = virtuals // 2

    def wide(k):
        return pl.ds(k * strip, strip)

    early, late = range(nz // 2), range(nz // 2, nz)

    def amps_of(slots, where=slice(None)):
        return amps[slots[0] * 2 * width : (slots[-1] + 1) * 2 * width, where]

    def part_three(group, core, where, slots):
        rows = [held[span(order[i], 2 * width), cols(group, core)] for i in slots]
        return lax.dot_general(
            jnp.concatenate(rows, axis=0), amps_of(slots, where), contract, preferred_element_type=F32
        )

    def part_vir(half, slots):
        new = lax.dot_general(
            amps_of(slots, span(half, middle)), amps_of(slots), contract, preferred_element_type=F32
        )
        return new.reshape((nz // 2,) + vir.shape[1:])

    def admit(i):
        chain = order[i]
        pl.when(distant(chain))(lambda: arrive(2 * chain + low))
        pl.when(jnp.abs(chain - z) == 2)(lambda: arrive_pieces(2 * chain + low))
        passed = jnp.logical_or(chain == z, chain == nearest(1))
        pl.when(passed)(lambda: arrive_pieces(2 * chain + 1 - low))
        pl.when(jnp.logical_not(passed))(lambda: arrive(2 * chain + 1 - low))
        absorb(i, chain)

    admit(0)
    for i in range(1, nz):
        base[i - 1] = overlap(order[i], q)
    for i in early[1:]:
        admit(i)
    for half in range(2):
        vir[pl.ds(half * (nz // 2), nz // 2)] = part_vir(half, early)
    for k in range(strips):
        t_give[k] = part_three(far, 1 - c, wide(k), early)
        t_mine[k] = part_three(far, c, wide(k), early)
    for i in late:
        admit(i)

    def far_swap(k):
        return remote(t_give.at[k], t_got.at[k], t_send, t_recv.at[k], partner)

    def coded_copies(code, scale, code_to, scale_to, sems, target):
        return (
            remote(code, code_to, sems[0].at[0], sems[1].at[0], target),
            remote(scale, scale_to, sems[0].at[1], sems[1].at[1], target),
        )

    def far_send(k):
        sems = (ts_send, ts_recv.at[k])
        return coded_copies(t_code.at[k], t_scale.at[k], t_code_in.at[k], t_scale_in.at[k], sems, opposite)

    def x_swap(chain):
        sems = (x_send, x_recv.at[chain])
        return coded_copies(
            x_code.at[chain], x_scale.at[chain], x_code_in.at[chain], x_scale_in.at[chain], sems, (side, s)
        )

    def along(to, sender):
        sems = (z_send, z_recv.at[sender])
        return coded_copies(
            z_code.at[to], z_scale.at[to], z_code_in.at[sender], z_scale_in.at[sender], sems, (2 * to + low, s)
        )

    def both_start(copies):
        for copy in copies:
            copy.start()

    def both_recv(copies):
        for copy in copies:
            copy.wait_recv()

    def both_sent(copies):
        for copy in copies:
            copy.wait_send()

    def encode(value, code, scale):
        parts = scale.shape[0]
        size = value.shape[0] // parts
        grouped = value.reshape(parts, size, value.shape[1])
        top = jnp.maximum(jnp.max(jnp.abs(grouped), axis=1, keepdims=True), TINY)
        scale[...] = top
        code[...] = jnp.exp(grouped * (SPAN / top)).astype(jnp.bfloat16).reshape(value.shape)

    def decode(code, scale):
        parts = scale.shape[0]
        words = jnp.log(code[...].astype(F32)).reshape(parts, code.shape[0] // parts, code.shape[1])
        return (words * (scale[...] * (1.0 / SPAN))).reshape(code.shape)

    def v_swap(chain):
        return remote(vir.at[chain, :, :, 1 - c], v_pair.at[chain], vp_send, vp_recv.at[chain], partner)

    def between():
        return coded_copies(y_code, y_scale, y_code_in, y_scale_in, (yv_send, yv_recv), opposite)

    near_swap = remote(n_give, n_got, n_sems.at[0], n_sems.at[1], partner)
    first = jnp.where(z < nz // 2, 1, 0)
    for half in (first, 1 - first):
        where = pl.ds(half * (nz // 2), nz // 2)
        vir[where] = vir[where] + part_vir(half, late)
        for t in range(nz // 2):
            v_swap(half * (nz // 2) + t).start()

    def pair_sum(chain, across):
        return (vir[chain, across, :, c] + v_pair[chain, across]).reshape(2 * rows, virtuals)

    farthest = [nearest(k) for k in reversed(range(nz))]

    def add_pair(chain):
        v_swap(chain).wait_recv()
        encode(pair_sum(chain, 1 - low), x_code.at[chain], x_scale.at[chain])
        both_start(x_swap(chain))

    for k in range(max(strips, nz)):
        if k < strips:
            t_give[k] += part_three(far, 1 - c, wide(k), late)
            far_swap(k).start()
        if k < nz:
            add_pair(farthest[k])
    for k in range(strips):
        new = t_mine[k] + part_three(far, c, wide(k), late)
        far_swap(k).wait_recv()
        encode(new + t_got[k], t_code.at[k], t_scale.at[k])
        both_start(far_send(k))
    def add_beside(chain, last):
        both_recv(x_swap(chain))
        total = pair_sum(chain, low) + decode(x_code_in.at[chain], x_scale_in.at[chain])
        if last:
            v_line[...] = total
        else:
            encode(total, z_code.at[chain], z_scale.at[chain])
            both_start(along(chain, z))

    def near_give():
        n_give[...] = part_three(q, 1 - c, slice(None), range(nz))
        near_swap.start()

    def near_keep():
        near_sum[...] = part_three(q, c, slice(None), range(nz))

    fillers = [near_give, near_keep]
    for k in range(nz):
        add_beside(farthest[k], k == nz - 1)
        if k < len(fillers):
            fillers[k]()
    for filler in fillers[nz:]:
        filler()
    near_swap.wait_recv()
    near_sum[...] += n_got[...]
    for k in range(1, nz):
        sender = nearest(k)
        both_recv(along(sender, sender))
        v_line[...] += decode(z_code_in.at[sender], z_scale_in.at[sender])
    v_col[...] = v_line[...].reshape(v_col.shape)
    encode(v_col[far], y_code, y_scale)
    both_start(between())
    for k in range(strips):
        both_recv(far_send(k))
        near_sum[:, wide(k)] += decode(t_code_in.at[k], t_scale_in.at[k])
    three_out[...] = near_sum[...].reshape(three_out.shape)
    both_recv(between())
    vir_out[...] = (v_col[q] + decode(y_code_in, y_scale_in)) / (n * virtuals)

    lend.wait_send()

    half_block = full.at[:part, : basis // 2]

    @pl.loop(0, nz)
    def _(chain):
        coef_relay(chain, half_block, half_block, c_recv.at[0, 0], sent)

    coef_far(half_block, half_block, c_recv.at[0, 0], sent)
    coef_halves(n - 1).wait_send()
    given().wait_send()

    def lent(blocks, sem):
        ref = cross.at[:blocks]
        return remote(ref, ref, y_send.at[sem], f_recv.at[0, 0], opposite)

    if nz > 2:
        lent(nz - 2, 0).wait_send()
    for k in range(2, nz):
        pl.when(distant(nearest(k)))(lambda: lent(1, k - 1).wait_send())

    both_rows = own.at[: 2 * width, :tile]
    hand_out([(0, 0, both_rows, both_rows)], sent)
    far_part(c).wait_send()
    near_part(c).wait_send()
    block_ref = held.at[:width, : 2 * tile]
    each_at(1, lambda chain: pass_on(chain, block_ref, f_recv.at[0, 0], sent))
    near_swap.wait_send()
    remote(t_give, t_give, t_send, t_recv.at[0], partner).wait_send()
    both_sent(coded_copies(t_code, t_scale, t_code, t_scale, (ts_send, ts_recv.at[0]), opposite))
    whole = vir.at[:, :, :, 0]
    remote(whole, whole, vp_send, vp_recv.at[0], partner).wait_send()
    both_sent(coded_copies(x_code, x_scale, x_code, x_scale, (x_send, x_recv.at[0]), (side, s)))
    codes, scales = z_code.at[: nz - 1], z_scale.at[: nz - 1]
    both_sent(coded_copies(codes, scales, codes, scales, (z_send, z_recv.at[0]), (side, s)))
    both_sent(between())


def paired(n, half_integrals, coef, occ_energy, vir_energy):
    _, tile, basis = half_integrals.shape
    part = coef.shape[0]
    virtuals = part * n
    width, rows, nz = virtuals // 4, virtuals // (4 * n), n // 2
    pieces = PIECES if basis % (256 * PIECES) == 0 else 1
    vmem = pl.BlockSpec(memory_space=pltpu.VMEM)
    dma = pltpu.SemaphoreType.DMA
    lanes = 128
    chunks = virtuals // lanes
    strip = 2 * lanes if chunks % 2 == 0 else lanes
    strips = virtuals // strip

    def room(*shape):
        return pltpu.VMEM(shape, F32)

    def packed(*shape):
        return pltpu.VMEM(shape, jnp.bfloat16)

    scratch = [
        packed(n, tile, basis), packed(tile, basis), packed(virtuals, basis), packed(virtuals, 4 * tile),
        packed(n * width, 4 * tile), packed(n, width, tile), packed(n, 2 * width, tile), packed(n * width, virtuals),
        room(nz - 1, 2 * width, virtuals),
        room(nz, 2, 2, 2, rows, virtuals),
        room(strips, tile, strip), room(strips, tile, strip), room(strips, tile, strip), room(tile, virtuals), room(tile, virtuals),
        room(tile, virtuals), room(nz, 2, 2, rows, virtuals), room(2 * rows, virtuals), room(2, rows, virtuals),
    ]
    groups = tile // 64
    for _ in range(2):
        scratch += [packed(strips, tile, strip), room(strips, groups, 1, strip)]
    for _ in range(4):
        scratch += [packed(nz, 2 * rows, virtuals), room(nz, 1, 1, virtuals)]
    for _ in range(2):
        scratch += [packed(rows, virtuals), room(1, 1, virtuals)]
    scratch += [pltpu.SMEM((n,), F32), room(virtuals)]
    scratch += [
        dma((2,)), dma, dma, dma, dma((2,)), dma((n, pieces)), dma((2,)), dma((2,)), dma((nz,)), dma((2, max(nz - 3, 1))), dma((2,)),
        dma((2,)), dma((2,)), dma((n, 2)), dma((3,)), dma((2,)), dma, dma((nz,)), dma((2,)),
        dma, dma((strips,)), dma((2,)), dma((strips, 2)), dma((2,)), dma, dma((nz,)),
        dma((2,)), dma((nz, 2)), dma((2,)), dma((nz, 2)), dma((2,)), dma((2,)),
    ]
    return pl.pallas_call(
        functools.partial(paired_kernel, n),
        out_shape=(
            pltpu.VMEM((tile, 1, virtuals), F32), pltpu.VMEM((rows, virtuals), F32),
        ),
        in_specs=[pl.BlockSpec(memory_space=pl.ANY)] * 4,
        out_specs=(vmem, vmem),
        scratch_shapes=scratch,
        compiler_params=pltpu.CompilerParams(
            collective_id=0, has_side_effects=True, vmem_limit_bytes=LIMIT
        ),
        name="densities",
    )(occ_energy, half_integrals, coef, vir_energy)


def per_device(half_integrals, vir_coef, occ_energy, vir_energy):
    n, aux = lax.axis_size("occ"), lax.axis_size("aux")
    nz, nq = n // 2, aux // 2
    _, tile, basis = half_integrals.shape
    part = vir_coef.shape[1]
    virtuals = part * n
    if nq == 2 and n % 2 == 0 and nz > 1 and nz % 2 == 0 and virtuals % (32 * n) == 0 and virtuals % 256 == 0 and tile % 64 == 0:
        three, vir_rows = paired(n, half_integrals, vir_coef.T, occ_energy, vir_energy)
        return three, vir_rows
    width, rows = virtuals // aux, virtuals // (n * aux)
    vmem = pl.BlockSpec(memory_space=pltpu.VMEM)
    dma = pltpu.SemaphoreType.DMA
    half = jnp.bfloat16
    lanes = 128
    chunks = virtuals // lanes

    def room(*shape):
        return pltpu.VMEM(shape, F32)

    def result(*shape):
        return jax.ShapeDtypeStruct(shape, F32)

    def call(kernel, name, number, in_specs, out_shape, scratch, operands):
        return pl.pallas_call(
            kernel,
            out_shape=out_shape,
            in_specs=in_specs,
            out_specs=(vmem,) * len(out_shape),
            scratch_shapes=scratch,
            compiler_params=pltpu.CompilerParams(
                collective_id=number, has_side_effects=True, vmem_limit_bytes=LIMIT
            ),
            name=name,
        )(*operands)

    operands = (occ_energy, half_integrals, vir_coef.T, vir_energy)
    specs = [pl.BlockSpec(memory_space=pltpu.SMEM), pl.BlockSpec(memory_space=pl.ANY), vmem, vmem]
    make_scratch = [
        pltpu.VMEM(half_integrals.shape, half),
        pltpu.VMEM((2, virtuals, basis // 2), half),
        pltpu.VMEM((nq, 2, nq, 2 * width, tile), half),
        pltpu.VMEM((nq, 2, n * width, tile), half),
        pltpu.VMEM((n, width, tile), half),
        pltpu.VMEM((n * width, virtuals), half),
        dma, dma((2,)), dma, dma((n,)), dma((nz,)), dma((nz,)), dma((nz,)), dma((n,)), dma((n,)),
        dma((nq, nq)), dma((nq, nq)), dma((nq, nq)), dma((nq, nq)), dma((nq,)), dma((nq,)), dma((n,)), dma((n,)),
        dma((nq, n)), dma((nq, nz)), dma((nq, nz)), dma((nq, nz)),
    ]
    reduce_scratch = [
        room(nq, tile, virtuals), room(nq, tile, virtuals), room(nq, tile, virtuals),
        room(chunks, n, nq, rows, lanes), room(chunks, nz, 2, nq, rows, lanes),
        room(chunks, nz, nq, rows, lanes), room(chunks, nz, nq, rows, lanes), room(chunks, nz, nq, rows, lanes),
        room(chunks, nq, rows, lanes), room(chunks, nq, rows, lanes),
        dma((nq,)), dma((nq,)), dma((nq,)), dma((nq,)), dma((chunks,)), dma((chunks,)), dma((chunks,)), dma((chunks,)),
        dma((chunks, nz)), dma((chunks, nz)), dma((chunks, nq)), dma((chunks, nq)),
    ]
    sums = (nq, 2, tile, virtuals)
    groups = (n, nq, 2, rows, virtuals)
    finals = (result(tile, virtuals), result(tile, virtuals), result(rows, virtuals))
    if rows % 8 == 0:
        kernel = functools.partial(whole_kernel, n, nq, len(specs), len(finals), len(make_scratch))
        scratch = [room(*sums), room(*groups)] + make_scratch + reduce_scratch
        near, far, vir_rows = call(kernel, "densities", 0, specs, finals, scratch, operands)
    else:
        kernel = functools.partial(amplitude_kernel, n, nq)
        partials = (result(*sums), result(virtuals, virtuals))
        three, vir = call(kernel, "amplitude", 0, specs, partials, make_scratch, operands)
        kernel = functools.partial(reduce_kernel, n, nq)
        near, far, vir_rows = call(
            kernel, "reduce", 1, [vmem, vmem], finals, reduce_scratch, (three, vir.reshape(groups))
        )
    return (near + far)[:, None, :], vir_rows / (n * virtuals)


def solution(mesh):
    return jax.shard_map(
        per_device,
        mesh=mesh,
        in_specs=(P(None, "aux", None), P(None, "occ"), P(), P()),
        out_specs=(P("aux", "occ", None), P(("occ", "aux"), None)),
        check_vma=False,
    )
```

```python
import functools

import jax
import jax.numpy as jnp
from jax import lax
from jax.experimental import pallas as pl
from jax.experimental.pallas import tpu as pltpu
from jax.sharding import PartitionSpec as P

MESH = pl.DeviceIdType.MESH
F32 = jnp.float32
PIECES = 4
SPAN = 80.0
TINY = 1e-30
LIMIT = 56 * 1024 * 1024


def remote(src, dst, send, recv, target):
    return pltpu.make_async_remote_copy(
        src_ref=src, dst_ref=dst, send_sem=send, recv_sem=recv, device_id=target, device_id_type=MESH
    )


def nearest_first(z, k, count):
    near = jnp.minimum(z, count - 1 - z)
    step = (k + 1) // 2
    both = z + step * (2 * (k % 2) - 1)
    low = z < count - 1 - z
    return jnp.where(k <= 2 * near, both, jnp.where(low, k, count - 1 - k))


def greet(n, nq):
    o = lax.axis_index("occ")
    s = lax.axis_index("aux")
    q, c = s // 2, s % 2
    z, low = o // 2, o % 2
    nz = n // 2
    barrier = pltpu.get_barrier_semaphore()
    peers = [(2 * z + 1 - low, s), (o, 2 * q + 1 - c)]
    peers += [(o, 2 * ((q + d) % nq) + c) for d in range(1, nq)]
    peers += [(2 * ((z + d) % nz) + low, s) for d in range(1, nz)]
    for peer in peers:
        pl.semaphore_signal(barrier, inc=1, device_id=peer, device_id_type=MESH)
    return lambda: pl.semaphore_wait(barrier, len(peers))


def make_densities(
    n, nq, occ_e, half, coef, vir_e, three, vir,
    ints, full, own, held, gift, amps,
    i_sem, c_copy, o_copy, c_recv, c_up, c_down, c_side, cp_send, cp_recv,
    own_send, own_recv, fw_send, fw_recv, pr_send, pr_recv, g_send, g_recv,
    h_recv, h_up, h_down, h_side,
    vir_done=lambda: None,
):
    o = lax.axis_index("occ")
    s = lax.axis_index("aux")
    q, c = s // 2, s % 2
    z, low = o // 2, o % 2
    nz = n // 2
    width = amps.shape[0] // n
    part = coef.shape[0]
    cut = coef.shape[1] // 2
    virtuals = amps.shape[1]
    above, below, side = o + 2, o - 2, 2 * z + 1 - low
    partner = (o, 2 * q + 1 - c)
    entered = greet(n, nq)

    fetch = pltpu.make_async_copy(half, ints, i_sem)
    fetch.start()

    def span(index, size):
        return pl.ds(pl.multiple_of(index * size, size), size)

    def keep(h):
        return pltpu.make_async_copy(coef.at[:, h * cut : (h + 1) * cut], full.at[h, span(o, part)], c_copy.at[h])

    keep(0).start()
    keep(1).start()
    entered()

    def relay(chain, src, dst, up, down, across, recv, act):
        pl.when(jnp.logical_and(chain <= z, z < nz - 1))(lambda: act(remote(src, dst, up, recv, (above, s))))
        pl.when(jnp.logical_and(chain >= z, z > 0))(lambda: act(remote(src, dst, down, recv, (below, s))))
        act(remote(src, dst, across, recv, (side, s)))

    def start(copy):
        copy.start()

    def sent(copy):
        copy.wait_send()

    def coef_slot(block):
        return full.at[c, span(block, part)]

    def coef_relay(chain, src, act):
        block = 2 * chain + low
        relay(chain, src, coef_slot(block), c_up.at[chain], c_down.at[chain], c_side.at[chain], c_recv.at[block], act)

    def coef_across(block):
        return remote(coef_slot(block), coef_slot(block), cp_send.at[block], cp_recv.at[block], partner)

    def coef_arrived(block):
        remote(coef_slot(block), coef_slot(block), c_side.at[0], c_recv.at[block], (side, s)).wait_recv()
        coef_across(block).start()

    coef_relay(z, coef.at[:, span(c, cut)], start)
    three[...] = jnp.zeros_like(three)
    vir[...] = jnp.zeros_like(vir)
    row_e = vir_e[...].reshape(1, virtuals)
    here = lax.broadcasted_iota(jnp.int32, (width, virtuals), 0) + s * width
    there = lax.broadcasted_iota(jnp.int32, (width, virtuals), 1)
    col_e = jnp.sum(jnp.where(here == there, row_e, 0.0), axis=1, keepdims=True)

    @pl.loop(1, nz)
    def _(k):
        chain = nearest_first(z, k, nz)
        block = 2 * chain + low
        remote(coef_slot(block), coef_slot(block), c_side.at[0], c_recv.at[block], (side, s)).wait_recv()
        coef_relay(chain, coef_slot(block), start)
        coef_across(block).start()
        coef_arrived(2 * nearest_first(z, k - 1, nz) + 1 - low)

    coef_arrived(2 * nearest_first(z, nz - 1, nz) + 1 - low)

    @pl.loop(1, n)
    def _(d):
        block = (o + d) % n
        other = full.at[1 - c, span(block, part)]
        remote(other, other, cp_send.at[block], cp_recv.at[block], partner).wait_recv()

    keep(0).wait()
    keep(1).wait()
    fetch.wait()

    def transform(block, rows):
        contract = (((1,), (1,)), ((), ()))
        return sum(
            lax.dot_general(
                full[h, rows, :], ints[block, :, h * cut : (h + 1) * cut], contract, preferred_element_type=F32
            )
            for h in range(2)
        ).astype(jnp.bfloat16)

    order = list(range(1, nq)) + [0]

    def chunk(there, core, group):
        return own.at[there, core, group]

    def to_partner(r):
        ref = chunk(q, c, (q + r) % nq)
        return remote(ref, ref, pr_send.at[r], pr_recv.at[r], partner)

    def to_chip(d, r):
        ref = chunk(q, c, (q + r) % nq)
        return remote(ref, ref, own_send.at[d, r], own_recv.at[d, r], (o, 2 * ((q + d) % nq) + c))

    def onward(d, r, core):
        there = (q + nq - d) % nq
        ref = chunk(there, core, (there + r) % nq)
        return remote(ref, ref, fw_send.at[d, r], fw_recv.at[d, r], partner)

    def from_chip(d, r):
        there = (q + nq - d) % nq
        ref = chunk(there, c, (there + r) % nq)
        remote(ref, ref, own_send.at[d, r], own_recv.at[d, r], partner).wait_recv()
        onward(d, r, c).start()

    for r in order:
        group = (q + r) % nq
        own[q, c, group] = transform(o, span(group, 2 * width))
        for d in range(1, nq):
            to_chip(d, r).start()
        to_partner(r).start()

    def give(block, core):
        return remote(
            gift.at[block], held.at[q, core, span(block, width)], g_send.at[block], g_recv.at[block], partner
        )

    @pl.loop(1, n)
    def _(d):
        block = (o + d) % n
        gift[block] = transform(block, span(2 * q + 1 - c, width))
        give(block, c).start()
        held[q, c, span(block, width), :] = transform(block, span(s, width))

    def held_slot(d, block):
        return held.at[(q + nq - d) % nq, :, span(block, width)]

    def own_slot(d):
        return own.at[(q + nq - d) % nq, :, q, span(c, width)]

    def held_relay(d, chain, src, act):
        block = 2 * chain + low
        relay(
            chain, src, held_slot(d, block), h_up.at[d, chain], h_down.at[d, chain], h_side.at[d, chain],
            h_recv.at[d, block], act,
        )

    def arrived(block):
        for d in range(1, nq):
            ref = held_slot(d, block)
            remote(ref, ref, h_side.at[d, 0], h_recv.at[d, block], (side, s)).wait_recv()

    for d in range(1, nq):
        from_chip(d, d)
    for d in range(1, nq):
        onward(d, d, 1 - c).wait_recv()
        held_relay(d, z, own_slot(d), start)
    rest = [(d, r) for d in range(1, nq) for r in order if r != d]
    for d, r in rest:
        from_chip(d, r)
    for r in order:
        ref = chunk(q, 1 - c, (q + r) % nq)
        remote(ref, ref, pr_send.at[r], pr_recv.at[r], partner).wait_recv()

    @pl.loop(1, n)
    def _(d):
        give((o + d) % n, 1 - c).wait_recv()

    for d, r in rest:
        onward(d, r, 1 - c).wait_recv()
    mine = pltpu.make_async_copy(
        own.at[:, :, q, span(c, width)], held.at[:, :, span(o, width)], o_copy
    )
    mine.start()
    mine.wait()

    def absorb(block):
        rows = span(block, width)
        coulomb = sum(
            lax.dot_general(
                held[t // 2, t % 2, rows, :], own[t // 2, t % 2].reshape(virtuals, -1),
                (((1,), (1,)), ((), ())), preferred_element_type=F32,
            )
            for t in range(2 * nq)
        )
        denominator = occ_e[o] + occ_e[block] - col_e - row_e
        amps[rows, :] = (coulomb / denominator).astype(jnp.bfloat16)

    contract = (((0,), (0,)), ((), ()))
    piece = virtuals // 2 if len(vir.shape) > 2 else 256

    def add_vir(chain):
        rows = span(chain, 2 * width)

        @pl.loop(0, virtuals // piece)
        def _(t):
            new = lax.dot_general(
                amps[rows, span(t, piece)], amps[rows, :], contract, preferred_element_type=F32
            )
            where = span(t, vir.shape[0] * piece // virtuals)
            vir[where] += new.reshape((-1,) + vir.shape[1:])

    def add_three(chain):
        rows = span(chain, 2 * width)

        @pl.loop(0, 2 * nq)
        def _(t):
            three[t // 2, t % 2] += lax.dot_general(
                held[t // 2, t % 2, rows, :], amps[rows, :], contract, preferred_element_type=F32
            )

    def both(chain):
        absorb(2 * chain + low)
        arrived(2 * chain + 1 - low)
        absorb(2 * chain + 1 - low)

    @pl.loop(1, nz)
    def _(k):
        chain = nearest_first(z, k, nz)
        arrived(2 * chain + low)
        for d in range(1, nq):
            held_relay(d, chain, held_slot(d, 2 * chain + low), start)
        before = nearest_first(z, k - 1, nz)
        both(before)
        add_vir(before)
        add_three(before)

    last = nearest_first(z, nz - 1, nz)
    both(last)
    add_vir(last)
    vir_done()
    add_three(last)

    def finish():
        @pl.loop(0, nz)
        def _(chain):
            coef_relay(chain, coef_slot(2 * chain + low), sent)
            for d in range(1, nq):
                held_relay(d, chain, held_slot(d, 2 * chain + low), sent)

        @pl.loop(1, n)
        def _(d):
            block = (o + d) % n
            coef_across(block).wait_send()
            give(block, c).wait_send()

        for r in order:
            to_partner(r).wait_send()
            for d in range(1, nq):
                to_chip(d, r).wait_send()
                onward(d, r, c).wait_send()

    return finish


def reduction(
    n, nq, three, vir, near_out, far_out, vir_out,
    t_pair, t_out, t_far, v_pair, v_sum, v_side, v_line, v_chain, v_col, v_far,
    pair_send, pair_recv, t_send, t_recv, vp_send, vp_recv, x_send, x_recv, z_send, z_recv, y_send, y_recv,
):
    o = lax.axis_index("occ")
    s = lax.axis_index("aux")
    q, c = s // 2, s % 2
    z, low = o // 2, o % 2
    nz = n // 2
    chunks, chunk = v_pair.shape[0], v_pair.shape[-1]
    partner = (o, 2 * q + 1 - c)
    side = (2 * z + 1 - low, s)

    def cols(k):
        return pl.ds(k * chunk, chunk)

    def v_swap(k):
        return remote(vir.at[:, :, 1 - c, :, cols(k)], v_pair.at[k], vp_send.at[k], vp_recv.at[k], partner)

    def x_swap(k):
        return remote(v_sum.at[k, :, 1 - low], v_side.at[k], x_send.at[k], x_recv.at[k], side)

    def along(k, d):
        there = (z + d) % nz
        return remote(
            v_line.at[k, there], v_chain.at[k, d], z_send.at[k, d], z_recv.at[k, d], (2 * there + low, s)
        )

    def between(k, d):
        there = (q + d) % nq
        return remote(v_col.at[k, there], v_far.at[k, d], y_send.at[k, d], y_recv.at[k, d], (o, 2 * there + c))

    def swap(d):
        return remote(three.at[(q + d) % nq, 1 - c], t_pair.at[d], pair_send.at[d], pair_recv.at[d], partner)

    def spread(d):
        return remote(t_out.at[d], t_far.at[d], t_send.at[d], t_recv.at[d], (o, 2 * ((q + d) % nq) + c))

    order = list(range(1, nq)) + [0]

    def open_vir():
        for k in range(chunks):
            v_swap(k).start()

    def close():
        for d in order:
            swap(d).start()
        for k in range(chunks):
            v_swap(k).wait()
            v_sum[k] = (vir[:, :, c, :, cols(k)] + v_pair[k]).reshape(v_sum.shape[1:])
            x_swap(k).start()
        for d in order[:-1]:
            swap(d).wait()
            t_out[d] = three[(q + d) % nq, c] + t_pair[d]
            spread(d).start()
        for k in range(chunks):
            x_swap(k).wait()
            v_line[k] = v_sum[k, :, low] + v_side[k]
            for d in range(1, nz):
                along(k, d).start()
            if k == 0:
                swap(0).wait()
                near_out[...] = three[q, c] + t_pair[0]
        for k in range(chunks):
            held = v_line[k, z]
            for d in range(1, nz):
                along(k, d).wait()
                held += v_chain[k, d]
            v_col[k] = held
            for d in range(1, nq):
                between(k, d).start()
        for d in order[:-1]:
            spread(d).wait()
            far_out[...] = t_far[d] if d == 1 else far_out[...] + t_far[d]
        for k in range(chunks):
            rows = v_col[k, q]
            for d in range(1, nq):
                between(k, d).wait()
                rows += v_far[k, d]
            vir_out[:, cols(k)] = rows

    return open_vir, close


def amplitude_kernel(n, nq, *refs):
    make_densities(n, nq, *refs)()


def reduce_kernel(n, nq, *refs):
    greet(n, nq)()
    open_vir, close = reduction(n, nq, *refs)
    open_vir()
    close()


def whole_kernel(n, nq, inputs, outputs, count, *refs):
    operands, results, scratch = refs[:inputs], refs[inputs : inputs + outputs], refs[inputs + outputs :]
    three, vir, rest = scratch[0], scratch[1], scratch[2:]
    open_vir, close = reduction(n, nq, three, vir, *results, *rest[count:])
    finish = make_densities(n, nq, *operands, three, vir, *rest[:count], vir_done=open_vir)
    close()
    finish()


def paired_kernel(
    n, occ_e, half, coef, vir_e, three_out, vir_out,
    ints, raw, full, own, held, gift, cross, amps, base, vir,
    t_give, t_mine, t_got, n_give, n_got, near_sum, v_pair, v_line, v_col,
    t_code, t_scale, t_code_in, t_scale_in, x_code, x_scale, x_code_in, x_scale_in,
    z_code, z_scale, z_code_in, z_scale_in, y_code, y_scale, y_code_in, y_scale_in, energies, levels,
    e_sems, i_sem, keep_sem, o_sem, raw_sems, c_recv, c_up, c_down, c_side, c_jump, cp_sems,
    pn_sems, pf_sems, f_recv, f_send, z_fwd, x_fwd, y_send, g_sems,
    t_send, ts_send, n_sems, vp_send, x_send, z_send, z_recv, yv_send, yv_recv,
):
    o = lax.axis_index("occ")
    s = lax.axis_index("aux")
    q, c = s // 2, s % 2
    z, low = o // 2, o % 2
    nz = n // 2
    far = 1 - q
    part, basis = coef.shape
    tile = raw.shape[0]
    virtuals = full.shape[0]
    width = virtuals // 4
    pieces = c_recv.shape[1]
    piece = basis // (2 * pieces)
    above, below, side = o + 2, o - 2, 2 * z + 1 - low
    other = 2 * q + 1 - c
    partner = (o, other)
    opposite = (o, 2 * far + c)

    def span(index, size):
        return pl.ds(pl.multiple_of(index * size, size), size)

    def start(copy):
        copy.start()

    def sent(copy):
        copy.wait_send()

    def nearest(k):
        return nearest_first(z, k, nz)

    at_end = jnp.logical_or(z == 0, z == nz - 1)
    inner_order = [0] + list(range(2, nz)) + [1]
    end_order = [0, nz - 1] + list(range(1, nz - 1))
    order = [nearest(jnp.where(at_end, a, b)) for a, b in zip(end_order, inner_order)]

    barrier = pltpu.get_barrier_semaphore()
    peers = [partner, opposite, (o, 2 * far + 1 - c), (side, s), (side, other)]
    peers += [(2 * ((z + d) % nz) + low, t) for d in range(1, nz) for t in (s, other)]
    for peer in peers:
        pl.semaphore_signal(barrier, inc=1, device_id=peer, device_id_type=MESH)
    small = [pltpu.make_async_copy(occ_e, energies, e_sems.at[0]), pltpu.make_async_copy(vir_e, levels, e_sems.at[1])]
    fetch = pltpu.make_async_copy(half, ints, i_sem)
    fetch.start()
    keep = pltpu.make_async_copy(coef, full.at[span(o, part)], keep_sem)
    keep.start()
    for copy in small:
        copy.start()
    pl.semaphore_wait(barrier, len(peers))

    lend = remote(half.at[o], raw, raw_sems.at[0], raw_sems.at[1], opposite)

    def coef_slot(block, core, h):
        return full.at[span(block, part), pl.ds(pl.multiple_of((pieces * core + h) * piece, piece), piece)]

    def coef_relay(chain, src, dst, recv, act):
        pl.when(jnp.logical_and(jnp.logical_and(chain <= z, chain > z - 2), z < nz - 1))(
            lambda: act(remote(src, dst, c_up.at[z - chain], recv, (above, s)))
        )
        pl.when(jnp.logical_and(jnp.logical_and(chain >= z, chain < z + 2), z > 0))(
            lambda: act(remote(src, dst, c_down.at[chain - z], recv, (below, s)))
        )
        act(remote(src, dst, c_side.at[chain], recv, (side, s)))

    def coef_across(block, h, core):
        ref = coef_slot(block, core, h)
        return remote(ref, ref, cp_sems.at[0], cp_sems.at[1], partner)

    def coef_wait(block, h):
        ref = coef_slot(block, c, h)
        remote(ref, ref, c_side.at[0], c_recv.at[block, h], (side, s)).wait_recv()

    def coef_own(h):
        return coef.at[:, pl.ds(pl.multiple_of((pieces * c + h) * piece, piece), piece)]

    def coef_far(src, dst, recv, act):
        for d in range(3, nz):
            pl.when(z + d < nz)(
                lambda: act(remote(src, dst, c_jump.at[0, d - 3], recv, (o + 2 * d, s)))
            )
            pl.when(z >= d)(
                lambda: act(remote(src, dst, c_jump.at[1, d - 3], recv, (o - 2 * d, s)))
            )

    for h in range(pieces):
        coef_relay(z, coef_own(h), coef_slot(o, c, h), c_recv.at[o, h], start)
    for h in range(pieces):
        coef_far(coef_own(h), coef_slot(o, c, h), c_recv.at[o, h], start)
    lend.start()
    for copy in small:
        copy.wait()
    row_e = levels[...].reshape(1, virtuals)
    here = lax.broadcasted_iota(jnp.int32, (width, virtuals), 0) + s * width
    there = lax.broadcasted_iota(jnp.int32, (width, virtuals), 1)
    col_e = jnp.sum(jnp.where(here == there, row_e, 0.0), axis=1, keepdims=True)

    def each_at(d, act):
        pl.when(z + d < nz)(lambda: act(z + d))
        pl.when(z >= d)(lambda: act(z - d))

    def coef_beside(chain, h):
        block = 2 * chain + 1 - low
        coef_wait(block, h)
        coef_across(block, h, c).start()

    def coef_along(chain, h):
        block = 2 * chain + low
        slot = coef_slot(block, c, h)
        coef_wait(block, h)
        coef_relay(chain, slot, slot, c_recv.at[block, h], start)
        coef_across(block, h, c).start()

    for h in range(pieces):
        each_at(1, lambda chain: coef_along(chain, h))
    for h in range(pieces):
        coef_beside(z, h)
        for d in list(range(3, nz)) + [2]:
            each_at(d, lambda chain: coef_along(chain, h))
    for d in [1] + list(range(3, nz)) + [2]:
        for h in range(pieces):
            each_at(d, lambda chain: coef_beside(chain, h))

    def coef_halves(blocks):
        ref = full.at[: blocks * part, : basis // 2]
        return remote(ref, ref, cp_sems.at[0], cp_sems.at[1], partner)

    coef_halves(n - 1).wait_recv()

    keep.wait()
    fetch.wait()

    def transform(rows, source):
        return lax.dot_general(rows, source, (((1,), (1,)), ((), ())), preferred_element_type=F32).astype(jnp.bfloat16)

    def cols(group, core):
        return span(2 * group + core, tile)

    def lend_block(block, sem, act):
        for core in range(2):
            act(
                remote(
                    cross.at[block, pl.ds(core * width, width)], held.at[span(block, width), cols(q, c)],
                    y_send.at[sem], f_recv.at[block, 0], (o, 2 * far + core),
                )
            )

    def distant(chain):
        return jnp.abs(chain - z) > 2

    def cross_over(block, sem):
        cross[block] = transform(full[span(far, 2 * width), :], ints[block])
        lend_block(block, sem, start)

    @pl.loop(2, nz)
    def _(k):
        chain = nearest(jnp.where(at_end, nz + 1 - k, k))
        cross_over(2 * chain + 1 - low, 0)
        pl.when(distant(chain))(lambda: cross_over(2 * chain + low, jnp.where(at_end, nz - k, k - 1)))

    def own_part(group, core):
        return own.at[:, cols(group, core)]

    def near_part(core):
        ref = own_part(q, core)
        return remote(ref, ref, pn_sems.at[0], pn_sems.at[1], partner)

    def far_part(core):
        ref = own_part(far, core)
        return remote(ref, ref, pf_sems.at[0], pf_sems.at[1], partner)

    def hand_out(parts, act):
        for core, t, src, dst in parts:
            recv = f_recv.at[o, t]
            to = 2 * q + core
            pl.when(z < nz - 1)(lambda: act(remote(src, dst, f_send.at[0], recv, (above, to))))
            pl.when(z > 0)(lambda: act(remote(src, dst, f_send.at[1], recv, (below, to))))
            act(remote(src, dst, f_send.at[2], recv, (side, to)))

    part_rows = width // 2

    def outgoing(core, t):
        rows = pl.ds(pl.multiple_of((2 * q + core) * width + t * part_rows, part_rows), part_rows)
        return core, t, own.at[rows, cols(far, c)], held.at[span(2 * o + t, part_rows), cols(far, c)]

    lend.wait_recv()
    own[:, cols(far, c)] = transform(full[...], raw[...])
    hand_out([outgoing(core, t) for t in range(2) for core in range(2)], start)
    far_part(c).start()
    own[:, cols(q, c)] = transform(full[...], ints[o])
    near_part(c).start()

    def give(block, core):
        return remote(
            gift.at[block], held.at[span(block, width), cols(q, core)], g_sems.at[0], g_sems.at[1], partner
        )

    @pl.loop(1, n)
    def _(d):
        block = (o + d) % n
        rows = jnp.concatenate([full[span(s, width), :], full[span(other, width), :]], axis=0)
        both = transform(rows, ints[block])
        held[span(block, width), cols(q, c)] = both[:width]
        gift[block] = both[width:]
        give(block, c).start()

    def given():
        ref = gift.at[: n - 1]
        return remote(ref, ref, g_sems.at[0], g_sems.at[1], partner)

    far_part(1 - c).wait_recv()
    near_part(1 - c).wait_recv()
    mine = pltpu.make_async_copy(own.at[span(s, width)], held.at[span(o, width)], o_sem)
    mine.start()

    def far_piece(block, t):
        return held.at[span(2 * block + t, part_rows), span(far, 2 * tile)]

    def arrive(block):
        ref = held.at[span(block, width), span(far, 2 * tile)]
        remote(ref, ref, x_fwd, f_recv.at[block, 0], (side, s)).wait_recv()

    def arrive_pieces(block):
        for t in range(2):
            ref = far_piece(block, t)
            remote(ref, ref, x_fwd, f_recv.at[block, t], (side, s)).wait_recv()

    def pass_on(chain, ref, recv, act):
        pl.when(jnp.logical_and(chain < z, z < nz - 1))(lambda: act(remote(ref, ref, z_fwd.at[0], recv, (above, s))))
        pl.when(jnp.logical_and(chain > z, z > 0))(lambda: act(remote(ref, ref, z_fwd.at[1], recv, (below, s))))
        pl.when(chain == nearest(1))(lambda: act(remote(ref, ref, x_fwd, recv, (side, s))))

    def take(chain, t):
        block = 2 * chain + low
        ref = far_piece(block, t)
        remote(ref, ref, x_fwd, f_recv.at[block, t], (side, s)).wait_recv()
        pass_on(chain, ref, f_recv.at[block, t], start)

    for t in range(2):
        each_at(1, lambda chain: take(chain, t))
    given().wait_recv()
    mine.wait()

    def overlap(chain, group):
        where = span(group, 2 * tile)
        return lax.dot_general(
            held[span(chain, 2 * width), where], own[:, where], (((1,), (1,)), ((), ())), preferred_element_type=F32
        )

    def absorb(slot, chain):
        if slot:
            coulomb = base[slot - 1] + overlap(chain, far)
        else:
            coulomb = lax.dot_general(
                held[span(chain, 2 * width), :], own[...], (((1,), (1,)), ((), ())), preferred_element_type=F32
            )
        left = jnp.concatenate([energies[o] + energies[2 * chain + t] - col_e for t in range(2)], axis=0)
        amps[slot * 2 * width : (slot + 1) * 2 * width, :] = (coulomb / (left - row_e)).astype(jnp.bfloat16)

    contract = (((0,), (0,)), ((), ()))
    strips, strip = t_give.shape[0], t_give.shape[-1]
    rows = vir.shape[4]
    middle = virtuals // 2

    def wide(k):
        return pl.ds(k * strip, strip)

    early, late = range(nz // 2), range(nz // 2, nz)

    def amps_of(slots, where=slice(None)):
        return amps[slots[0] * 2 * width : (slots[-1] + 1) * 2 * width, where]

    def part_three(group, core, where, slots):
        rows = [held[span(order[i], 2 * width), cols(group, core)] for i in slots]
        return lax.dot_general(
            jnp.concatenate(rows, axis=0), amps_of(slots, where), contract, preferred_element_type=F32
        )

    def part_vir(half, slots):
        new = lax.dot_general(
            amps_of(slots, span(half, middle)), amps_of(slots), contract, preferred_element_type=F32
        )
        return new.reshape((nz // 2,) + vir.shape[1:])

    def admit(i):
        chain = order[i]
        pl.when(distant(chain))(lambda: arrive(2 * chain + low))
        pl.when(jnp.abs(chain - z) == 2)(lambda: arrive_pieces(2 * chain + low))
        passed = jnp.logical_or(chain == z, chain == nearest(1))
        pl.when(passed)(lambda: arrive_pieces(2 * chain + 1 - low))
        pl.when(jnp.logical_not(passed))(lambda: arrive(2 * chain + 1 - low))
        absorb(i, chain)

    admit(0)
    for i in range(1, nz):
        base[i - 1] = overlap(order[i], q)
    for i in early[1:]:
        admit(i)
    for half in range(2):
        vir[pl.ds(half * (nz // 2), nz // 2)] = part_vir(half, early)
    for k in range(strips):
        t_give[k] = part_three(far, 1 - c, wide(k), early)
        t_mine[k] = part_three(far, c, wide(k), early)
    for i in late:
        admit(i)

    def far_swap(k):
        return remote(t_give.at[k], t_got.at[k], t_send, c_recv.at[nz + k, 2], partner)

    def coded_copies(code, scale, code_to, scale_to, sems, target):
        return (
            remote(code, code_to, sems[0].at[0], sems[1].at[0], target),
            remote(scale, scale_to, sems[0].at[1], sems[1].at[1], target),
        )

    def far_send(k):
        sems = (ts_send, c_recv.at[nz + k])
        return coded_copies(t_code.at[k], t_scale.at[k], t_code_in.at[k], t_scale_in.at[k], sems, opposite)

    def x_swap(chain):
        sems = (x_send, c_recv.at[chain])
        return coded_copies(
            x_code.at[chain], x_scale.at[chain], x_code_in.at[chain], x_scale_in.at[chain], sems, (side, s)
        )

    def along(to, sender):
        sems = (z_send, z_recv.at[sender])
        return coded_copies(
            z_code.at[to], z_scale.at[to], z_code_in.at[sender], z_scale_in.at[sender], sems, (2 * to + low, s)
        )

    def both_start(copies):
        for copy in copies:
            copy.start()

    def both_recv(copies):
        for copy in copies:
            copy.wait_recv()

    def both_sent(copies):
        for copy in copies:
            copy.wait_send()

    def encode(value, code, scale):
        parts = scale.shape[0]
        size = value.shape[0] // parts
        grouped = value.reshape(parts, size, value.shape[1])
        top = jnp.maximum(jnp.max(jnp.abs(grouped), axis=1, keepdims=True), TINY)
        scale[...] = top
        code[...] = jnp.exp(grouped * (SPAN / top)).astype(jnp.bfloat16).reshape(value.shape)

    def decode(code, scale):
        parts = scale.shape[0]
        words = jnp.log(code[...].astype(F32)).reshape(parts, code.shape[0] // parts, code.shape[1])
        return (words * (scale[...] * (1.0 / SPAN))).reshape(code.shape)

    def v_swap(chain):
        return remote(vir.at[chain, :, :, 1 - c], v_pair.at[chain], vp_send, c_recv.at[chain, 2], partner)

    def between():
        return coded_copies(y_code, y_scale, y_code_in, y_scale_in, (yv_send, yv_recv), opposite)

    near_swap = remote(n_give, n_got, n_sems.at[0], n_sems.at[1], partner)
    first = jnp.where(z < nz // 2, 1, 0)
    for half in (first, 1 - first):
        where = pl.ds(half * (nz // 2), nz // 2)
        vir[where] = vir[where] + part_vir(half, late)
        for t in range(nz // 2):
            v_swap(half * (nz // 2) + t).start()

    def pair_sum(chain, across):
        return (vir[chain, across, :, c] + v_pair[chain, across]).reshape(2 * rows, virtuals)

    farthest = [nearest(k) for k in reversed(range(nz))]

    def add_pair(chain):
        v_swap(chain).wait_recv()
        encode(pair_sum(chain, 1 - low), x_code.at[chain], x_scale.at[chain])
        both_start(x_swap(chain))

    for k in range(max(strips, nz)):
        if k < strips:
            t_give[k] += part_three(far, 1 - c, wide(k), late)
            far_swap(k).start()
        if k < nz:
            add_pair(farthest[k])
    for k in range(strips):
        new = t_mine[k] + part_three(far, c, wide(k), late)
        far_swap(k).wait_recv()
        encode(new + t_got[k], t_code.at[k], t_scale.at[k])
        both_start(far_send(k))
    def add_beside(chain, last):
        both_recv(x_swap(chain))
        total = pair_sum(chain, low) + decode(x_code_in.at[chain], x_scale_in.at[chain])
        if last:
            v_line[...] = total
        else:
            encode(total, z_code.at[chain], z_scale.at[chain])
            both_start(along(chain, z))

    def near_give():
        n_give[...] = part_three(q, 1 - c, slice(None), range(nz))
        near_swap.start()

    def near_keep():
        near_sum[...] = part_three(q, c, slice(None), range(nz))

    fillers = [near_give, near_keep]
    for k in range(nz):
        add_beside(farthest[k], k == nz - 1)
        if k < len(fillers):
            fillers[k]()
    for filler in fillers[nz:]:
        filler()
    near_swap.wait_recv()
    near_sum[...] += n_got[...]
    for k in range(1, nz):
        sender = nearest(k)
        both_recv(along(sender, sender))
        v_line[...] += decode(z_code_in.at[sender], z_scale_in.at[sender])
    v_col[...] = v_line[...].reshape(v_col.shape)
    encode(v_col[far], y_code, y_scale)
    both_start(between())
    for k in range(strips):
        both_recv(far_send(k))
        near_sum[:, wide(k)] += decode(t_code_in.at[k], t_scale_in.at[k])
    three_out[...] = near_sum[...].reshape(three_out.shape)
    both_recv(between())
    vir_out[...] = (v_col[q] + decode(y_code_in, y_scale_in)) / (n * virtuals)

    lend.wait_send()

    half_block = full.at[:part, : basis // 2]

    @pl.loop(0, nz)
    def _(chain):
        coef_relay(chain, half_block, half_block, c_recv.at[0, 0], sent)

    coef_far(half_block, half_block, c_recv.at[0, 0], sent)
    coef_halves(n - 1).wait_send()
    given().wait_send()

    def lent(blocks, sem):
        ref = cross.at[:blocks]
        return remote(ref, ref, y_send.at[sem], f_recv.at[0, 0], opposite)

    if nz > 2:
        lent(nz - 2, 0).wait_send()
    for k in range(2, nz):
        pl.when(distant(nearest(k)))(lambda: lent(1, k - 1).wait_send())

    both_rows = own.at[: 2 * width, :tile]
    hand_out([(0, 0, both_rows, both_rows)], sent)
    far_part(c).wait_send()
    near_part(c).wait_send()
    block_ref = held.at[:width, : 2 * tile]
    each_at(1, lambda chain: pass_on(chain, block_ref, f_recv.at[0, 0], sent))
    near_swap.wait_send()
    remote(t_give, t_give, t_send, c_recv.at[nz, 2], partner).wait_send()
    both_sent(coded_copies(t_code, t_scale, t_code, t_scale, (ts_send, c_recv.at[nz]), opposite))
    whole = vir.at[:, :, :, 0]
    remote(whole, whole, vp_send, c_recv.at[0, 2], partner).wait_send()
    both_sent(coded_copies(x_code, x_scale, x_code, x_scale, (x_send, c_recv.at[0]), (side, s)))
    codes, scales = z_code.at[: nz - 1], z_scale.at[: nz - 1]
    both_sent(coded_copies(codes, scales, codes, scales, (z_send, z_recv.at[0]), (side, s)))
    both_sent(between())


def paired(n, half_integrals, coef, occ_energy, vir_energy):
    _, tile, basis = half_integrals.shape
    part = coef.shape[0]
    virtuals = part * n
    width, rows, nz = virtuals // 4, virtuals // (4 * n), n // 2
    pieces = PIECES if basis % (256 * PIECES) == 0 else 1
    vmem = pl.BlockSpec(memory_space=pltpu.VMEM)
    dma = pltpu.SemaphoreType.DMA
    lanes = 128
    chunks = virtuals // lanes
    strip = 2 * lanes if chunks % 2 == 0 else lanes
    strips = virtuals // strip

    def room(*shape):
        return pltpu.VMEM(shape, F32)

    def packed(*shape):
        return pltpu.VMEM(shape, jnp.bfloat16)

    scratch = [
        packed(n, tile, basis), packed(tile, basis), packed(virtuals, basis), packed(virtuals, 4 * tile),
        packed(n * width, 4 * tile), packed(n, width, tile), packed(n, 2 * width, tile), packed(n * width, virtuals),
        room(nz - 1, 2 * width, virtuals),
        room(nz, 2, 2, 2, rows, virtuals),
        room(strips, tile, strip), room(strips, tile, strip), room(strips, tile, strip), room(tile, virtuals), room(tile, virtuals),
        room(tile, virtuals), room(nz, 2, 2, rows, virtuals), room(2 * rows, virtuals), room(2, rows, virtuals),
    ]
    groups = tile // 64
    for _ in range(2):
        scratch += [packed(strips, tile, strip), room(strips, groups, 1, strip)]
    for _ in range(4):
        scratch += [packed(nz, 2 * rows, virtuals), room(nz, 1, 1, virtuals)]
    for _ in range(2):
        scratch += [packed(rows, virtuals), room(1, 1, virtuals)]
    scratch += [pltpu.SMEM((n,), F32), room(virtuals)]
    scratch += [
        dma((2,)), dma, dma, dma, dma((2,)), dma((n, pieces)), dma((2,)), dma((2,)), dma((nz,)), dma((2, max(nz - 3, 1))), dma((2,)),
        dma((2,)), dma((2,)), dma((n, 2)), dma((3,)), dma((2,)), dma, dma((nz,)), dma((2,)),
        dma, dma((2,)), dma((2,)), dma, dma((2,)), dma((2,)), dma((nz, 2)), dma((2,)), dma((2,)),
    ]
    return pl.pallas_call(
        functools.partial(paired_kernel, n),
        out_shape=(
            pltpu.VMEM((tile, 1, virtuals), F32), pltpu.VMEM((rows, virtuals), F32),
        ),
        in_specs=[pl.BlockSpec(memory_space=pl.ANY)] * 4,
        out_specs=(vmem, vmem),
        scratch_shapes=scratch,
        compiler_params=pltpu.CompilerParams(
            collective_id=0, has_side_effects=True, vmem_limit_bytes=LIMIT
        ),
        name="densities",
    )(occ_energy, half_integrals, coef, vir_energy)


def per_device(half_integrals, vir_coef, occ_energy, vir_energy):
    n, aux = lax.axis_size("occ"), lax.axis_size("aux")
    nz, nq = n // 2, aux // 2
    _, tile, basis = half_integrals.shape
    part = vir_coef.shape[1]
    virtuals = part * n
    if nq == 2 and n % 2 == 0 and nz > 1 and nz % 2 == 0 and virtuals % (32 * n) == 0 and virtuals % 256 == 0 and tile % 64 == 0 and basis % (256 * PIECES) == 0 and nz >= virtuals // 256:
        three, vir_rows = paired(n, half_integrals, vir_coef.T, occ_energy, vir_energy)
        return three, vir_rows
    width, rows = virtuals // aux, virtuals // (n * aux)
    vmem = pl.BlockSpec(memory_space=pltpu.VMEM)
    dma = pltpu.SemaphoreType.DMA
    half = jnp.bfloat16
    lanes = 128
    chunks = virtuals // lanes

    def room(*shape):
        return pltpu.VMEM(shape, F32)

    def result(*shape):
        return jax.ShapeDtypeStruct(shape, F32)

    def call(kernel, name, number, in_specs, out_shape, scratch, operands):
        return pl.pallas_call(
            kernel,
            out_shape=out_shape,
            in_specs=in_specs,
            out_specs=(vmem,) * len(out_shape),
            scratch_shapes=scratch,
            compiler_params=pltpu.CompilerParams(
                collective_id=number, has_side_effects=True, vmem_limit_bytes=LIMIT
            ),
            name=name,
        )(*operands)

    operands = (occ_energy, half_integrals, vir_coef.T, vir_energy)
    specs = [pl.BlockSpec(memory_space=pltpu.SMEM), pl.BlockSpec(memory_space=pl.ANY), vmem, vmem]
    make_scratch = [
        pltpu.VMEM(half_integrals.shape, half),
        pltpu.VMEM((2, virtuals, basis // 2), half),
        pltpu.VMEM((nq, 2, nq, 2 * width, tile), half),
        pltpu.VMEM((nq, 2, n * width, tile), half),
        pltpu.VMEM((n, width, tile), half),
        pltpu.VMEM((n * width, virtuals), half),
        dma, dma((2,)), dma, dma((n,)), dma((nz,)), dma((nz,)), dma((nz,)), dma((n,)), dma((n,)),
        dma((nq, nq)), dma((nq, nq)), dma((nq, nq)), dma((nq, nq)), dma((nq,)), dma((nq,)), dma((n,)), dma((n,)),
        dma((nq, n)), dma((nq, nz)), dma((nq, nz)), dma((nq, nz)),
    ]
    reduce_scratch = [
        room(nq, tile, virtuals), room(nq, tile, virtuals), room(nq, tile, virtuals),
        room(chunks, n, nq, rows, lanes), room(chunks, nz, 2, nq, rows, lanes),
        room(chunks, nz, nq, rows, lanes), room(chunks, nz, nq, rows, lanes), room(chunks, nz, nq, rows, lanes),
        room(chunks, nq, rows, lanes), room(chunks, nq, rows, lanes),
        dma((nq,)), dma((nq,)), dma((nq,)), dma((nq,)), dma((chunks,)), dma((chunks,)), dma((chunks,)), dma((chunks,)),
        dma((chunks, nz)), dma((chunks, nz)), dma((chunks, nq)), dma((chunks, nq)),
    ]
    sums = (nq, 2, tile, virtuals)
    groups = (n, nq, 2, rows, virtuals)
    finals = (result(tile, virtuals), result(tile, virtuals), result(rows, virtuals))
    if rows % 8 == 0:
        kernel = functools.partial(whole_kernel, n, nq, len(specs), len(finals), len(make_scratch))
        scratch = [room(*sums), room(*groups)] + make_scratch + reduce_scratch
        near, far, vir_rows = call(kernel, "densities", 0, specs, finals, scratch, operands)
    else:
        kernel = functools.partial(amplitude_kernel, n, nq)
        partials = (result(*sums), result(virtuals, virtuals))
        three, vir = call(kernel, "amplitude", 0, specs, partials, make_scratch, operands)
        kernel = functools.partial(reduce_kernel, n, nq)
        near, far, vir_rows = call(
            kernel, "reduce", 1, [vmem, vmem], finals, reduce_scratch, (three, vir.reshape(groups))
        )
    return (near + far)[:, None, :], vir_rows / (n * virtuals)


def solution(mesh):
    return jax.shard_map(
        per_device,
        mesh=mesh,
        in_specs=(P(None, "aux", None), P(None, "occ"), P(), P()),
        out_specs=(P("aux", "occ", None), P(("occ", "aux"), None)),
        check_vma=False,
    )
```
